32 devices in a mesh: tm: 16 (over z, x, core), rows: 2 (over y).
Axes of the slice: x: 2, y: 2, z: 4, core: 2. Of those that a mesh axis runs over, the one named last changes fastest.
Arguments:
- video: bfloat16 [32, 16, 480, 128], P('tm', 'rows'), may hold values from -1000 to 1000, as said below
- spatial_weight: bfloat16 [3, 3, 128, 128], replicated, may hold values from -0.1875 to 0.1875
- norm_gain: float32 [128], replicated, may hold values from 0.5 to 1.5
- norm_shift: float32 [128], replicated, may hold values from -3 to 3
- temporal_weight: bfloat16 [3, 3, 128, 128], replicated, may hold values from -0.3125 to 0.3125
Outputs:
- encoded: bfloat16 [32, 16, 480, 128], P('tm', 'rows')
The draws below stay inside these ranges and needn't reach their ends.
Inputs may be any that keep to these rules, and one draw needn't show every extreme that they name: `video`: feature values are finite and of moderate size.
All inputs are finite; a program needn't handle non-finite values.
Results may differ from the reference program's by a relative error of at most 0.0065.
Values may be sent and summed in bfloat16 or wider, within the bound.
No kernel may reach another device: no remote copies, remote signals or barrier semaphores. Data moves between devices by JAX's collectives and lax.ppermute only.
A program may use at most 64 MiB of HBM per device.

```python
import jax
import jax.numpy as jnp
from jax import lax

CH = 128
GROUPS = 32
WIDTH_PX = 480
FRAMES = 32
HEIGHT = 16


def draw_video(key, part):
    key_base = jax.random.fold_in(key, 11)
    key_rough = jax.random.fold_in(key, 12)
    key_cols = jax.random.fold_in(key, 13)
    key_chan = jax.random.fold_in(key, 14)
    position = jnp.arange(HEIGHT, dtype=jnp.float32).reshape(1, HEIGHT, 1, 1) / max(HEIGHT - 1, 1)
    rough = jnp.exp(jax.random.uniform(key_rough, (FRAMES, HEIGHT, 1, 1), jnp.float32, -0.35, 0.35))
    column_scale = jnp.exp(jax.random.uniform(key_cols, (1, 1, WIDTH_PX, 1), jnp.float32, 0.0, 2.3))
    chan_scale = jnp.exp(jax.random.uniform(key_chan, (1, 1, 1, CH), jnp.float32, -0.7, 0.7))
    base = jnp.clip(jax.random.normal(key_base, (FRAMES, HEIGHT, WIDTH_PX, CH), jnp.float32), -6.0, 6.0)
    row_scale = 0.3 * jnp.exp(2.3 * position)
    return (base * row_scale * rough * column_scale * chan_scale).astype(jnp.bfloat16)


def normal_values(own_key, dims, spread, limit, kind=jnp.bfloat16):
    drawn = spread * jax.random.normal(own_key, dims, jnp.float32)
    return jnp.clip(drawn, min=-limit, max=limit).astype(kind)


def setup_inputs(seed: int = 0) -> dict:
    key_list = jax.random.split(jax.random.key(seed), 6)
    return {
        "video": draw_video(jax.random.fold_in(key_list[5], 71), 0),
        "spatial_weight": normal_values(key_list[1], (3, 3, CH, CH), (9 * CH) ** -0.5, 0.1875),
        "norm_gain": jnp.clip(1.0 + 0.1 * jax.random.normal(key_list[2], (CH,), jnp.float32), 0.5, 1.5),
        "norm_shift": normal_values(key_list[3], (CH,), 0.5, 3.0, jnp.float32),
        "temporal_weight": normal_values(key_list[4], (3, 3, CH, CH), (3 * CH) ** -0.5, 0.3125),
    }


def spatial(frame, spatial_weight):
    height, width, chans = frame.shape
    padded = jnp.pad(frame, ((1, 1), (1, 1), (0, 0)))
    pieces = [padded[row_tap:row_tap + height, col_tap:col_tap + width, :] for row_tap in range(3) for col_tap in range(3)]
    patches = jnp.concatenate(pieces, axis=-1).reshape(height * width, 9 * chans)
    result = jnp.dot(patches, spatial_weight.reshape(9 * chans, chans), preferred_element_type=jnp.float32)
    return result.reshape(height, width, chans)

def normalize(frame, spatial_weight, norm_gain, norm_shift):
    conv = spatial(frame, spatial_weight)
    height, width, chans = conv.shape
    grouped = conv.reshape(height, width, GROUPS, chans // GROUPS)
    count = jnp.float32(height * width * (chans // GROUPS))
    mean = lax.optimization_barrier(jnp.sum(grouped, axis=(0, 1, 3))) / count
    var = lax.optimization_barrier(jnp.sum(grouped * grouped, axis=(0, 1, 3))) / count - mean * mean
    normed = (grouped - mean[None, None, :, None]) * lax.rsqrt(var + 1e-05)[None, None, :, None]
    normed = normed.reshape(height, width, chans) * norm_gain + norm_shift
    return jax.nn.silu(normed).astype(jnp.bfloat16)

def temporal_row(line, temporal_weight):
    frames, width, chans = line.shape
    current = line
    for layer, dilation in enumerate((1, 2, 4)):
        lead = 2 * dilation
        extended = jnp.pad(current, ((lead, 0), (0, 0), (0, 0)))
        total = current.astype(jnp.float32)
        for tap_index in range(3):
            start = lead - tap_index * dilation
            window = extended[start:start + frames].reshape(frames * width, chans)
            total = total + jnp.dot(window, temporal_weight[layer, tap_index], preferred_element_type=jnp.float32).reshape(frames, width, chans)
        current = total.astype(jnp.bfloat16)
    return current

def reference(video, spatial_weight, norm_gain, norm_shift, temporal_weight):
    hidden = lax.map(lambda frame: normalize(frame, spatial_weight, norm_gain, norm_shift), video)
    by_rows = jnp.moveaxis(hidden, 1, 0)
    result = lax.map(lambda line: temporal_row(line, temporal_weight), by_rows)
    return jnp.moveaxis(result, 0, 1)
```

```python
import functools

import jax
import jax.numpy as jnp
from jax import lax
from jax.experimental import pallas as pl
from jax.experimental.pallas import tpu as pltpu
from jax.sharding import PartitionSpec as P

GROUPS = 32
SPAN = 8
CHUNKS = 4
VMEM = pltpu.VMEM
ANY = pl.ANY
F32 = jnp.float32
BF16 = jnp.bfloat16


def vspec():
    return pl.BlockSpec(memory_space=VMEM)


def sspec():
    return pl.BlockSpec(memory_space=pltpu.SMEM)


def params(mib):
    return pltpu.CompilerParams(vmem_limit_bytes=mib << 20)


def cost(flops, nbytes):
    return pl.CostEstimate(flops=int(flops), bytes_accessed=int(nbytes), transcendentals=0)


def shifted_sum(taps):
    width, ch = taps.shape[0], taps.shape[1] // 3
    column = lax.broadcasted_iota(jnp.int32, (width, ch), 0)
    left = jnp.where(column == 0, 0.0, pltpu.roll(taps[:, :ch], 1, 0))
    right = jnp.where(column == width - 1, 0.0, pltpu.roll(taps[:, 2 * ch :], width - 1, 0))
    return left + taps[:, ch : 2 * ch] + right


def fold(value):
    return jnp.sum(value.reshape(value.shape[0] // 8, 8, value.shape[1]), axis=0)


def conv_kernel(band, video_ref, weight_ref, inner_ref, edge_ref, sums_ref, wide_ref):
    ch = video_ref.shape[-1]

    @pl.when(pl.program_id(0) == 0)
    def _():
        wide_ref[...] = jnp.zeros_like(wide_ref)
        for out in range(2):
            for col in range(3):
                for row in range(3):
                    wide_ref[
                        (out + row) * ch : (out + row + 1) * ch,
                        (out * 3 + col) * ch : (out * 3 + col + 1) * ch,
                    ] = weight_ref[row, col]

    total = jnp.zeros((8, ch), F32)
    square = jnp.zeros((8, ch), F32)
    for first in range(0, band, 2):
        rows = [r for r in range(first - 1, first + 3) if 0 <= r < band]
        lhs = jnp.concatenate([video_ref[0, r] for r in rows], axis=-1)
        skip = (rows[0] - (first - 1)) * ch
        wide = jnp.dot(
            lhs, wide_ref[skip : skip + len(rows) * ch, :], preferred_element_type=F32
        )
        for out in range(2):
            value = shifted_sum(wide[:, out * 3 * ch : (out + 1) * 3 * ch])
            row = first + out
            if row == 0:
                edge_ref[0, 0] = value
            elif row == band - 1:
                edge_ref[0, 1] = value
            else:
                inner_ref[0, row - 1] = value
                total = total + fold(value)
                square = square + fold(value * value)
    sums_ref[0, 0] = total
    sums_ref[0, 1] = square


def conv_call(video, weight):
    frames, band, width, ch = video.shape
    return pl.pallas_call(
        functools.partial(conv_kernel, band),
        grid=(frames,),
        in_specs=[
            pl.BlockSpec((1, band, width, ch), lambda f: (f, 0, 0, 0)),
            pl.BlockSpec(weight.shape, lambda f: (0, 0, 0, 0)),
        ],
        out_specs=[
            pl.BlockSpec((1, band - 2, width, ch), lambda f: (f, 0, 0, 0)),
            pl.BlockSpec((1, 2, width, ch), lambda f: (f, 0, 0, 0)),
            pl.BlockSpec((1, 2, 8, ch), lambda f: (f, 0, 0, 0)),
        ],
        out_shape=[
            jax.ShapeDtypeStruct((frames, band - 2, width, ch), F32),
            jax.ShapeDtypeStruct((frames, 2, width, ch), F32),
            jax.ShapeDtypeStruct((frames, 2, 8, ch), F32),
        ],
        scratch_shapes=[VMEM((4 * ch, 6 * ch), BF16)],
        compiler_params=params(32),
        cost_estimate=cost(frames * band * width * 18 * ch * ch, frames * band * width * ch * 6),
        name="conv",
    )(video, weight)


def edge_kernel(flag_ref, part_ref, above_ref, below_ref, weight_ref, sums_ref, edge_ref, out_sums_ref):
    frames = part_ref.shape[0]
    for frame in range(frames):
        total, square = sums_ref[frame, 0], sums_ref[frame, 1]
        for side, (halo_ref, tap) in enumerate(((above_ref, 0), (below_ref, 2))):
            halo = halo_ref[frame]
            halo = jnp.where(flag_ref[side] > 0, halo, jnp.zeros_like(halo))
            taps = jnp.concatenate([weight_ref[tap, col] for col in range(3)], axis=-1)
            wide = jnp.dot(halo, taps, preferred_element_type=F32)
            value = part_ref[frame, side] + shifted_sum(wide)
            edge_ref[frame, side] = value
            total = total + fold(value)
            square = square + fold(value * value)
        out_sums_ref[frame, 0] = total
        out_sums_ref[frame, 1] = square


def edge_call(flags, part, above, below, weight, sums):
    return pl.pallas_call(
        edge_kernel,
        in_specs=[sspec()] + [vspec()] * 5,
        out_specs=[vspec()] * 2,
        out_shape=[
            jax.ShapeDtypeStruct(part.shape, F32),
            jax.ShapeDtypeStruct(sums.shape, F32),
        ],
        compiler_params=params(32),
        cost_estimate=cost(part.size * 6 * part.shape[-1], part.size * 10),
        name="edge",
    )(flags, part, above, below, weight, sums)


def over_groups(value, per_group):
    lane = lax.broadcasted_iota(jnp.int32, value.shape, 1)
    lanes = value.shape[1]
    step = 1
    while step < per_group:
        value = value + pltpu.roll(value, lanes - step, 1)
        step *= 2
    value = jnp.where(lane % per_group == 0, value, 0.0)
    step = 1
    while step < per_group:
        value = value + pltpu.roll(value, step, 1)
        step *= 2
    return value


def norm_kernel(count, per_group, members, chunks, me_ref, inner_ref, edge_ref, own_ref, peer_ref, gain_ref, shift_ref, *refs):
    outs, hidden_ref = refs[:-1], refs[-1]
    frames, inner, width, ch = inner_ref.shape
    band = inner + 2
    for frame in range(frames):
        sums = [
            jnp.broadcast_to(
                jnp.sum(own_ref[frame, i] + peer_ref[frame, i], axis=0, keepdims=True), (8, ch)
            )
            for i in range(2)
        ]
        mean = over_groups(sums[0], per_group) / count
        var = over_groups(sums[1], per_group) / count - mean * mean
        scale = (lax.rsqrt(var + 1e-05) * gain_ref[...])[:1]
        mean = mean[:1]
        shift = shift_ref[...]

        def put(row, value):
            v = (value - mean) * scale + shift
            v = 0.5 * v * (1.0 + jnp.tanh(0.5 * v))
            hidden_ref[frame, row] = v.astype(BF16)

        put(0, edge_ref[frame, 0])
        put(band - 1, edge_ref[frame, 1])

        @pl.loop(0, inner)
        def _(row):
            put(row + 1, inner_ref[frame, row])

    flat = hidden_ref.reshape(frames, band * width, ch)
    size = band * width // (members * chunks)
    me = me_ref[0]
    for chunk in range(chunks):
        for k in range(members):
            start = pl.multiple_of(((me ^ k) * chunks + chunk) * size, 16)
            outs[chunk * members + k][...] = flat[:, pl.ds(start, size), :]


def norm_call(me, inner, edge, own, peer, gain, shift, count, members, chunks):
    frames, rows, width, ch = inner.shape
    band = rows + 2
    size = band * width // (members * chunks)
    return pl.pallas_call(
        functools.partial(norm_kernel, count, ch // GROUPS, members, chunks),
        in_specs=[sspec()] + [vspec()] * 6,
        out_specs=[vspec()] * (members * chunks),
        out_shape=[jax.ShapeDtypeStruct((frames, size, ch), BF16)] * (members * chunks),
        scratch_shapes=[VMEM((frames, band, width, ch), BF16)],
        compiler_params=params(40),
        cost_estimate=cost(frames * band * width * ch * 10, frames * band * width * ch * 6),
        name="norm",
    )(me, inner, edge, own, peer, gain.reshape(1, ch), shift.reshape(1, ch))


def pair_weights(weight_ref, layer, wide_ref):
    ch = weight_ref.shape[-1]
    wide_ref[...] = jnp.zeros_like(wide_ref)
    for out in range(2):
        for tap in range(3):
            row = out + 2 - tap
            wide_ref[row * ch : (row + 1) * ch, out * ch : (out + 1) * ch] = weight_ref[layer, tap]


def pair(read, write, time, dilation, wide_ref):
    ch = wide_ref.shape[1] // 2
    frames = [read(time + (a - 2) * dilation) for a in range(4)]
    both = jnp.dot(jnp.concatenate(frames, axis=-1), wide_ref[...], preferred_element_type=F32)
    write(time, (both[:, :ch] + frames[2].astype(F32)).astype(BF16))
    write(time + dilation, (both[:, ch:] + frames[3].astype(F32)).astype(BF16))


def early_kernel(members, me_ref, *refs):
    pieces, (halo_ref, weight_ref, out_ref, u0_ref, u1_ref, wide_ref) = refs[:members], refs[members:]
    step = pieces[0].shape[0]
    u0_ref[: SPAN - 2] = halo_ref[...]
    for k in range(members):
        u0_ref[pl.ds(SPAN - 2 + (me_ref[0] ^ k) * step, step)] = pieces[k][...]
    pair_weights(weight_ref, 0, wide_ref)

    def write1(t, value):
        u1_ref[t + 4] = value

    def write2(t, value):
        out_ref[t] = value

    for time in range(-4, SPAN, 2):
        pair(lambda t: u0_ref[t + SPAN - 2], write1, time, 1, wide_ref)
    pair_weights(weight_ref, 1, wide_ref)
    for time in range(0, SPAN, 4):
        for odd in range(2):
            pair(lambda t: u1_ref[t + 4], write2, time + odd, 2, wide_ref)


def early_call(me, pieces, halo, weight):
    members = len(pieces)
    _, size, ch = pieces[0].shape
    return pl.pallas_call(
        functools.partial(early_kernel, members),
        in_specs=[sspec()] + [vspec()] * (members + 2),
        out_specs=vspec(),
        out_shape=jax.ShapeDtypeStruct((SPAN, size, ch), BF16),
        scratch_shapes=[
            VMEM((2 * SPAN - 2, size, ch), BF16),
            VMEM((SPAN + 4, size, ch), BF16),
            VMEM((4 * ch, 2 * ch), BF16),
        ],
        compiler_params=params(32),
        cost_estimate=cost(20 * size * 6 * ch * ch, 22 * size * ch * 2),
        name="early",
    )(me, *pieces, halo, weight)


def late_kernel(members, me_ref, own_ref, halo_ref, weight_ref, *refs):
    outs, (u3_ref, wide_ref) = refs[:members], refs[members:]
    step = outs[0].shape[0]
    pair_weights(weight_ref, 2, wide_ref)

    def write3(t, value):
        u3_ref[t] = value

    for time in range(4):
        pair(
            lambda t: own_ref[t] if t >= 0 else halo_ref[t + SPAN], write3, time, 4, wide_ref
        )
    for k in range(members):
        outs[k][...] = u3_ref[pl.ds((me_ref[0] ^ k) * step, step)]


def late_call(me, own, halo, weight, members):
    frames, size, ch = own.shape
    return pl.pallas_call(
        functools.partial(late_kernel, members),
        in_specs=[sspec()] + [vspec()] * 3,
        out_specs=[vspec()] * members,
        out_shape=[jax.ShapeDtypeStruct((frames // members, size, ch), BF16)] * members,
        scratch_shapes=[VMEM(own.shape, BF16), VMEM((4 * ch, 2 * ch), BF16)],
        compiler_params=params(32),
        cost_estimate=cost(8 * size * 6 * ch * ch, 24 * size * ch * 2),
        name="late",
    )(me, own, halo, weight)


def place_kernel(members, chunks, me_ref, *refs):
    pieces, (out_ref, sem) = refs[: members * chunks], refs[members * chunks :]
    copies = [
        pltpu.make_async_copy(
            pieces[chunk * members + k],
            out_ref.at[:, me_ref[0] ^ k, chunk],
            sem.at[chunk * members + k],
        )
        for chunk in range(chunks)
        for k in range(members)
    ]
    for copy in copies:
        copy.start()
    for copy in copies:
        copy.wait()


def place_call(me, pieces, members, chunks):
    frames, size, ch = pieces[0].shape
    return pl.pallas_call(
        functools.partial(place_kernel, members, chunks),
        in_specs=[sspec()] + [pl.BlockSpec(memory_space=ANY)] * len(pieces),
        out_specs=pl.BlockSpec(memory_space=ANY),
        out_shape=jax.ShapeDtypeStruct((frames, members, chunks, size, ch), BF16),
        scratch_shapes=[pltpu.SemaphoreType.DMA((len(pieces),))],
        cost_estimate=cost(0, 2 * len(pieces) * frames * size * ch * 2),
        name="place",
    )(me, *pieces)


def halo_rows(video):
    size, row = lax.axis_size("rows"), lax.axis_index("rows")
    band = video.shape[1]
    if size == 2:
        mine = lax.dynamic_slice_in_dim(video, jnp.where(row == 0, band - 1, 0), 1, axis=1)[:, 0]
        other = lax.ppermute(mine, "rows", [(0, 1), (1, 0)])
        return other, other
    up = [(i, i + 1) for i in range(size - 1)]
    down = [(j, i) for i, j in up]
    return lax.ppermute(video[:, -1], "rows", up), lax.ppermute(video[:, 0], "rows", down)


def other_sums(sums):
    if lax.axis_size("rows") == 2:
        return lax.ppermute(sums, "rows", [(0, 1), (1, 0)])
    return lax.psum(sums, "rows") - sums


def body(video, spatial_weight, norm_gain, norm_shift, temporal_weight):
    frames, band, width, ch = video.shape
    total, here = lax.axis_size("tm"), lax.axis_index("tm")
    members = SPAN // frames
    me = jnp.reshape(here % members, (1,)).astype(jnp.int32)
    row, rows = lax.axis_index("rows"), lax.axis_size("rows")
    flags = jnp.stack([row > 0, row < rows - 1]).astype(jnp.int32)
    swaps = [[(i, i ^ k) for i in range(total)] for k in range(members)]
    onward = [(i, i + members) for i in range(total - members)]

    above, below = halo_rows(video)
    inner, part, sums = conv_call(video, spatial_weight)
    edge, sums = edge_call(flags, part, above, below, spatial_weight, sums)
    count = band * rows * width * (ch // GROUPS)
    pieces = norm_call(
        me, inner, edge, sums, other_sums(sums), norm_gain, norm_shift, count, members, CHUNKS
    )

    def swap(four):
        return [four[0]] + [lax.ppermute(four[k], "tm", swaps[k]) for k in range(1, members)]

    mine = [swap(pieces[c * members : (c + 1) * members]) for c in range(CHUNKS)]
    results = []
    for four in mine:
        slots = [
            functools.reduce(
                lambda acc, k: jnp.where(me[0] == (slot ^ k), four[k], acc),
                range(1, members),
                four[0],
            )
            for slot in range(1, members)
        ]
        tail = jnp.concatenate(slots, axis=0)[-(SPAN - 2) :]
        halo = lax.ppermute(tail, "tm", onward)
        u2 = early_call(me, four, halo, temporal_weight)
        before = lax.ppermute(u2, "tm", onward)
        results += swap(late_call(me, u2, before, temporal_weight, members))
    out = place_call(me, results, members, CHUNKS)
    return out.reshape(frames, band, width, ch)


def solution(mesh):
    return jax.shard_map(
        body,
        mesh=mesh,
        in_specs=(P("tm", "rows", None, None), P(), P(), P(), P()),
        out_specs=P("tm", "rows", None, None),
        check_vma=False,
    )
```

```python
import functools

import jax
import jax.numpy as jnp
from jax import lax
from jax.experimental import pallas as pl
from jax.experimental.pallas import tpu as pltpu
from jax.sharding import PartitionSpec as P

GROUPS = 32
SPAN = 8
IN_SIZES = (240, 720)
OUT_SIZES = ((240,), (240, 240, 240))
VMEM = pltpu.VMEM
ANY = pl.ANY
F32 = jnp.float32
BF16 = jnp.bfloat16


def vspec():
    return pl.BlockSpec(memory_space=VMEM)


def sspec():
    return pl.BlockSpec(memory_space=pltpu.SMEM)


def params(mib):
    return pltpu.CompilerParams(vmem_limit_bytes=mib << 20)


def cost(flops, nbytes):
    return pl.CostEstimate(flops=int(flops), bytes_accessed=int(nbytes), transcendentals=0)


def shifted_sum(taps):
    width, ch = taps.shape[0], taps.shape[1] // 3
    column = lax.broadcasted_iota(jnp.int32, (width, ch), 0)
    left = jnp.where(column == 0, 0.0, pltpu.roll(taps[:, :ch], 1, 0))
    right = jnp.where(column == width - 1, 0.0, pltpu.roll(taps[:, 2 * ch :], width - 1, 0))
    return left + taps[:, ch : 2 * ch] + right


def fold(value):
    return jnp.sum(value.reshape(value.shape[0] // 8, 8, value.shape[1]), axis=0)


def conv_kernel(band, sources, *refs):
    video_refs = refs[:sources]
    if sources == 2:
        pick_ref, refs = refs[2], refs[:2] + refs[3:]
    weight_ref, inner_ref, edge_ref, sums_ref, wide_ref = refs[sources:]
    ch = weight_ref.shape[-1]

    def read(row):
        if sources == 1:
            return video_refs[0][0, row]
        return jnp.where(pick_ref[0] > 0, video_refs[1][0, row], video_refs[0][0, row])

    @pl.when(pl.program_id(0) == 0)
    def _():
        wide_ref[...] = jnp.zeros_like(wide_ref)
        for out in range(2):
            for col in range(3):
                for row in range(3):
                    wide_ref[
                        (out + row) * ch : (out + row + 1) * ch,
                        (out * 3 + col) * ch : (out * 3 + col + 1) * ch,
                    ] = weight_ref[row, col]

    total = jnp.zeros((8, ch), F32)
    square = jnp.zeros((8, ch), F32)
    for first in range(0, band, 2):
        rows = [r for r in range(first - 1, first + 3) if 0 <= r < band]
        lhs = jnp.concatenate([read(r) for r in rows], axis=-1)
        skip = (rows[0] - (first - 1)) * ch
        wide = jnp.dot(
            lhs, wide_ref[skip : skip + len(rows) * ch, :], preferred_element_type=F32
        )
        for out in range(2):
            value = shifted_sum(wide[:, out * 3 * ch : (out + 1) * 3 * ch])
            row = first + out
            if row == 0:
                edge_ref[0, 0] = value
            elif row == band - 1:
                edge_ref[0, 1] = value
            else:
                inner_ref[0, row - 1] = value
                total = total + fold(value)
                square = square + fold(value * value)
    sums_ref[0, 0] = total
    sums_ref[0, 1] = square


def conv_call(videos, weight, *pick):
    frames, band, width, ch = videos[0].shape
    return pl.pallas_call(
        functools.partial(conv_kernel, band, len(videos)),
        grid=(frames,),
        in_specs=[pl.BlockSpec((1, band, width, ch), lambda f: (f, 0, 0, 0)) for _ in videos]
        + [sspec() for _ in pick]
        + [pl.BlockSpec(weight.shape, lambda f: (0, 0, 0, 0))],
        out_specs=[
            pl.BlockSpec((1, band - 2, width, ch), lambda f: (f, 0, 0, 0)),
            pl.BlockSpec((1, 2, width, ch), lambda f: (f, 0, 0, 0)),
            pl.BlockSpec((1, 2, 8, ch), lambda f: (f, 0, 0, 0)),
        ],
        out_shape=[
            jax.ShapeDtypeStruct((frames, band - 2, width, ch), F32),
            jax.ShapeDtypeStruct((frames, 2, width, ch), F32),
            jax.ShapeDtypeStruct((frames, 2, 8, ch), F32),
        ],
        scratch_shapes=[VMEM((4 * ch, 6 * ch), BF16)],
        compiler_params=params(12),
        cost_estimate=cost(frames * band * width * 18 * ch * ch, frames * band * width * ch * 6),
        name="conv",
    )(*videos, *pick, weight)


def edge_kernel(flag_ref, part_ref, above_ref, below_ref, weight_ref, sums_ref, edge_ref, out_sums_ref):
    frames = part_ref.shape[0]
    for frame in range(frames):
        total, square = sums_ref[frame, 0], sums_ref[frame, 1]
        for side, (halo_ref, tap) in enumerate(((above_ref, 0), (below_ref, 2))):
            halo = halo_ref[frame]
            halo = jnp.where(flag_ref[side] > 0, halo, jnp.zeros_like(halo))
            taps = jnp.concatenate([weight_ref[tap, col] for col in range(3)], axis=-1)
            wide = jnp.dot(halo, taps, preferred_element_type=F32)
            value = part_ref[frame, side] + shifted_sum(wide)
            edge_ref[frame, side] = value
            total = total + fold(value)
            square = square + fold(value * value)
        out_sums_ref[frame, 0] = total
        out_sums_ref[frame, 1] = square


def edge_call(flags, part, above, below, weight, sums):
    return pl.pallas_call(
        edge_kernel,
        in_specs=[sspec()] + [vspec()] * 5,
        out_specs=[vspec()] * 2,
        out_shape=[
            jax.ShapeDtypeStruct(part.shape, F32),
            jax.ShapeDtypeStruct(sums.shape, F32),
        ],
        compiler_params=params(12),
        cost_estimate=cost(part.size * 6 * part.shape[-1], part.size * 10),
        name="edge",
    )(flags, part, above, below, weight, sums)


def over_groups(value, per_group):
    lane = lax.broadcasted_iota(jnp.int32, value.shape, 1)
    lanes = value.shape[1]
    step = 1
    while step < per_group:
        value = value + pltpu.roll(value, lanes - step, 1)
        step *= 2
    value = jnp.where(lane % per_group == 0, value, 0.0)
    step = 1
    while step < per_group:
        value = value + pltpu.roll(value, step, 1)
        step *= 2
    return value


def norm_kernel(count, per_group, members, sizes, flag_ref, inner_ref, edge_ref, sums_ref, gain_ref, shift_ref, *refs):
    outs, hidden_ref = refs[:-1], refs[-1]
    frames, inner, width, ch = inner_ref.shape
    band = inner + 2
    alive = flag_ref[1] > 0
    for frame in range(frames):
        sums = [
            jnp.broadcast_to(jnp.sum(sums_ref[frame, i], axis=0, keepdims=True), (8, ch))
            for i in range(2)
        ]
        mean = over_groups(sums[0], per_group) / count
        var = over_groups(sums[1], per_group) / count - mean * mean
        scale = (lax.rsqrt(var + 1e-05) * gain_ref[...])[:1]
        mean = mean[:1]
        shift = shift_ref[...]

        def put(row, value):
            v = (value - mean) * scale + shift
            v = 0.5 * v * (1.0 + jnp.tanh(0.5 * v))
            hidden_ref[frame, row] = jnp.where(alive, v, 0.0).astype(BF16)

        put(0, edge_ref[frame, 0])
        put(band - 1, edge_ref[frame, 1])

        @pl.loop(0, inner)
        def _(row):
            put(row + 1, inner_ref[frame, row])

    flat = hidden_ref.reshape(frames, band * width, ch)
    me = flag_ref[0]
    offset = 0
    for i, size in enumerate(sizes):
        for k in range(members):
            start = pl.multiple_of((me ^ k) * sum(sizes) + offset, 16)
            outs[i * members + k][...] = flat[:, pl.ds(start, size), :]
        offset += size


def norm_call(flags, inner, edge, sums, gain, shift, count, members, sizes):
    frames, rows, width, ch = inner.shape
    band = rows + 2
    return pl.pallas_call(
        functools.partial(norm_kernel, count, ch // GROUPS, members, sizes),
        in_specs=[sspec()] + [vspec()] * 5,
        out_specs=[vspec()] * (members * len(sizes)),
        out_shape=[
            jax.ShapeDtypeStruct((frames, size, ch), BF16) for size in sizes for _ in range(members)
        ],
        scratch_shapes=[VMEM((frames, band, width, ch), BF16)],
        compiler_params=params(16),
        cost_estimate=cost(frames * band * width * ch * 10, frames * band * width * ch * 6),
        name="norm",
    )(flags, inner, edge, sums, gain.reshape(1, ch), shift.reshape(1, ch))


def pair_weights(weight_ref, layer, wide_ref):
    ch = weight_ref.shape[-1]
    wide_ref[...] = jnp.zeros_like(wide_ref)
    for out in range(2):
        for tap in range(3):
            row = out + 2 - tap
            wide_ref[row * ch : (row + 1) * ch, out * ch : (out + 1) * ch] = weight_ref[layer, tap]


def pair(read, write, time, dilation, wide_ref):
    ch = wide_ref.shape[1] // 2
    frames = [read(time + (a - 2) * dilation) for a in range(4)]
    both = jnp.dot(jnp.concatenate(frames, axis=-1), wide_ref[...], preferred_element_type=F32)
    write(time, (both[:, :ch] + frames[2].astype(F32)).astype(BF16))
    write(time + dilation, (both[:, ch:] + frames[3].astype(F32)).astype(BF16))


def early_kernel(members, offset, size, me_ref, *refs):
    pieces, guests = refs[:members], refs[members : 2 * members]
    halo_ref, weight_ref, out_ref, u0_ref, u1_ref, wide_ref = refs[2 * members :]
    step = pieces[0].shape[0]
    lead = SPAN - 2
    rows = pl.ds(offset, size)
    for k in range(members):
        other = me_ref[0] ^ k
        u0_ref[pl.ds(lead + other * step, step)] = pieces[k][:, rows]
        u0_ref[other + (other & 2)] = guests[k][0, rows]
    u0_ref[2:4] = halo_ref[:, rows]
    pair_weights(weight_ref, 0, wide_ref)

    def write1(t, value):
        u1_ref[t + 4] = value

    def write2(t, value):
        out_ref[t] = value

    for time in range(-4, SPAN, 2):
        pair(lambda t: u0_ref[t + lead], write1, time, 1, wide_ref)
    pair_weights(weight_ref, 1, wide_ref)
    for time in range(0, SPAN, 4):
        for odd in range(2):
            pair(lambda t: u1_ref[t + 4], write2, time + odd, 2, wide_ref)


def early_call(me, pieces, guests, halo, weight, offset, size):
    members, ch = len(pieces), pieces[0].shape[-1]
    return pl.pallas_call(
        functools.partial(early_kernel, members, offset, size),
        in_specs=[sspec()] + [vspec()] * (2 * members + 2),
        out_specs=vspec(),
        out_shape=jax.ShapeDtypeStruct((SPAN, size, ch), BF16),
        scratch_shapes=[
            VMEM((2 * SPAN - 2, size, ch), BF16),
            VMEM((SPAN + 4, size, ch), BF16),
            VMEM((4 * ch, 2 * ch), BF16),
        ],
        compiler_params=params(12),
        cost_estimate=cost(20 * size * 6 * ch * ch, 22 * size * ch * 2),
        name="early",
    )(me, *pieces, *guests, halo, weight)


def late_kernel(members, me_ref, own_ref, halo_ref, weight_ref, *refs):
    outs, (u3_ref, wide_ref) = refs[:members], refs[members:]
    step = outs[0].shape[0]
    pair_weights(weight_ref, 2, wide_ref)

    def write3(t, value):
        u3_ref[t] = value

    for time in range(4):
        pair(
            lambda t: own_ref[t] if t >= 0 else halo_ref[t + SPAN], write3, time, 4, wide_ref
        )
    for k in range(members):
        outs[k][...] = u3_ref[pl.ds((me_ref[0] ^ k) * step, step)]


def late_call(me, own, halo, weight, members):
    frames, size, ch = own.shape
    return pl.pallas_call(
        functools.partial(late_kernel, members),
        in_specs=[sspec()] + [vspec()] * 3,
        out_specs=[vspec()] * members,
        out_shape=[jax.ShapeDtypeStruct((frames // members, size, ch), BF16)] * members,
        scratch_shapes=[VMEM(own.shape, BF16), VMEM((4 * ch, 2 * ch), BF16)],
        compiler_params=params(12),
        cost_estimate=cost(8 * size * 6 * ch * ch, 24 * size * ch * 2),
        name="late",
    )(me, own, halo, weight)


def place_kernel(members, sizes, me_ref, *refs):
    pieces, (out_ref, sem) = refs[: members * len(sizes)], refs[members * len(sizes) :]
    copies = []
    offset = 0
    for i, size in enumerate(sizes):
        for k in range(members):
            n = i * members + k
            place = out_ref.at[:, me_ref[0] ^ k, pl.ds(offset, size)]
            copies.append(pltpu.make_async_copy(pieces[n], place, sem.at[n]))
        offset += size
    for copy in copies:
        copy.start()
    for copy in copies:
        copy.wait()


def place_call(me, pieces, members, sizes):
    frames, _, ch = pieces[0].shape
    return pl.pallas_call(
        functools.partial(place_kernel, members, sizes),
        in_specs=[sspec()] + [vspec()] * len(pieces),
        out_specs=pl.BlockSpec(memory_space=ANY),
        out_shape=jax.ShapeDtypeStruct((frames, members, sum(sizes), ch), BF16),
        scratch_shapes=[pltpu.SemaphoreType.DMA((len(pieces),))],
        compiler_params=params(8),
        cost_estimate=cost(0, 2 * members * frames * sum(sizes) * ch * 2),
        name="place",
    )(me, *pieces)


def halo_rows(video):
    size, row = lax.axis_size("rows"), lax.axis_index("rows")
    band = video.shape[1]
    if size == 2:
        mine = lax.dynamic_slice_in_dim(video, jnp.where(row == 0, band - 1, 0), 1, axis=1)[:, 0]
        other = lax.ppermute(mine, "rows", [(0, 1), (1, 0)])
        return other, other
    up = [(i, i + 1) for i in range(size - 1)]
    down = [(j, i) for i, j in up]
    return lax.ppermute(video[:, -1], "rows", up), lax.ppermute(video[:, 0], "rows", down)


def other_sums(sums):
    if lax.axis_size("rows") == 2:
        return lax.ppermute(sums, "rows", [(0, 1), (1, 0)])
    return lax.psum(sums, "rows") - sums


def after(value, *others):
    return lax.optimization_barrier((value, *others))[0]


def body(video, spatial_weight, norm_gain, norm_shift, temporal_weight):
    frames, band, width, ch = video.shape
    total, here = lax.axis_size("tm"), lax.axis_index("tm")
    members = SPAN // frames
    me = jnp.reshape(here % members, (1,)).astype(jnp.int32)
    row, rows = lax.axis_index("rows"), lax.axis_size("rows")
    flags = jnp.stack([row > 0, row < rows - 1]).astype(jnp.int32)
    swaps = [[(i, i ^ k) for i in range(total)] for k in range(members)]
    onward = [(i, i + members) for i in range(total - members)]
    guest_pairs = [
        [(i, i + members - 1 + odd) for i in range(1, total - members, 2)] for odd in range(2)
    ]
    odd = me % 2

    guests = [lax.ppermute(video[f : f + 1], "tm", guest_pairs[f]) for f in range(2)]
    above, below = halo_rows(video)
    inner, part, sums = conv_call([video], spatial_weight)
    edge, sums = edge_call(flags, part, above, below, spatial_weight, sums)
    sums = sums + other_sums(sums)
    count = band * rows * width * (ch // GROUPS)
    exists = jnp.concatenate([me, jnp.ones_like(me)])
    pieces = norm_call(
        exists, inner, edge, sums, norm_gain, norm_shift, count, members, IN_SIZES
    )

    guest_sums = [lax.ppermute(sums[f : f + 1], "tm", guest_pairs[f]) for f in range(2)]
    guest_sums = guest_sums[0] + guest_sums[1]
    guest_rows = halo_rows(jnp.where(odd[0] > 0, guests[1], guests[0]))
    guest_inner, guest_part, guest_own = conv_call(guests, spatial_weight, odd)
    guest_edge, _ = edge_call(flags, guest_part, *guest_rows, spatial_weight, guest_own)
    exists = jnp.concatenate([me, (here >= members).astype(jnp.int32).reshape(1)])
    guest_pieces = norm_call(
        exists, guest_inner, guest_edge, guest_sums, norm_gain, norm_shift, count, members, IN_SIZES
    )

    def swap(four):
        return [four[0]] + [lax.ppermute(four[k], "tm", swaps[k]) for k in range(1, members)]

    results, u2s = [], []
    for i, size in enumerate(IN_SIZES):
        four = swap(pieces[i * members : (i + 1) * members])
        guest_four = swap(guest_pieces[i * members : (i + 1) * members])
        middle = functools.reduce(
            lambda acc, k: jnp.where(me[0] == (2 ^ k), four[k], acc), range(1, members), four[0]
        )
        halo = lax.ppermute(middle, "tm", onward)
        offset = 0
        for part_size in OUT_SIZES[i]:
            u2s.append(
                early_call(me, four, guest_four, halo, temporal_weight, offset, part_size)
            )
            offset += part_size
    befores = []
    for i, u2 in enumerate(u2s):
        if i >= 2:
            u2 = after(u2, befores[i - 2])
        before = lax.ppermute(u2, "tm", onward)
        befores.append(before)
        results += swap(late_call(me, u2s[i], before, temporal_weight, members))
    out = place_call(me, results, members, [n for sizes in OUT_SIZES for n in sizes])
    return out.reshape(frames, band, width, ch)


def solution(mesh):
    return jax.shard_map(
        body,
        mesh=mesh,
        in_specs=(P("tm", "rows", None, None), P(), P(), P(), P()),
        out_specs=P("tm", "rows", None, None),
        check_vma=False,
    )
```

```python
import functools

import jax
import jax.numpy as jnp
from jax import lax
from jax.experimental import pallas as pl
from jax.experimental.pallas import tpu as pltpu
from jax.sharding import PartitionSpec as P

GROUPS = 32
SPAN = 8
OWN_SIZES = (480, 480)
GUEST_SIZES = (320, 640)
OUT_SIZES = (320, 320, 192, 128)
VMEM = pltpu.VMEM
ANY = pl.ANY
F32 = jnp.float32
BF16 = jnp.bfloat16


def vspec():
    return pl.BlockSpec(memory_space=VMEM)


def params(mib):
    return pltpu.CompilerParams(vmem_limit_bytes=mib << 20)


COST = pl.CostEstimate(flops=0, bytes_accessed=0, transcendentals=0)
LONG = pl.CostEstimate(flops=20_000_000_000, bytes_accessed=0, transcendentals=0)


def hspec():
    return pl.BlockSpec(memory_space=ANY)


def hbm(value):
    return pltpu.with_memory_space_constraint(value, pltpu.HBM)


def shifted_sum(taps):
    width, ch = taps.shape[0], taps.shape[1] // 3
    column = lax.broadcasted_iota(jnp.int32, (width, ch), 0)
    left = jnp.where(column == 0, 0.0, pltpu.roll(taps[:, :ch], 1, 0))
    right = jnp.where(column == width - 1, 0.0, pltpu.roll(taps[:, 2 * ch :], width - 1, 0))
    return left + taps[:, ch : 2 * ch] + right


def fold(value):
    return jnp.sum(value.reshape(value.shape[0] // 8, 8, value.shape[1]), axis=0)


def widen(weight_ref, wide_ref):
    ch = weight_ref.shape[-1]
    wide_ref[...] = jnp.zeros_like(wide_ref)
    for out in range(2):
        for col in range(3):
            for row in range(3):
                wide_ref[
                    (out + row) * ch : (out + row + 1) * ch,
                    (out * 3 + col) * ch : (out * 3 + col + 1) * ch,
                ] = weight_ref[row, col]


def conv_rows(band, read, wide_ref, write):
    ch = wide_ref.shape[0] // 4
    for first in range(0, band, 2):
        lhs = jnp.concatenate([read(r) for r in range(first - 1, first + 3)], axis=-1)
        wide = jnp.dot(lhs, wide_ref[...], preferred_element_type=F32)
        for out in range(2):
            write(first + out, shifted_sum(wide[:, out * 3 * ch : (out + 1) * 3 * ch]))


def padded_read(band, row_of, above, below):
    row, rows = lax.axis_index("rows"), lax.axis_size("rows")

    def read(r):
        if r < 0:
            return jnp.where(row > 0, above(), jnp.zeros_like(above()))
        if r == band:
            return jnp.where(row < rows - 1, below(), jnp.zeros_like(below()))
        return row_of(r)

    return read


def conv_kernel(band, video_ref, weight_ref, out_ref, sums_ref, wide_ref):
    @pl.when(pl.program_id(0) == 0)
    def _():
        widen(weight_ref, wide_ref)

    ch = weight_ref.shape[-1]
    sums = [jnp.zeros((8, ch), F32), jnp.zeros((8, ch), F32)]

    def read(row):
        if 0 <= row < band:
            return video_ref[0, row]
        return jnp.zeros_like(video_ref[0, 0])

    def write(row, value):
        out_ref[0, row] = value
        if 0 < row < band - 1:
            sums[0] = sums[0] + fold(value)
            sums[1] = sums[1] + fold(value * value)

    conv_rows(band, read, wide_ref, write)
    sums_ref[0, 0] = sums[0]
    sums_ref[0, 1] = sums[1]


def frame_spec(*shape):
    return pl.BlockSpec((1,) + shape, lambda f, *_: (f,) + (0,) * len(shape))


def conv_call(video, weight):
    frames, band, width, ch = video.shape
    return pl.pallas_call(
        functools.partial(conv_kernel, band),
        grid=(frames,),
        in_specs=[
            frame_spec(band, width, ch),
            pl.BlockSpec(weight.shape, lambda f: (0, 0, 0, 0)),
        ],
        out_specs=[frame_spec(band, width, ch), frame_spec(2, 8, ch)],
        out_shape=[
            jax.ShapeDtypeStruct(video.shape, F32),
            jax.ShapeDtypeStruct((frames, 2, 8, ch), F32),
        ],
        scratch_shapes=[VMEM((4 * ch, 6 * ch), BF16)],
        compiler_params=params(16),
        cost_estimate=LONG,
        name="conv",
    )(hbm(video), hbm(weight))


def edge_kernel(conv_ref, above_ref, below_ref, weight_ref, sums_ref, out_ref, out_sums_ref):
    side = pl.program_id(1)
    row, rows = lax.axis_index("rows"), lax.axis_size("rows")

    @pl.when(side == 0)
    def _():
        out_sums_ref[...] = sums_ref[...]

    def add(halo_ref, tap, there):
        halo = jnp.where(there, halo_ref[0], jnp.zeros_like(halo_ref[0]))
        taps = jnp.concatenate([weight_ref[tap, col] for col in range(3)], axis=-1)
        wide = jnp.dot(halo, taps, preferred_element_type=F32)
        value = conv_ref[0, 0] + shifted_sum(wide)
        out_ref[0, 0] = value
        out_sums_ref[0, 0] += fold(value)
        out_sums_ref[0, 1] += fold(value * value)

    @pl.when(side == 0)
    def _():
        add(above_ref, 0, row > 0)

    @pl.when(side == 1)
    def _():
        add(below_ref, 2, row < rows - 1)


def edge_call(conv, above, below, weight, sums):
    frames, band, width, ch = conv.shape
    edge = pl.BlockSpec((1, 1, width, ch), lambda f, side: (f, side * (band - 1), 0, 0))
    return pl.pallas_call(
        edge_kernel,
        grid=(frames, 2),
        in_specs=[
            edge,
            frame_spec(width, ch),
            frame_spec(width, ch),
            pl.BlockSpec(weight.shape, lambda f, side: (0, 0, 0, 0)),
            frame_spec(2, 8, ch),
        ],
        out_specs=[edge, frame_spec(2, 8, ch)],
        out_shape=[
            jax.ShapeDtypeStruct(conv.shape, F32),
            jax.ShapeDtypeStruct(sums.shape, F32),
        ],
        input_output_aliases={0: 0},
        compiler_params=params(12),
        cost_estimate=COST,
        name="edge",
    )(conv, above, below, hbm(weight), sums)


def over_groups(value, per_group):
    lane = lax.broadcasted_iota(jnp.int32, value.shape, 1)
    lanes = value.shape[1]
    step = 1
    while step < per_group:
        value = value + pltpu.roll(value, lanes - step, 1)
        step *= 2
    value = jnp.where(lane % per_group == 0, value, 0.0)
    step = 1
    while step < per_group:
        value = value + pltpu.roll(value, step, 1)
        step *= 2
    return value


def norm_frame(conv_ref, frame, sums, count, gain_ref, shift_ref, hidden_ref, alive=None):
    band, _, ch = conv_ref.shape[1:]
    total = [
        over_groups(jnp.broadcast_to(jnp.sum(x, axis=0, keepdims=True), (8, ch)), ch // GROUPS)
        for x in sums
    ]
    mean = total[0] / count
    var = total[1] / count - mean * mean
    scale = (lax.rsqrt(var + 1e-05) * gain_ref[...])[:1]
    mean = mean[:1]
    shift = shift_ref[...]

    @pl.loop(0, band)
    def _(row):
        v = (conv_ref[frame, row] - mean) * scale + shift
        v = 0.5 * v * (1.0 + jnp.tanh(0.5 * v))
        if alive is not None:
            v = jnp.where(alive, v, 0.0)
        hidden_ref[frame, row] = v.astype(BF16)


def piece_copies(hidden_ref, frame, outs, sizes, members, sem):
    frames, band, width, ch = hidden_ref.shape
    flat = hidden_ref.reshape(frames, band * width, ch)
    me = lax.axis_index("tm") % members
    copies, offset = [], 0
    for i, size in enumerate(sizes):
        for k in range(members):
            n = i * members + k
            start = pl.multiple_of((me ^ k) * sum(sizes) + offset, 16)
            copies.append(
                pltpu.make_async_copy(
                    flat.at[frame, pl.ds(start, size)], outs[n].at[frame], sem.at[n, frame]
                )
            )
        offset += size
    return copies


def norm_kernel(count, members, sizes, conv_ref, own_ref, other_ref, above_ref, below_ref, gain_ref, shift_ref, packet_ref, *refs):
    outs, (hidden_ref, sem) = refs[:-2], refs[-2:]
    frames, band, width, ch = conv_ref.shape
    for frame in range(frames):
        sums = [own_ref[frame, i] + other_ref[frame, i] for i in range(2)]
        packet_ref[frame, :width] = above_ref[frame]
        packet_ref[frame, width : 2 * width] = below_ref[frame]
        for i in range(2):
            rest = sums[i]
            for part in range(3):
                short = rest.astype(BF16).astype(F32)
                rest = rest - short
                at = 2 * width + (i * 3 + part) * 16
                packet_ref[frame, at : at + 16] = jnp.concatenate(
                    [short, jnp.zeros_like(short)], axis=0
                ).astype(BF16)
        norm_frame(conv_ref, frame, sums, count, gain_ref, shift_ref, hidden_ref)
        for copy in piece_copies(hidden_ref, frame, outs, sizes, members, sem):
            copy.start()
    for frame in range(frames):
        for copy in piece_copies(hidden_ref, frame, outs, sizes, members, sem):
            copy.wait()


def piece_shapes(frames, members, sizes, ch):
    return [pltpu.HBM((frames, size, ch), BF16) for size in sizes for _ in range(members)]


def norm_call(conv, own, other, above, below, gain, shift, count, members, sizes):
    frames, band, width, ch = conv.shape
    pieces = members * len(sizes)
    return pl.pallas_call(
        functools.partial(norm_kernel, count, members, sizes),
        in_specs=[vspec()] * 7,
        out_specs=[vspec()] + [hspec()] * pieces,
        out_shape=[jax.ShapeDtypeStruct((frames, 2 * width + 96, ch), BF16)]
        + piece_shapes(frames, members, sizes, ch),
        scratch_shapes=[
            VMEM((frames, band, width, ch), BF16),
            pltpu.SemaphoreType.DMA((pieces, frames)),
        ],
        compiler_params=params(16),
        cost_estimate=COST,
        name="norm",
    )(conv, own, other, above, below, gain.reshape(1, ch), shift.reshape(1, ch))


def guest_kernel(count, members, sizes, video_hbm, packet_ref, weight_ref, gain_ref, shift_ref, *refs):
    outs, (video_ref, conv_ref, hidden_ref, wide_ref, in_sem, sem) = refs[:-6], refs[-6:]
    frames, band, width, ch = video_hbm.shape
    here = lax.axis_index("tm")

    @pl.when(jnp.logical_and(here >= members, here % 2 == 0))
    def _():
        loads = [
            pltpu.make_async_copy(video_hbm.at[f], video_ref.at[f], in_sem.at[f])
            for f in range(frames)
        ]
        for copy in loads:
            copy.start()
        widen(weight_ref, wide_ref)
        for frame in range(frames):
            loads[frame].wait()

            def write(row, value):
                conv_ref[frame, row] = value

            read = padded_read(
                band,
                lambda r: video_ref[frame, r],
                lambda: packet_ref[frame, :width],
                lambda: packet_ref[frame, width : 2 * width],
            )
            conv_rows(band, read, wide_ref, write)
            sums = []
            for i in range(2):
                at = 2 * width + i * 48
                parts = packet_ref[frame, at : at + 48].astype(F32)
                sums.append(parts[:16] + parts[16:32] + parts[32:])
            norm_frame(conv_ref, frame, sums, count, gain_ref, shift_ref, hidden_ref)
            for copy in piece_copies(hidden_ref, frame, outs, sizes, members, sem):
                copy.start()
        for frame in range(frames):
            for copy in piece_copies(hidden_ref, frame, outs, sizes, members, sem):
                copy.wait()

    @pl.when(here < members)
    def _():
        hidden_ref[...] = jnp.zeros_like(hidden_ref)
        for frame in range(frames):
            for copy in piece_copies(hidden_ref, frame, outs, sizes, members, sem):
                copy.start()
        for frame in range(frames):
            for copy in piece_copies(hidden_ref, frame, outs, sizes, members, sem):
                copy.wait()


def guest_call(video, packet, weight, gain, shift, count, members, sizes):
    frames, band, width, ch = video.shape
    pieces = members * len(sizes)
    return pl.pallas_call(
        functools.partial(guest_kernel, count, members, sizes),
        in_specs=[hspec()] + [vspec()] * 4,
        out_specs=[hspec()] * pieces,
        out_shape=piece_shapes(frames, members, sizes, ch),
        scratch_shapes=[
            VMEM(video.shape, BF16),
            VMEM(video.shape, F32),
            VMEM(video.shape, BF16),
            VMEM((4 * ch, 6 * ch), BF16),
            pltpu.SemaphoreType.DMA((frames,)),
            pltpu.SemaphoreType.DMA((pieces, frames)),
        ],
        compiler_params=params(24),
        cost_estimate=LONG,
        name="guest",
    )(video, packet, weight, gain.reshape(1, ch), shift.reshape(1, ch))


def pair_weights(weight_ref, layer, wide_ref):
    ch = weight_ref.shape[-1]
    wide_ref[...] = jnp.zeros_like(wide_ref)
    for out in range(2):
        for tap in range(3):
            row = out + 2 - tap
            wide_ref[row * ch : (row + 1) * ch, out * ch : (out + 1) * ch] = weight_ref[layer, tap]


def pair(read, write, time, dilation, wide_ref):
    ch = wide_ref.shape[1] // 2
    frames = [read(time + (a - 2) * dilation) for a in range(4)]
    both = jnp.dot(jnp.concatenate(frames, axis=-1), wide_ref[...], preferred_element_type=F32)
    write(time, (both[:, :ch] + frames[2].astype(F32)).astype(BF16))
    write(time + dilation, (both[:, ch:] + frames[3].astype(F32)).astype(BF16))


def early_kernel(members, spans, size, *refs):
    own, guest = spans
    count = [len({i for i, *_ in kind}) for kind in spans]
    pieces, refs = refs[: count[0] * members], refs[count[0] * members :]
    halos, refs = refs[: count[0]], refs[count[0] :]
    guests, refs = refs[: count[1] * members], refs[count[1] * members :]
    weight_ref, out_ref, u0_ref, u1_ref, wide_ref = refs
    step = pieces[0].shape[0]
    lead = SPAN - 2
    me = lax.axis_index("tm") % members
    for i, source, target, rows in own:
        for k in range(members):
            u0_ref[pl.ds(lead + (me ^ k) * step, step), target : target + rows] = pieces[
                i * members + k
            ][:, source : source + rows]
        u0_ref[2:4, target : target + rows] = halos[i][:, source : source + rows]
    for i, source, target, rows in guest:
        for k in range(members):

            @pl.when((me ^ k) % 2 == 0)
            def _():
                u0_ref[pl.ds(2 * (me ^ k), step), target : target + rows] = guests[
                    i * members + k
                ][:, source : source + rows]

    pair_weights(weight_ref, 0, wide_ref)

    def write1(t, value):
        u1_ref[t + 4] = value

    def write2(t, value):
        out_ref[t] = value

    for time in range(-4, SPAN, 2):
        pair(lambda t: u0_ref[t + lead], write1, time, 1, wide_ref)
    pair_weights(weight_ref, 1, wide_ref)
    for time in range(0, SPAN, 4):
        for odd in range(2):
            pair(lambda t: u1_ref[t + 4], write2, time + odd, 2, wide_ref)


def overlaps(sizes, first, last):
    found, at = [], 0
    for i, size in enumerate(sizes):
        low, high = max(first, at), min(last, at + size)
        if low < high:
            found.append((i, low - at, low - first, high - low))
        at += size
    return found


def early_call(own, halos, guest, weight, first, size):
    members, ch = len(own[0]), weight.shape[-1]
    spans, arrays = [], []
    for kind, (blocks, sizes) in enumerate(((own, OWN_SIZES), (guest, GUEST_SIZES))):
        parts = overlaps(sizes, first, first + size)
        base = parts[0][0]
        spans.append([(i - base, *rest) for i, *rest in parts])
        arrays += sum([blocks[i] for i, *_ in parts], [])
        if kind == 0:
            arrays += [halos[i] for i, *_ in parts]
    return pl.pallas_call(
        functools.partial(early_kernel, members, spans, size),
        in_specs=[vspec()] * (len(arrays) + 1),
        out_specs=vspec(),
        out_shape=jax.ShapeDtypeStruct((SPAN, size, ch), BF16),
        scratch_shapes=[
            VMEM((2 * SPAN - 2, size, ch), BF16),
            VMEM((SPAN + 4, size, ch), BF16),
            VMEM((4 * ch, 2 * ch), BF16),
        ],
        compiler_params=params(16),
        cost_estimate=COST,
        name="early",
    )(*arrays, weight)


def late_kernel(members, own_ref, halo_ref, weight_ref, *refs):
    outs, (u3_ref, wide_ref) = refs[:members], refs[members:]
    step = outs[0].shape[0]
    pair_weights(weight_ref, 2, wide_ref)

    def write3(t, value):
        u3_ref[t] = value

    for time in range(4):
        pair(
            lambda t: own_ref[t] if t >= 0 else halo_ref[t + SPAN], write3, time, 4, wide_ref
        )
    me = lax.axis_index("tm") % members
    for k in range(members):
        outs[k][...] = u3_ref[pl.ds((me ^ k) * step, step)]


def late_call(own, halo, weight, members):
    frames, size, ch = own.shape
    return pl.pallas_call(
        functools.partial(late_kernel, members),
        in_specs=[vspec()] * 3,
        out_specs=[vspec()] * members,
        out_shape=[jax.ShapeDtypeStruct((frames // members, size, ch), BF16)] * members,
        scratch_shapes=[VMEM(own.shape, BF16), VMEM((4 * ch, 2 * ch), BF16)],
        compiler_params=params(12),
        cost_estimate=COST,
        name="late",
    )(own, halo, weight)


def place_kernel(members, sizes, *refs):
    pieces, (out_ref, sem) = refs[: members * len(sizes)], refs[members * len(sizes) :]
    me = lax.axis_index("tm") % members
    copies = []
    offset = 0
    for i, size in enumerate(sizes):
        for k in range(members):
            n = i * members + k
            place = out_ref.at[:, me ^ k, pl.ds(offset, size)]
            copies.append(pltpu.make_async_copy(pieces[n], place, sem.at[n]))
        offset += size
    for copy in copies:
        copy.start()
    for copy in copies:
        copy.wait()


def place_call(pieces, members, sizes):
    frames, _, ch = pieces[0].shape
    return pl.pallas_call(
        functools.partial(place_kernel, members, sizes),
        in_specs=[vspec()] * len(pieces),
        out_specs=pl.BlockSpec(memory_space=ANY),
        out_shape=jax.ShapeDtypeStruct((frames, members, sum(sizes), ch), BF16),
        scratch_shapes=[pltpu.SemaphoreType.DMA((len(pieces),))],
        compiler_params=params(8),
        cost_estimate=COST,
        name="place",
    )(*pieces)


def halo_rows(video):
    size, row = lax.axis_size("rows"), lax.axis_index("rows")
    band = video.shape[1]
    if size == 2:
        mine = lax.dynamic_slice_in_dim(video, jnp.where(row == 0, band - 1, 0), 1, axis=1)[:, 0]
        other = lax.ppermute(mine, "rows", [(0, 1), (1, 0)])
        return other, other
    up = [(i, i + 1) for i in range(size - 1)]
    down = [(j, i) for i, j in up]
    return lax.ppermute(video[:, -1], "rows", up), lax.ppermute(video[:, 0], "rows", down)


def other_sums(sums):
    if lax.axis_size("rows") == 2:
        return lax.ppermute(sums, "rows", [(0, 1), (1, 0)])
    return lax.psum(sums, "rows") - sums


def after(value, *others):
    return lax.optimization_barrier((value, *others))[0]


def body(video, spatial_weight, norm_gain, norm_shift, temporal_weight):
    frames, band, width, ch = video.shape
    total = lax.axis_size("tm")
    me = lax.axis_index("tm") % (SPAN // frames)
    rows = lax.axis_size("rows")
    members = SPAN // frames
    swaps = [[(i, i ^ k) for i in range(total)] for k in range(members)]
    onward = [(i, i + members) for i in range(total - members)]
    guest_pairs = [(i, i + members - 1) for i in range(1, total - members, 2)]
    guest_swaps = [[(i, i ^ k) for i in range(0, total, 2)] for k in range(members)]

    guest_video = lax.ppermute(video, "tm", guest_pairs)
    above, below = halo_rows(video)
    conv, sums = conv_call(video, spatial_weight)
    conv, sums = edge_call(conv, above, below, spatial_weight, sums)
    count = band * rows * width * (ch // GROUPS)
    packet, *pieces = norm_call(
        conv, sums, other_sums(sums), above, below, norm_gain, norm_shift, count, members, OWN_SIZES
    )
    guest_packet = lax.ppermute(packet, "tm", guest_pairs)

    def swap(four, pairs, waits=None):
        got = [four[0]]
        for k in range(1, members):
            value = four[k] if waits is None else after(four[k], waits[k])
            got.append(lax.ppermute(value, "tm", pairs[k]))
        return got

    def blocks(arrays):
        return [arrays[i : i + members] for i in range(0, len(arrays), members)]

    def forward(value):
        value = after(value, passed[-2]) if len(passed) > 1 else value
        passed.append(lax.ppermute(value, "tm", onward))
        return passed[-1]

    guest_pieces = guest_call(
        guest_video, guest_packet, spatial_weight, norm_gain, norm_shift, count, members, GUEST_SIZES
    )
    passed, own, halos, guest = [], [], [], []
    for four, guest_four in zip(blocks(pieces), blocks(guest_pieces), strict=True):
        own.append(swap(four, swaps, guest[-1] if own else None))
        four = after(own[-1], guest_pieces[0])
        middle = functools.reduce(
            lambda acc, k: jnp.where(me == (2 ^ k), four[k], acc), range(1, members), four[0]
        )
        halos.append(forward(middle))
        guest.append(swap(guest_four, guest_swaps, own[-1] if guest else None))
    results, first = [], 0
    for size in OUT_SIZES:
        u2 = early_call(own, halos, guest, temporal_weight, first, size)
        late = late_call(u2, forward(u2), temporal_weight, members)
        results.append(swap(late, swaps, results[-1] if results else None))
        first += size
    out = place_call(sum(results, []), members, OUT_SIZES)
    return out.reshape(frames, band, width, ch)


def solution(mesh):
    return jax.shard_map(
        body,
        mesh=mesh,
        in_specs=(P("tm", "rows", None, None), P(), P(), P(), P()),
        out_specs=P("tm", "rows", None, None),
        check_vma=False,
    )
```

```python
import functools

import jax
import jax.numpy as jnp
from jax import lax
from jax.experimental import pallas as pl
from jax.experimental.pallas import tpu as pltpu
from jax.sharding import PartitionSpec as P

GROUPS = 32
SPAN = 8
GUEST_PARTS = (26, 34)
OUT_PARTS = (26, 16, 10, 8)
VMEM = pltpu.VMEM
ANY = pl.ANY
F32 = jnp.float32
BF16 = jnp.bfloat16


def vspec():
    return pl.BlockSpec(memory_space=VMEM)


def params(mib):
    return pltpu.CompilerParams(vmem_limit_bytes=mib << 20)


COST = pl.CostEstimate(flops=0, bytes_accessed=0, transcendentals=0)
LONG = pl.CostEstimate(flops=20_000_000_000, bytes_accessed=0, transcendentals=0)


def hspec():
    return pl.BlockSpec(memory_space=ANY)


def hbm(value):
    return pltpu.with_memory_space_constraint(value, pltpu.HBM)


def shifted_sum(taps):
    width, ch = taps.shape[0], taps.shape[1] // 3
    column = lax.broadcasted_iota(jnp.int32, (width, ch), 0)
    left = jnp.where(column == 0, 0.0, pltpu.roll(taps[:, :ch], 1, 0))
    right = jnp.where(column == width - 1, 0.0, pltpu.roll(taps[:, 2 * ch :], width - 1, 0))
    return left + taps[:, ch : 2 * ch] + right


def fold(value):
    return jnp.sum(value.reshape(value.shape[0] // 8, 8, value.shape[1]), axis=0)


def widen(weight_ref, wide_ref):
    ch = weight_ref.shape[-1]
    wide_ref[...] = jnp.zeros_like(wide_ref)
    for out in range(2):
        for col in range(3):
            for row in range(3):
                wide_ref[
                    (out + row) * ch : (out + row + 1) * ch,
                    (out * 3 + col) * ch : (out * 3 + col + 1) * ch,
                ] = weight_ref[row, col]


def conv_rows(band, read, wide_ref, write):
    ch = wide_ref.shape[0] // 4
    for first in range(0, band, 2):
        lhs = jnp.concatenate([read(r) for r in range(first - 1, first + 3)], axis=-1)
        wide = jnp.dot(lhs, wide_ref[...], preferred_element_type=F32)
        for out in range(2):
            write(first + out, shifted_sum(wide[:, out * 3 * ch : (out + 1) * 3 * ch]))


def padded_read(band, row_of, above, below):
    row, rows = lax.axis_index("rows"), lax.axis_size("rows")

    def read(r):
        if r < 0:
            return jnp.where(row > 0, above(), jnp.zeros_like(above()))
        if r == band:
            return jnp.where(row < rows - 1, below(), jnp.zeros_like(below()))
        return row_of(r)

    return read


def conv_kernel(band, video_ref, weight_ref, out_ref, sums_ref, wide_ref):
    @pl.when(pl.program_id(0) == 0)
    def _():
        widen(weight_ref, wide_ref)

    ch = weight_ref.shape[-1]
    sums = [jnp.zeros((8, ch), F32), jnp.zeros((8, ch), F32)]

    def read(row):
        if 0 <= row < band:
            return video_ref[0, row]
        return jnp.zeros_like(video_ref[0, 0])

    def write(row, value):
        out_ref[0, row] = value
        if 0 < row < band - 1:
            sums[0] = sums[0] + fold(value)
            sums[1] = sums[1] + fold(value * value)

    conv_rows(band, read, wide_ref, write)
    sums_ref[0, 0] = sums[0]
    sums_ref[0, 1] = sums[1]


def frame_spec(*shape):
    return pl.BlockSpec((1,) + shape, lambda f, *_: (f,) + (0,) * len(shape))


def conv_call(video, weight):
    frames, band, width, ch = video.shape
    return pl.pallas_call(
        functools.partial(conv_kernel, band),
        grid=(frames,),
        in_specs=[
            frame_spec(band, width, ch),
            pl.BlockSpec(weight.shape, lambda f: (0, 0, 0, 0)),
        ],
        out_specs=[frame_spec(band, width, ch), frame_spec(2, 8, ch)],
        out_shape=[
            jax.ShapeDtypeStruct(video.shape, F32),
            jax.ShapeDtypeStruct((frames, 2, 8, ch), F32),
        ],
        scratch_shapes=[VMEM((4 * ch, 6 * ch), BF16)],
        compiler_params=params(16),
        cost_estimate=LONG,
        name="conv",
    )(hbm(video), hbm(weight))


def edge_kernel(conv_ref, above_ref, below_ref, weight_ref, sums_ref, out_ref, out_sums_ref):
    side = pl.program_id(1)
    row, rows = lax.axis_index("rows"), lax.axis_size("rows")

    @pl.when(side == 0)
    def _():
        out_sums_ref[...] = sums_ref[...]

    def add(halo_ref, tap, there):
        halo = jnp.where(there, halo_ref[0], jnp.zeros_like(halo_ref[0]))
        taps = jnp.concatenate([weight_ref[tap, col] for col in range(3)], axis=-1)
        wide = jnp.dot(halo, taps, preferred_element_type=F32)
        value = conv_ref[0, 0] + shifted_sum(wide)
        out_ref[0, 0] = value
        out_sums_ref[0, 0] += fold(value)
        out_sums_ref[0, 1] += fold(value * value)

    @pl.when(side == 0)
    def _():
        add(above_ref, 0, row > 0)

    @pl.when(side == 1)
    def _():
        add(below_ref, 2, row < rows - 1)


def edge_call(conv, above, below, weight, sums):
    frames, band, width, ch = conv.shape
    edge = pl.BlockSpec((1, 1, width, ch), lambda f, side: (f, side * (band - 1), 0, 0))
    return pl.pallas_call(
        edge_kernel,
        grid=(frames, 2),
        in_specs=[
            edge,
            frame_spec(width, ch),
            frame_spec(width, ch),
            pl.BlockSpec(weight.shape, lambda f, side: (0, 0, 0, 0)),
            frame_spec(2, 8, ch),
        ],
        out_specs=[edge, frame_spec(2, 8, ch)],
        out_shape=[
            jax.ShapeDtypeStruct(conv.shape, F32),
            jax.ShapeDtypeStruct(sums.shape, F32),
        ],
        input_output_aliases={0: 0},
        compiler_params=params(12),
        cost_estimate=COST,
        name="edge",
    )(conv, above, below, hbm(weight), sums)


def over_groups(value, per_group):
    lane = lax.broadcasted_iota(jnp.int32, value.shape, 1)
    lanes = value.shape[1]
    step = 1
    while step < per_group:
        value = value + pltpu.roll(value, lanes - step, 1)
        step *= 2
    value = jnp.where(lane % per_group == 0, value, 0.0)
    step = 1
    while step < per_group:
        value = value + pltpu.roll(value, step, 1)
        step *= 2
    return value


def norm_frame(conv_ref, frame, sums, count, gain_ref, shift_ref, hidden_ref, alive=None):
    band, _, ch = conv_ref.shape[1:]
    total = [
        over_groups(jnp.broadcast_to(jnp.sum(x, axis=0, keepdims=True), (8, ch)), ch // GROUPS)
        for x in sums
    ]
    mean = total[0] / count
    var = total[1] / count - mean * mean
    scale = (lax.rsqrt(var + 1e-05) * gain_ref[...])[:1]
    mean = mean[:1]
    shift = shift_ref[...]

    @pl.loop(0, band)
    def _(row):
        v = (conv_ref[frame, row] - mean) * scale + shift
        v = 0.5 * v * (1.0 + jnp.tanh(0.5 * v))
        if alive is not None:
            v = jnp.where(alive, v, 0.0)
        hidden_ref[frame, row] = v.astype(BF16)


def piece_copies(hidden_ref, frame, outs, members, sem):
    frames, band, width, ch = hidden_ref.shape
    flat = hidden_ref.reshape(frames, band * width, ch)
    me = lax.axis_index("tm") % members
    quarter = band * width // members
    copies = []
    for k, blocks in enumerate(outs):
        offset = 0
        for block in blocks:
            rows = pl.ds(pl.multiple_of((me ^ k) * quarter + offset, 16), block.shape[1])
            copies.append(
                pltpu.make_async_copy(
                    flat.at[frame, rows], block.at[frame], sem.at[len(copies), frame]
                )
            )
            offset += block.shape[1]
    return copies


def norm_kernel(count, members, rows, conv_ref, own_ref, other_ref, gain_ref, shift_ref, *refs):
    row_refs, packet_ref, (hidden_ref, sem) = refs[:rows], refs[rows], refs[-2:]
    outs = [[ref] for ref in refs[rows + 1 : -2]]
    frames, band, width, ch = conv_ref.shape
    for frame in range(frames):
        sums = [own_ref[frame, i] + other_ref[frame, i] for i in range(2)]
        for i, ref in enumerate(row_refs):
            packet_ref[frame, i * width : (i + 1) * width] = ref[frame]
        for i in range(2):
            rest = sums[i]
            for part in range(3):
                short = rest.astype(BF16).astype(F32)
                rest = rest - short
                at = rows * width + (i * 3 + part) * 16
                packet_ref[frame, at : at + 16] = jnp.concatenate(
                    [short, jnp.zeros_like(short)], axis=0
                ).astype(BF16)
        norm_frame(conv_ref, frame, sums, count, gain_ref, shift_ref, hidden_ref)
        for copy in piece_copies(hidden_ref, frame, outs, members, sem):
            copy.start()
    for frame in range(frames):
        for copy in piece_copies(hidden_ref, frame, outs, members, sem):
            copy.wait()


def norm_call(conv, own, other, halo_rows, gain, shift, count, members):
    frames, band, width, ch = conv.shape
    rows = len(halo_rows)
    return pl.pallas_call(
        functools.partial(norm_kernel, count, members, rows),
        in_specs=[vspec()] * (5 + rows),
        out_specs=[vspec()] + [hspec()] * members,
        out_shape=[jax.ShapeDtypeStruct((frames, rows * width + 96, ch), BF16)]
        + [pltpu.HBM((frames, band * width // members, ch), BF16)] * members,
        scratch_shapes=[
            VMEM((frames, band, width, ch), BF16),
            pltpu.SemaphoreType.DMA((members, frames)),
        ],
        compiler_params=params(16),
        cost_estimate=COST,
        name="norm",
    )(conv, own, other, gain.reshape(1, ch), shift.reshape(1, ch), *halo_rows)


def guest_kernel(count, members, video_hbm, packet_ref, weight_ref, gain_ref, shift_ref, *refs):
    keep_ref, mate_ref, *away_refs = refs[:-6]
    video_ref, conv_ref, hidden_ref, wide_ref, in_sem, sem = refs[-6:]
    outs = [[keep_ref], [mate_ref]] + [[ref.at[k] for ref in away_refs] for k in range(2)]
    frames, band, width, ch = video_hbm.shape
    rows = (packet_ref.shape[1] - 96) // width
    here = lax.axis_index("tm")

    @pl.when(jnp.logical_and(here >= members, here % 2 == 0))
    def _():
        loads = [
            pltpu.make_async_copy(video_hbm.at[f], video_ref.at[f], in_sem.at[f])
            for f in range(frames)
        ]
        for copy in loads:
            copy.start()
        widen(weight_ref, wide_ref)
        for frame in range(frames):
            loads[frame].wait()

            def write(row, value):
                conv_ref[frame, row] = value

            read = padded_read(
                band,
                lambda r: video_ref[frame, r],
                lambda: packet_ref[frame, :width],
                lambda: packet_ref[frame, (rows - 1) * width : rows * width],
            )
            conv_rows(band, read, wide_ref, write)
            sums = []
            for i in range(2):
                at = rows * width + i * 48
                parts = packet_ref[frame, at : at + 48].astype(F32)
                sums.append(parts[:16] + parts[16:32] + parts[32:])
            norm_frame(conv_ref, frame, sums, count, gain_ref, shift_ref, hidden_ref)
            for copy in piece_copies(hidden_ref, frame, outs, members, sem):
                copy.start()
        for frame in range(frames):
            for copy in piece_copies(hidden_ref, frame, outs, members, sem):
                copy.wait()

    @pl.when(here < members)
    def _():
        hidden_ref[...] = jnp.zeros_like(hidden_ref)
        for frame in range(frames):
            for copy in piece_copies(hidden_ref, frame, outs, members, sem):
                copy.start()
        for frame in range(frames):
            for copy in piece_copies(hidden_ref, frame, outs, members, sem):
                copy.wait()


def guest_call(video, packet, weight, gain, shift, count, members, sizes):
    frames, band, width, ch = video.shape
    piece = (frames, band * width // members, ch)
    shapes = [piece, piece] + [(2, frames, size, ch) for size in sizes]
    return pl.pallas_call(
        functools.partial(guest_kernel, count, members),
        in_specs=[hspec()] + [vspec()] * 4,
        out_specs=[hspec()] * len(shapes),
        out_shape=[pltpu.HBM(shape, BF16) for shape in shapes],
        scratch_shapes=[
            VMEM(video.shape, BF16),
            VMEM(video.shape, F32),
            VMEM(video.shape, BF16),
            VMEM((4 * ch, 6 * ch), BF16),
            pltpu.SemaphoreType.DMA((frames,)),
            pltpu.SemaphoreType.DMA((2 + 2 * len(sizes), frames)),
        ],
        compiler_params=params(24),
        cost_estimate=LONG,
        name="guest",
    )(video, packet, weight, gain.reshape(1, ch), shift.reshape(1, ch))


def pack_kernel(weight_ref, out_ref):
    ch = weight_ref.shape[-1]
    out_ref[...] = jnp.zeros_like(out_ref)
    for layer in range(3):
        for out in range(2):
            for tap in range(3):
                row = out + 2 - tap
                out_ref[layer, row * ch : (row + 1) * ch, out * ch : (out + 1) * ch] = weight_ref[
                    layer, tap
                ]


def pack_call(weight):
    layers, _, ch, _ = weight.shape
    return pl.pallas_call(
        pack_kernel,
        in_specs=[vspec()],
        out_specs=vspec(),
        out_shape=jax.ShapeDtypeStruct((layers, 4 * ch, 2 * ch), BF16),
        compiler_params=params(8),
        cost_estimate=LONG,
        name="pack",
    )(weight)


def pair(read, write, time, layer, wide_ref):
    ch = wide_ref.shape[2] // 2
    dilation = 2**layer
    frames = [read(time + (a - 2) * dilation) for a in range(4)]
    both = jnp.dot(jnp.concatenate(frames, axis=-1), wide_ref[layer], preferred_element_type=F32)
    write(time, (both[:, :ch] + frames[2].astype(F32)).astype(BF16))
    write(time + dilation, (both[:, ch:] + frames[3].astype(F32)).astype(BF16))


def ahead_kernel(members, *refs):
    pieces, (wide_ref, out_ref, u0_ref) = refs[:members], refs[members:]
    step = pieces[0].shape[0]
    me = lax.axis_index("tm") % members
    for k in range(members):
        u0_ref[pl.ds((me ^ k) * step, step)] = pieces[k][...]

    def write1(t, value):
        out_ref[t - 2] = value

    for time in range(2, SPAN, 2):
        pair(lambda t: u0_ref[t], write1, time, 0, wide_ref)


def ahead_call(own, wide):
    members = len(own)
    _, size, ch = own[0].shape
    return pl.pallas_call(
        functools.partial(ahead_kernel, members),
        in_specs=[vspec()] * (members + 1),
        out_specs=vspec(),
        out_shape=jax.ShapeDtypeStruct((SPAN - 2, size, ch), BF16),
        scratch_shapes=[VMEM((SPAN, size, ch), BF16)],
        compiler_params=params(16),
        cost_estimate=LONG,
        name="ahead",
    )(*own, wide)


def early_kernel(members, plan, first, *refs):
    arrays, (ahead_ref, wide_ref, out_ref, u0_ref, u1_ref) = refs[: len(plan)], refs[len(plan) :]
    size = out_ref.shape[1]
    lead = SPAN - 2
    me = lax.axis_index("tm") % members
    for ref, (kind, k, source, target, rows) in zip(arrays, plan):
        value = ref.at[0] if len(ref.shape) == 4 else ref
        step = value.shape[0]
        here, there = slice(target, target + rows), slice(source, source + rows)
        if kind == "own":

            @pl.when(me == k)
            def _():
                u0_ref[lead : lead + step, here] = value[:, there]

        elif kind == "middle":
            u0_ref[2:4, here] = value[:, there]
        else:

            @pl.when((me ^ k) % 2 == 0)
            def _():
                u0_ref[pl.ds(2 * (me ^ k), step), here] = value[:, there]

    def write1(t, value):
        u1_ref[t + 4] = value

    def read1(t):
        return u1_ref[t + 4] if t < 2 else ahead_ref[t - 2, first : first + size]

    def write2(t, value):
        out_ref[t] = value

    for time in range(-4, 2, 2):
        pair(lambda t: u0_ref[t + lead], write1, time, 0, wide_ref)
    for time in range(0, SPAN, 4):
        for odd in range(2):
            pair(read1, write2, time + odd, 1, wide_ref)


def early_call(sources, ahead, wide, members, first, size):
    plan, arrays = [], []
    for kind, k, blocks in sources:
        at = 0
        for block in blocks:
            rows = block.shape[-2]
            low, high = max(first, at), min(first + size, at + rows)
            if low < high:
                plan.append((kind, k, low - at, low - first, high - low))
                arrays.append(block)
            at += rows
    ch = wide.shape[-1] // 2
    return pl.pallas_call(
        functools.partial(early_kernel, members, plan, first),
        in_specs=[vspec()] * (len(arrays) + 2),
        out_specs=vspec(),
        out_shape=jax.ShapeDtypeStruct((SPAN, size, ch), BF16),
        scratch_shapes=[VMEM((SPAN, size, ch), BF16), VMEM((6, size, ch), BF16)],
        compiler_params=params(16),
        cost_estimate=COST,
        name="early",
    )(*arrays, ahead, wide)


def late_kernel(members, own_ref, halo_ref, wide_ref, *refs):
    outs, u3_ref = refs[:-1], refs[-1]
    step = outs[0].shape[0]
    me = lax.axis_index("tm") % members

    def write3(t, value):
        u3_ref[t] = value

    for time in range(4):
        pair(
            lambda t: own_ref[t] if t >= 0 else halo_ref[t + SPAN], write3, time, 2, wide_ref
        )
    for k in range(members):
        outs[k][...] = u3_ref[pl.ds((me ^ k) * step, step)]


def late_call(own, halo, wide, members):
    frames, size, ch = own.shape
    return pl.pallas_call(
        functools.partial(late_kernel, members),
        in_specs=[vspec()] * 3,
        out_specs=[vspec()] * members,
        out_shape=[jax.ShapeDtypeStruct((frames // members, size, ch), BF16)] * members,
        scratch_shapes=[VMEM(own.shape, BF16)],
        compiler_params=params(12),
        cost_estimate=COST,
        name="late",
    )(own, halo, wide)


def place_kernel(members, sizes, *refs):
    pieces, (out_ref, sem) = refs[: members * len(sizes)], refs[members * len(sizes) :]
    me = lax.axis_index("tm") % members
    copies = []
    offset = 0
    for i, size in enumerate(sizes):
        for k in range(members):
            n = i * members + k
            place = out_ref.at[:, me ^ k, pl.ds(offset, size)]
            copies.append(pltpu.make_async_copy(pieces[n], place, sem.at[n]))
        offset += size
    for copy in copies:
        copy.start()
    for copy in copies:
        copy.wait()


def place_call(pieces, members, sizes):
    frames, _, ch = pieces[0].shape
    return pl.pallas_call(
        functools.partial(place_kernel, members, sizes),
        in_specs=[vspec()] * len(pieces),
        out_specs=pl.BlockSpec(memory_space=ANY),
        out_shape=jax.ShapeDtypeStruct((frames, members, sum(sizes), ch), BF16),
        scratch_shapes=[pltpu.SemaphoreType.DMA((len(pieces),))],
        compiler_params=params(8),
        cost_estimate=COST,
        name="place",
    )(*pieces)


def halo_rows(video):
    size, row = lax.axis_size("rows"), lax.axis_index("rows")
    band = video.shape[1]
    if size == 2:
        mine = lax.dynamic_slice_in_dim(video, jnp.where(row == 0, band - 1, 0), 1, axis=1)[:, 0]
        other = lax.ppermute(mine, "rows", [(0, 1), (1, 0)])
        return other, other
    up = [(i, i + 1) for i in range(size - 1)]
    down = [(j, i) for i, j in up]
    return lax.ppermute(video[:, -1], "rows", up), lax.ppermute(video[:, 0], "rows", down)


def other_sums(sums):
    if lax.axis_size("rows") == 2:
        return lax.ppermute(sums, "rows", [(0, 1), (1, 0)])
    return lax.psum(sums, "rows") - sums


def after(value, *others):
    return lax.optimization_barrier((value, *others))[0]


def body(video, spatial_weight, norm_gain, norm_shift, temporal_weight):
    frames, band, width, ch = video.shape
    total = lax.axis_size("tm")
    me = lax.axis_index("tm") % (SPAN // frames)
    rows = lax.axis_size("rows")
    members = SPAN // frames
    swaps = [[(i, i ^ k) for i in range(total)] for k in range(members)]
    onward = [(i, i + members) for i in range(total - members)]
    guest_pairs = [(i, i + members - 1) for i in range(1, total - members, 2)]
    guest_swaps = [[(i, i ^ k) for i in range(0, total, 2)] for k in range(members)]

    guest_video = lax.ppermute(video, "tm", guest_pairs)
    above, below = halo_rows(video)
    conv, sums = conv_call(video, spatial_weight)
    conv, sums = edge_call(conv, above, below, spatial_weight, sums)
    count = band * rows * width * (ch // GROUPS)
    quarter = band * width // members
    guest_sizes, out_sizes = [
        [quarter * part // 60 for part in parts] for parts in (GUEST_PARTS, OUT_PARTS)
    ]
    halo_list = [above] if above is below else [above, below]
    packet, *pieces = norm_call(
        conv, sums, other_sums(sums), halo_list, norm_gain, norm_shift, count, members
    )

    def swap(four, waits=None):
        got = [four[0]]
        for k in range(1, members):
            value = four[k] if waits is None else after(four[k], waits[k])
            got.append(lax.ppermute(value, "tm", swaps[k]))
        return got

    own = swap(pieces)
    guest_packet = lax.ppermute(packet, "tm", guest_pairs)
    keep, mate, *aways = guest_call(
        guest_video, guest_packet, spatial_weight, norm_gain, norm_shift, count, members, guest_sizes
    )
    wide = pack_call(after(temporal_weight, keep))
    crossed = [lax.ppermute(away, "tm", guest_swaps[2]) for away in aways]
    guest = [[keep], [lax.ppermute(mate, "tm", guest_swaps[1])], crossed]
    four = after(own, wide)
    middle = functools.reduce(
        lambda acc, k: jnp.where(me == (2 ^ k), four[k], acc), range(1, members), four[0]
    )
    halo = lax.ppermute(middle, "tm", onward)
    ahead = ahead_call(own, after(wide, middle, crossed[0]))
    guest.append(
        [lax.ppermute(after(block[1], ahead), "tm", guest_swaps[1]) for block in crossed]
    )
    sources = [("own", k, [own[k]]) for k in range(members)]
    sources += [("guest", k, guest[k]) for k in range(members)]
    sources.append(("middle", 0, [halo]))
    results, passed, first = [], [], 0
    for i, size in enumerate(out_sizes):
        u2 = early_call(sources, ahead, wide, members, first, size)
        passed.append(lax.ppermute(after(u2, passed[-2]) if i > 1 else u2, "tm", onward))
        late = late_call(u2, passed[-1], wide, members)
        results.append(swap(late, results[-1] if results else None))
        first += size
    out = place_call(sum(results, []), members, out_sizes)
    return out.reshape(frames, band, width, ch)


def solution(mesh):
    return jax.shard_map(
        body,
        mesh=mesh,
        in_specs=(P("tm", "rows", None, None), P(), P(), P(), P()),
        out_specs=P("tm", "rows", None, None),
        check_vma=False,
    )
```

```python
import functools

import jax
import jax.numpy as jnp
from jax import lax
from jax.experimental import pallas as pl
from jax.experimental.pallas import tpu as pltpu
from jax.sharding import PartitionSpec as P

GROUPS = 32
SPAN = 8
OWN_PARTS = (42, 18)
GUEST_PARTS = (42, 18)
OUT_PARTS = (26, 16, 10, 8)
VMEM = pltpu.VMEM
ANY = pl.ANY
F32 = jnp.float32
BF16 = jnp.bfloat16


def vspec():
    return pl.BlockSpec(memory_space=VMEM)


def params(mib):
    return pltpu.CompilerParams(vmem_limit_bytes=mib << 20)


COST = pl.CostEstimate(flops=0, bytes_accessed=0, transcendentals=0)
LONG = pl.CostEstimate(flops=20_000_000_000, bytes_accessed=0, transcendentals=0)


def hspec():
    return pl.BlockSpec(memory_space=ANY)


def hbm(value):
    return pltpu.with_memory_space_constraint(value, pltpu.HBM)


def shifted_sum(taps):
    width, ch = taps.shape[0], taps.shape[1] // 3
    column = lax.broadcasted_iota(jnp.int32, (width, ch), 0)
    left = jnp.where(column == 0, 0.0, pltpu.roll(taps[:, :ch], 1, 0))
    right = jnp.where(column == width - 1, 0.0, pltpu.roll(taps[:, 2 * ch :], width - 1, 0))
    return left + taps[:, ch : 2 * ch] + right


def fold(value):
    return jnp.sum(value.reshape(value.shape[0] // 8, 8, value.shape[1]), axis=0)


def widen(weight_ref, wide_ref):
    ch = weight_ref.shape[-1]
    wide_ref[...] = jnp.zeros_like(wide_ref)
    for out in range(2):
        for col in range(3):
            for row in range(3):
                wide_ref[
                    (out + row) * ch : (out + row + 1) * ch,
                    (out * 3 + col) * ch : (out * 3 + col + 1) * ch,
                ] = weight_ref[row, col]


def conv_rows(band, read, wide_ref, write):
    ch = wide_ref.shape[0] // 4
    for first in range(0, band, 2):
        lhs = jnp.concatenate([read(r) for r in range(first - 1, first + 3)], axis=-1)
        wide = jnp.dot(lhs, wide_ref[...], preferred_element_type=F32)
        for out in range(2):
            write(first + out, shifted_sum(wide[:, out * 3 * ch : (out + 1) * 3 * ch]))


def padded_read(band, row_of, above, below):
    row, rows = lax.axis_index("rows"), lax.axis_size("rows")

    def read(r):
        if r < 0:
            return jnp.where(row > 0, above(), jnp.zeros_like(above()))
        if r == band:
            return jnp.where(row < rows - 1, below(), jnp.zeros_like(below()))
        return row_of(r)

    return read


def conv_kernel(band, video_ref, weight_ref, out_ref, sums_ref, wide_ref):
    @pl.when(pl.program_id(0) == 0)
    def _():
        widen(weight_ref, wide_ref)

    ch = weight_ref.shape[-1]
    sums = [jnp.zeros((8, ch), F32), jnp.zeros((8, ch), F32)]

    def read(row):
        if 0 <= row < band:
            return video_ref[0, row]
        return jnp.zeros_like(video_ref[0, 0])

    def write(row, value):
        out_ref[0, row] = value
        if 0 < row < band - 1:
            sums[0] = sums[0] + fold(value)
            sums[1] = sums[1] + fold(value * value)

    conv_rows(band, read, wide_ref, write)
    sums_ref[0, 0] = sums[0]
    sums_ref[0, 1] = sums[1]


def frame_spec(*shape):
    return pl.BlockSpec((1,) + shape, lambda f, *_: (f,) + (0,) * len(shape))


def conv_call(video, weight):
    frames, band, width, ch = video.shape
    return pl.pallas_call(
        functools.partial(conv_kernel, band),
        grid=(frames,),
        in_specs=[
            frame_spec(band, width, ch),
            pl.BlockSpec(weight.shape, lambda f: (0, 0, 0, 0)),
        ],
        out_specs=[frame_spec(band, width, ch), frame_spec(2, 8, ch)],
        out_shape=[
            jax.ShapeDtypeStruct(video.shape, F32),
            jax.ShapeDtypeStruct((frames, 2, 8, ch), F32),
        ],
        scratch_shapes=[VMEM((4 * ch, 6 * ch), BF16)],
        compiler_params=params(16),
        cost_estimate=LONG,
        name="conv",
    )(hbm(video), hbm(weight))


def edge_kernel(conv_ref, above_ref, below_ref, weight_ref, sums_ref, out_ref, out_sums_ref):
    side = pl.program_id(1)
    row, rows = lax.axis_index("rows"), lax.axis_size("rows")

    @pl.when(side == 0)
    def _():
        out_sums_ref[...] = sums_ref[...]

    def add(halo_ref, tap, there):
        halo = jnp.where(there, halo_ref[0], jnp.zeros_like(halo_ref[0]))
        taps = jnp.concatenate([weight_ref[tap, col] for col in range(3)], axis=-1)
        wide = jnp.dot(halo, taps, preferred_element_type=F32)
        value = conv_ref[0, 0] + shifted_sum(wide)
        out_ref[0, 0] = value
        out_sums_ref[0, 0] += fold(value)
        out_sums_ref[0, 1] += fold(value * value)

    @pl.when(side == 0)
    def _():
        add(above_ref, 0, row > 0)

    @pl.when(side == 1)
    def _():
        add(below_ref, 2, row < rows - 1)


def edge_call(conv, above, below, weight, sums):
    frames, band, width, ch = conv.shape
    edge = pl.BlockSpec((1, 1, width, ch), lambda f, side: (f, side * (band - 1), 0, 0))
    return pl.pallas_call(
        edge_kernel,
        grid=(frames, 2),
        in_specs=[
            edge,
            frame_spec(width, ch),
            frame_spec(width, ch),
            pl.BlockSpec(weight.shape, lambda f, side: (0, 0, 0, 0)),
            frame_spec(2, 8, ch),
        ],
        out_specs=[edge, frame_spec(2, 8, ch)],
        out_shape=[
            jax.ShapeDtypeStruct(conv.shape, F32),
            jax.ShapeDtypeStruct(sums.shape, F32),
        ],
        input_output_aliases={0: 0},
        compiler_params=params(12),
        cost_estimate=COST,
        name="edge",
    )(conv, above, below, hbm(weight), sums)


def over_groups(value, per_group):
    lane = lax.broadcasted_iota(jnp.int32, value.shape, 1)
    lanes = value.shape[1]
    step = 1
    while step < per_group:
        value = value + pltpu.roll(value, lanes - step, 1)
        step *= 2
    value = jnp.where(lane % per_group == 0, value, 0.0)
    step = 1
    while step < per_group:
        value = value + pltpu.roll(value, step, 1)
        step *= 2
    return value


def norm_of(sums, count, gain_ref, shift_ref):
    ch = gain_ref.shape[-1]
    total = [
        over_groups(jnp.broadcast_to(jnp.sum(x, axis=0, keepdims=True), (8, ch)), ch // GROUPS)
        for x in sums
    ]
    mean = total[0] / count
    var = total[1] / count - mean * mean
    scale = (lax.rsqrt(var + 1e-05) * gain_ref[...])[:1]
    mean = mean[:1]
    shift = shift_ref[...]

    def apply(value):
        v = (value - mean) * scale + shift
        return (0.5 * v * (1.0 + jnp.tanh(0.5 * v))).astype(BF16)

    return apply


def piece_copies(hidden_ref, frame, outs, members, sem):
    frames, band, width, ch = hidden_ref.shape
    flat = hidden_ref.reshape(frames, band * width, ch)
    me = lax.axis_index("tm") % members
    quarter = band * width // members
    copies = []
    for k, blocks in enumerate(outs):
        offset = 0
        for block in blocks:
            rows = pl.ds(pl.multiple_of((me ^ k) * quarter + offset, 16), block.shape[1])
            copies.append(
                pltpu.make_async_copy(
                    flat.at[frame, rows], block.at[frame], sem.at[len(copies), frame]
                )
            )
            offset += block.shape[1]
    return copies


def norm_kernel(count, members, rows, conv_ref, own_ref, other_ref, gain_ref, shift_ref, *refs):
    row_refs, packet_ref, (hidden_ref, sem) = refs[:rows], refs[rows], refs[-2:]
    outs = [refs[rows + 1 + k : -2 : members] for k in range(members)]
    frames, band, width, ch = conv_ref.shape
    for frame in range(frames):
        sums = [own_ref[frame, i] + other_ref[frame, i] for i in range(2)]
        for i, ref in enumerate(row_refs):
            packet_ref[frame, i * width : (i + 1) * width] = ref[frame]
        for i in range(2):
            rest = sums[i]
            for part in range(3):
                short = rest.astype(BF16).astype(F32)
                rest = rest - short
                at = rows * width + (i * 3 + part) * 16
                packet_ref[frame, at : at + 16] = jnp.concatenate(
                    [short, jnp.zeros_like(short)], axis=0
                ).astype(BF16)
        apply = norm_of(sums, count, gain_ref, shift_ref)

        @pl.loop(0, band)
        def _(row):
            hidden_ref[frame, row] = apply(conv_ref[frame, row])

        for copy in piece_copies(hidden_ref, frame, outs, members, sem):
            copy.start()
    for frame in range(frames):
        for copy in piece_copies(hidden_ref, frame, outs, members, sem):
            copy.wait()


def norm_call(conv, own, other, halo_rows, gain, shift, count, members, sizes):
    frames, band, width, ch = conv.shape
    rows = len(halo_rows)
    return pl.pallas_call(
        functools.partial(norm_kernel, count, members, rows),
        in_specs=[vspec()] * (5 + rows),
        out_specs=[vspec()] + [hspec()] * (members * len(sizes)),
        out_shape=[jax.ShapeDtypeStruct((frames, rows * width + 96, ch), BF16)]
        + [pltpu.HBM((frames, size, ch), BF16) for size in sizes for _ in range(members)],
        scratch_shapes=[
            VMEM((frames, band, width, ch), BF16),
            pltpu.SemaphoreType.DMA((members * len(sizes), frames)),
        ],
        compiler_params=params(16),
        cost_estimate=COST,
        name="norm",
    )(conv, own, other, gain.reshape(1, ch), shift.reshape(1, ch), *halo_rows)


def guest_kernel(count, members, video_hbm, packet_ref, weight_ref, gain_ref, shift_ref, *refs):
    keep_ref, mate_ref, *away_refs = refs[:-5]
    video_ref, hidden_ref, wide_ref, in_sem, sem = refs[-5:]
    outs = [[keep_ref], [mate_ref]] + [[ref.at[k] for ref in away_refs] for k in range(2)]
    frames, band, width, ch = video_hbm.shape
    rows = (packet_ref.shape[1] - 96) // width
    here = lax.axis_index("tm")

    @pl.when(jnp.logical_and(here >= members, here % 2 == 0))
    def _():
        loads = [
            pltpu.make_async_copy(video_hbm.at[f], video_ref.at[f], in_sem.at[f])
            for f in range(frames)
        ]
        for copy in loads:
            copy.start()
        widen(weight_ref, wide_ref)
        for frame in range(frames):
            loads[frame].wait()
            sums = []
            for i in range(2):
                at = rows * width + i * 48
                parts = packet_ref[frame, at : at + 48].astype(F32)
                sums.append(parts[:16] + parts[16:32] + parts[32:])
            apply = norm_of(sums, count, gain_ref, shift_ref)

            def write(row, value):
                hidden_ref[frame, row] = apply(value)

            read = padded_read(
                band,
                lambda r: video_ref[frame, r],
                lambda: packet_ref[frame, :width],
                lambda: packet_ref[frame, (rows - 1) * width : rows * width],
            )
            conv_rows(band, read, wide_ref, write)
            for copy in piece_copies(hidden_ref, frame, outs, members, sem):
                copy.start()
        for frame in range(frames):
            for copy in piece_copies(hidden_ref, frame, outs, members, sem):
                copy.wait()

    @pl.when(here < members)
    def _():
        hidden_ref[...] = jnp.zeros_like(hidden_ref)
        for frame in range(frames):
            for copy in piece_copies(hidden_ref, frame, outs, members, sem):
                copy.start()
        for frame in range(frames):
            for copy in piece_copies(hidden_ref, frame, outs, members, sem):
                copy.wait()


def guest_call(video, packet, weight, gain, shift, count, members, sizes):
    frames, band, width, ch = video.shape
    piece = (frames, band * width // members, ch)
    shapes = [piece, piece] + [(2, frames, size, ch) for size in sizes]
    return pl.pallas_call(
        functools.partial(guest_kernel, count, members),
        in_specs=[hspec()] + [vspec()] * 4,
        out_specs=[hspec()] * len(shapes),
        out_shape=[pltpu.HBM(shape, BF16) for shape in shapes],
        scratch_shapes=[
            VMEM(video.shape, BF16),
            VMEM(video.shape, BF16),
            VMEM((4 * ch, 6 * ch), BF16),
            pltpu.SemaphoreType.DMA((frames,)),
            pltpu.SemaphoreType.DMA((2 + 2 * len(sizes), frames)),
        ],
        compiler_params=params(24),
        cost_estimate=LONG,
        name="guest",
    )(video, packet, weight, gain.reshape(1, ch), shift.reshape(1, ch))


def pack_kernel(weight_ref, out_ref):
    ch = weight_ref.shape[-1]
    out_ref[...] = jnp.zeros_like(out_ref)
    for layer in range(3):
        for out in range(2):
            for tap in range(3):
                row = out + 2 - tap
                out_ref[layer, row * ch : (row + 1) * ch, out * ch : (out + 1) * ch] = weight_ref[
                    layer, tap
                ]


def pack_call(weight):
    layers, _, ch, _ = weight.shape
    return pl.pallas_call(
        pack_kernel,
        in_specs=[vspec()],
        out_specs=vspec(),
        out_shape=jax.ShapeDtypeStruct((layers, 4 * ch, 2 * ch), BF16),
        compiler_params=params(8),
        cost_estimate=LONG,
        name="pack",
    )(weight)


def pair(read, write, time, layer, wide_ref):
    ch = wide_ref.shape[2] // 2
    dilation = 2**layer
    frames = [read(time + (a - 2) * dilation) for a in range(4)]
    both = jnp.dot(jnp.concatenate(frames, axis=-1), wide_ref[layer], preferred_element_type=F32)
    write(time, (both[:, :ch] + frames[2].astype(F32)).astype(BF16))
    write(time + dilation, (both[:, ch:] + frames[3].astype(F32)).astype(BF16))


def ahead_kernel(members, *refs):
    pieces, (wide_ref, out_ref, u0_ref) = refs[:members], refs[members:]
    step = pieces[0].shape[0]
    me = lax.axis_index("tm") % members
    for k in range(members):
        u0_ref[pl.ds((me ^ k) * step, step)] = pieces[k][...]

    def write1(t, value):
        out_ref[t - 2] = value

    for time in range(2, SPAN, 2):
        pair(lambda t: u0_ref[t], write1, time, 0, wide_ref)


def ahead_call(own, wide, cost):
    members = len(own)
    _, size, ch = own[0].shape
    return pl.pallas_call(
        functools.partial(ahead_kernel, members),
        in_specs=[vspec()] * (members + 1),
        out_specs=vspec(),
        out_shape=jax.ShapeDtypeStruct((SPAN - 2, size, ch), BF16),
        scratch_shapes=[VMEM((SPAN, size, ch), BF16)],
        compiler_params=params(16),
        cost_estimate=cost,
        name="ahead",
    )(*own, wide)


def early_kernel(members, plan, first, *refs):
    arrays, (ahead_ref, wide_ref, out_ref, u0_ref, u1_ref) = refs[: len(plan)], refs[len(plan) :]
    size = out_ref.shape[1]
    lead = SPAN - 2
    me = lax.axis_index("tm") % members
    for ref, (kind, k, source, target, rows) in zip(arrays, plan):
        value = ref.at[0] if len(ref.shape) == 4 else ref
        step = value.shape[0]
        here, there = slice(target, target + rows), slice(source, source + rows)
        if kind == "own":

            @pl.when(me == k)
            def _():
                u0_ref[lead : lead + step, here] = value[:, there]

        elif kind == "middle":
            u0_ref[2:4, here] = value[:, there]
        else:

            @pl.when((me ^ k) % 2 == 0)
            def _():
                u0_ref[pl.ds(2 * (me ^ k), step), here] = value[:, there]

    def write1(t, value):
        u1_ref[t + 4] = value

    def read1(t):
        return u1_ref[t + 4] if t < 2 else ahead_ref[t - 2, first : first + size]

    def write2(t, value):
        out_ref[t] = value

    for time in range(-4, 2, 2):
        pair(lambda t: u0_ref[t + lead], write1, time, 0, wide_ref)
    for time in range(0, SPAN, 4):
        for odd in range(2):
            pair(read1, write2, time + odd, 1, wide_ref)


def early_call(sources, aheads, wide, members, first, size):
    plan, arrays = [], []
    start, ahead = first, aheads[0]
    for block in aheads[1:]:
        if start >= ahead.shape[1]:
            start, ahead = start - ahead.shape[1], block
    for kind, k, blocks in sources:
        at = 0
        for block in blocks:
            rows = block.shape[-2]
            low, high = max(first, at), min(first + size, at + rows)
            if low < high:
                plan.append((kind, k, low - at, low - first, high - low))
                arrays.append(block)
            at += rows
    ch = wide.shape[-1] // 2
    return pl.pallas_call(
        functools.partial(early_kernel, members, plan, start),
        in_specs=[vspec()] * (len(arrays) + 2),
        out_specs=vspec(),
        out_shape=jax.ShapeDtypeStruct((SPAN, size, ch), BF16),
        scratch_shapes=[VMEM((SPAN, size, ch), BF16), VMEM((6, size, ch), BF16)],
        compiler_params=params(16),
        cost_estimate=COST,
        name="early",
    )(*arrays, ahead, wide)


def late_kernel(members, own_ref, halo_ref, wide_ref, *refs):
    outs, u3_ref = refs[:-1], refs[-1]
    step = outs[0].shape[0]
    me = lax.axis_index("tm") % members

    def write3(t, value):
        u3_ref[t] = value

    for time in range(4):
        pair(
            lambda t: own_ref[t] if t >= 0 else halo_ref[t + SPAN], write3, time, 2, wide_ref
        )
    for k in range(members):
        outs[k][...] = u3_ref[pl.ds((me ^ k) * step, step)]


def late_call(own, halo, wide, members):
    frames, size, ch = own.shape
    return pl.pallas_call(
        functools.partial(late_kernel, members),
        in_specs=[vspec()] * 3,
        out_specs=[vspec()] * members,
        out_shape=[jax.ShapeDtypeStruct((frames // members, size, ch), BF16)] * members,
        scratch_shapes=[VMEM(own.shape, BF16)],
        compiler_params=params(12),
        cost_estimate=COST,
        name="late",
    )(own, halo, wide)


def place_kernel(members, offsets, *refs):
    count = members * len(offsets)
    pieces, (out_ref, sem) = refs[:count], refs[-2:]
    me = lax.axis_index("tm") % members
    copies = []
    for i, offset in enumerate(offsets):
        for k in range(members):
            n = i * members + k
            rows = pl.ds(offset, pieces[n].shape[1])
            copies.append(
                pltpu.make_async_copy(pieces[n], out_ref.at[:, me ^ k, rows], sem.at[n])
            )
    for copy in copies:
        copy.start()
    for copy in copies:
        copy.wait()


def place_call(chunks, offsets, quarter, before=None):
    members = len(chunks[0])
    frames, _, ch = chunks[0][0].shape
    pieces = sum(chunks, [])
    shape = jax.ShapeDtypeStruct((frames, members, quarter, ch), BF16)
    return pl.pallas_call(
        functools.partial(place_kernel, members, offsets),
        in_specs=[vspec()] * len(pieces) + [hspec()] * (before is not None),
        out_specs=hspec(),
        out_shape=pltpu.HBM(shape.shape, BF16),
        input_output_aliases={} if before is None else {len(pieces): 0},
        scratch_shapes=[pltpu.SemaphoreType.DMA((len(pieces),))],
        compiler_params=params(8),
        cost_estimate=COST,
        name="place",
    )(*pieces, *([] if before is None else [hbm(before)]))


def halo_rows(video):
    size, row = lax.axis_size("rows"), lax.axis_index("rows")
    band = video.shape[1]
    if size == 2:
        mine = lax.dynamic_slice_in_dim(video, jnp.where(row == 0, band - 1, 0), 1, axis=1)[:, 0]
        other = lax.ppermute(mine, "rows", [(0, 1), (1, 0)])
        return other, other
    up = [(i, i + 1) for i in range(size - 1)]
    down = [(j, i) for i, j in up]
    return lax.ppermute(video[:, -1], "rows", up), lax.ppermute(video[:, 0], "rows", down)


def other_sums(sums):
    if lax.axis_size("rows") == 2:
        return lax.ppermute(sums, "rows", [(0, 1), (1, 0)])
    return lax.psum(sums, "rows") - sums


def after(value, *others):
    return lax.optimization_barrier((value, *others))[0]


def body(video, spatial_weight, norm_gain, norm_shift, temporal_weight):
    frames, band, width, ch = video.shape
    total = lax.axis_size("tm")
    me = lax.axis_index("tm") % (SPAN // frames)
    rows = lax.axis_size("rows")
    members = SPAN // frames
    swaps = [[(i, i ^ k) for i in range(total)] for k in range(members)]
    onward = [(i, i + members) for i in range(total - members)]
    guest_pairs = [(i, i + members - 1) for i in range(1, total - members, 2)]
    guest_swaps = [[(i, i ^ k) for i in range(0, total, 2)] for k in range(members)]

    guest_video = lax.ppermute(video, "tm", guest_pairs)
    above, below = halo_rows(video)
    conv, sums = conv_call(video, spatial_weight)
    conv, sums = edge_call(conv, above, below, spatial_weight, sums)
    count = band * rows * width * (ch // GROUPS)
    quarter = band * width // members
    own_sizes, guest_sizes, out_sizes = [
        [quarter * part // 60 for part in parts] for parts in (OWN_PARTS, GUEST_PARTS, OUT_PARTS)
    ]
    halo_list = [above] if above is below else [above, below]
    packet, *pieces = norm_call(
        conv, sums, other_sums(sums), halo_list, norm_gain, norm_shift, count, members, own_sizes
    )

    def swap(four, waits=None):
        got = [four[0]]
        for k in range(1, members):
            value = four[k] if waits is None else after(four[k], waits[k])
            got.append(lax.ppermute(value, "tm", swaps[k]))
        return got

    guest_packet = lax.ppermute(packet, "tm", guest_pairs)
    keep, mate, *aways = guest_call(
        guest_video, guest_packet, spatial_weight, norm_gain, norm_shift, count, members, guest_sizes
    )
    wide = pack_call(after(temporal_weight, keep))
    sources = [(kind, k, []) for kind in ("own", "guest") for k in range(members)]
    sources.append(("middle", 0, []))

    def add(start, arrays):
        for (_, _, blocks), array in zip(sources[start:], arrays):
            blocks.append(array)

    aheads, passed, results = [], [], []

    def block(i, gate):
        four = pieces[i * members : (i + 1) * members]
        own = swap(four, [gate] * members if i else None)
        crossed = lax.ppermute(after(aways[i], own[2]) if i else aways[i], "tm", guest_swaps[2])
        four = own if i else after(own, wide)
        middle = functools.reduce(
            lambda acc, k: jnp.where(me == (2 ^ k), four[k], acc), range(1, members), four[0]
        )
        add(0, own)
        add(2 * members, [lax.ppermute(middle, "tm", onward)])
        if i == 0:
            add(members, [keep, lax.ppermute(after(mate, wide), "tm", guest_swaps[1])])
        waits = [middle] if i else [middle, crossed]
        aheads.append(ahead_call(own, after(wide, *waits), COST if i else LONG))
        forward = crossed[1] if i else after(crossed[1], aheads[0])
        add(members + 2, [crossed, lax.ppermute(forward, "tm", guest_swaps[1])])

    block(0, None)
    first = 0
    for i, size in enumerate(out_sizes):
        u2 = early_call(sources, aheads, wide, members, first, size)
        if i == 0:
            block(1, aheads[0])
        if i > 1:
            u2 = after(u2, passed[0] if i == 2 else late[0])
        passed.append(lax.ppermute(u2, "tm", onward))
        following = late_call(u2, passed[-1], wide, members)
        results.append(swap(following, results[-1] if results else None))
        late = following if i < 2 else late
        first += size
    offsets = [sum(out_sizes[:i]) for i in range(len(out_sizes))]
    out = place_call(results[:2], offsets[:2], quarter)
    out = place_call(results[2:], offsets[2:], quarter, out)
    return out.reshape(frames, band, width, ch)


def solution(mesh):
    return jax.shard_map(
        body,
        mesh=mesh,
        in_specs=(P("tm", "rows", None, None), P(), P(), P(), P()),
        out_specs=P("tm", "rows", None, None),
        check_vma=False,
    )
```

```python
import functools

import jax
import jax.numpy as jnp
from jax import lax
from jax.experimental import pallas as pl
from jax.experimental.pallas import tpu as pltpu
from jax.sharding import PartitionSpec as P

GROUPS = 32
SPAN = 8
OWN_PARTS = (42, 18)
GUEST_PARTS = (42, 18)
OUT_PARTS = (28, 14, 10, 8)
VMEM = pltpu.VMEM
ANY = pl.ANY
F32 = jnp.float32
BF16 = jnp.bfloat16


def vspec():
    return pl.BlockSpec(memory_space=VMEM)


def params(mib):
    return pltpu.CompilerParams(vmem_limit_bytes=mib << 20)


COST = pl.CostEstimate(flops=0, bytes_accessed=0, transcendentals=0)
LONG = pl.CostEstimate(flops=20_000_000_000, bytes_accessed=0, transcendentals=0)


def hspec():
    return pl.BlockSpec(memory_space=ANY)


def hbm(value):
    return pltpu.with_memory_space_constraint(value, pltpu.HBM)


def shifted_sum(taps):
    width, ch = taps.shape[0], taps.shape[1] // 3
    column = lax.broadcasted_iota(jnp.int32, (width, ch), 0)
    left = jnp.where(column == 0, 0.0, pltpu.roll(taps[:, :ch], 1, 0))
    right = jnp.where(column == width - 1, 0.0, pltpu.roll(taps[:, 2 * ch :], width - 1, 0))
    return left + taps[:, ch : 2 * ch] + right


def fold(value):
    return jnp.sum(value.reshape(value.shape[0] // 8, 8, value.shape[1]), axis=0)


def widen(weight_ref, wide_ref):
    ch = weight_ref.shape[-1]
    wide_ref[...] = jnp.zeros_like(wide_ref)
    for out in range(2):
        for col in range(3):
            for row in range(3):
                wide_ref[
                    (out + row) * ch : (out + row + 1) * ch,
                    (out * 3 + col) * ch : (out * 3 + col + 1) * ch,
                ] = weight_ref[row, col]


def conv_rows(band, read, wide_ref, write):
    ch = wide_ref.shape[0] // 4
    for first in range(0, band, 2):
        lhs = jnp.concatenate([read(r) for r in range(first - 1, first + 3)], axis=-1)
        wide = jnp.dot(lhs, wide_ref[...], preferred_element_type=F32)
        for out in range(2):
            write(first + out, shifted_sum(wide[:, out * 3 * ch : (out + 1) * 3 * ch]))


def padded_read(band, row_of, above, below):
    row, rows = lax.axis_index("rows"), lax.axis_size("rows")

    def read(r):
        if r < 0:
            return jnp.where(row > 0, above(), jnp.zeros_like(above()))
        if r == band:
            return jnp.where(row < rows - 1, below(), jnp.zeros_like(below()))
        return row_of(r)

    return read


def conv_kernel(band, video_ref, weight_ref, out_ref, sums_ref, wide_ref):
    @pl.when(pl.program_id(0) == 0)
    def _():
        widen(weight_ref, wide_ref)

    ch = weight_ref.shape[-1]
    sums = [jnp.zeros((8, ch), F32), jnp.zeros((8, ch), F32)]

    def read(row):
        if 0 <= row < band:
            return video_ref[0, row]
        return jnp.zeros_like(video_ref[0, 0])

    def write(row, value):
        out_ref[0, row] = value
        if 0 < row < band - 1:
            sums[0] = sums[0] + fold(value)
            sums[1] = sums[1] + fold(value * value)

    conv_rows(band, read, wide_ref, write)
    sums_ref[0, 0] = sums[0]
    sums_ref[0, 1] = sums[1]


def frame_spec(*shape):
    return pl.BlockSpec((1,) + shape, lambda f, *_: (f,) + (0,) * len(shape))


def conv_call(video, weight):
    frames, band, width, ch = video.shape
    return pl.pallas_call(
        functools.partial(conv_kernel, band),
        grid=(frames,),
        in_specs=[
            frame_spec(band, width, ch),
            pl.BlockSpec(weight.shape, lambda f: (0, 0, 0, 0)),
        ],
        out_specs=[frame_spec(band, width, ch), frame_spec(2, 8, ch)],
        out_shape=[
            jax.ShapeDtypeStruct(video.shape, F32),
            jax.ShapeDtypeStruct((frames, 2, 8, ch), F32),
        ],
        scratch_shapes=[VMEM((4 * ch, 6 * ch), BF16)],
        compiler_params=params(16),
        cost_estimate=LONG,
        name="conv",
    )(hbm(video), hbm(weight))


def edge_kernel(conv_ref, above_ref, below_ref, weight_ref, sums_ref, out_ref, out_sums_ref):
    frames, band = conv_ref.shape[:2]
    row, rows = lax.axis_index("rows"), lax.axis_size("rows")
    sides = ((0, above_ref, 0, row > 0), (band - 1, below_ref, 2, row < rows - 1))
    for frame in range(frames):
        total, square = sums_ref[frame, 0], sums_ref[frame, 1]
        for place, halo_ref, tap, there in sides:
            halo = jnp.where(there, halo_ref[frame], jnp.zeros_like(halo_ref[frame]))
            taps = jnp.concatenate([weight_ref[tap, col] for col in range(3)], axis=-1)
            wide = jnp.dot(halo, taps, preferred_element_type=F32)
            value = conv_ref[frame, place] + shifted_sum(wide)
            out_ref[frame, place] = value
            total = total + fold(value)
            square = square + fold(value * value)
        out_sums_ref[frame, 0] = total
        out_sums_ref[frame, 1] = square


def edge_call(conv, above, below, weight, sums):
    return pl.pallas_call(
        edge_kernel,
        in_specs=[vspec()] * 5,
        out_specs=[vspec()] * 2,
        out_shape=[
            jax.ShapeDtypeStruct(conv.shape, F32),
            jax.ShapeDtypeStruct(sums.shape, F32),
        ],
        input_output_aliases={0: 0},
        compiler_params=params(12),
        cost_estimate=COST,
        name="edge",
    )(conv, above, below, weight, sums)


def over_groups(value, per_group):
    lane = lax.broadcasted_iota(jnp.int32, value.shape, 1)
    lanes = value.shape[1]
    step = 1
    while step < per_group:
        value = value + pltpu.roll(value, lanes - step, 1)
        step *= 2
    value = jnp.where(lane % per_group == 0, value, 0.0)
    step = 1
    while step < per_group:
        value = value + pltpu.roll(value, step, 1)
        step *= 2
    return value


def norm_of(sums, count, gain_ref, shift_ref):
    ch = gain_ref.shape[-1]
    total = [
        over_groups(jnp.broadcast_to(jnp.sum(x, axis=0, keepdims=True), (8, ch)), ch // GROUPS)
        for x in sums
    ]
    mean = total[0] / count
    var = total[1] / count - mean * mean
    scale = (lax.rsqrt(var + 1e-05) * gain_ref[...])[:1]
    mean = mean[:1]
    shift = shift_ref[...]

    def apply(value):
        v = (value - mean) * scale + shift
        return (0.5 * v * (1.0 + jnp.tanh(0.5 * v))).astype(BF16)

    return apply


def piece_copies(hidden_ref, frame, outs, members, sem):
    frames, band, width, ch = hidden_ref.shape
    flat = hidden_ref.reshape(frames, band * width, ch)
    me = lax.axis_index("tm") % members
    quarter = band * width // members
    copies = []
    for k, blocks in enumerate(outs):
        offset = 0
        for block in blocks:
            rows = pl.ds(pl.multiple_of((me ^ k) * quarter + offset, 16), block.shape[1])
            copies.append(
                pltpu.make_async_copy(
                    flat.at[frame, rows], block.at[frame], sem.at[len(copies), frame]
                )
            )
            offset += block.shape[1]
    return copies


def norm_kernel(count, members, rows, conv_ref, own_ref, other_ref, gain_ref, shift_ref, *refs):
    row_refs, packet_ref, (hidden_ref, sem) = refs[:rows], refs[rows], refs[-2:]
    outs = [refs[rows + 1 + k : -2 : members] for k in range(members)]
    frames, band, width, ch = conv_ref.shape
    for frame in range(frames):
        sums = [own_ref[frame, i] + other_ref[frame, i] for i in range(2)]
        for i, ref in enumerate(row_refs):
            packet_ref[frame, i * width : (i + 1) * width] = ref[frame]
        for i in range(2):
            rest = sums[i]
            for part in range(3):
                short = rest.astype(BF16).astype(F32)
                rest = rest - short
                at = rows * width + (i * 3 + part) * 16
                packet_ref[frame, at : at + 16] = jnp.concatenate(
                    [short, jnp.zeros_like(short)], axis=0
                ).astype(BF16)
        apply = norm_of(sums, count, gain_ref, shift_ref)

        @pl.loop(0, band)
        def _(row):
            hidden_ref[frame, row] = apply(conv_ref[frame, row])

        for copy in piece_copies(hidden_ref, frame, outs, members, sem):
            copy.start()
    for frame in range(frames):
        for copy in piece_copies(hidden_ref, frame, outs, members, sem):
            copy.wait()


def norm_call(conv, own, other, halo_rows, gain, shift, count, members, sizes):
    frames, band, width, ch = conv.shape
    rows = len(halo_rows)
    return pl.pallas_call(
        functools.partial(norm_kernel, count, members, rows),
        in_specs=[vspec()] * (5 + rows),
        out_specs=[vspec()] + [hspec()] * (members * len(sizes)),
        out_shape=[jax.ShapeDtypeStruct((frames, rows * width + 96, ch), BF16)]
        + [pltpu.HBM((frames, size, ch), BF16) for size in sizes for _ in range(members)],
        scratch_shapes=[
            VMEM((frames, band, width, ch), BF16),
            pltpu.SemaphoreType.DMA((members * len(sizes), frames)),
        ],
        compiler_params=params(16),
        cost_estimate=COST,
        name="norm",
    )(conv, own, other, gain.reshape(1, ch), shift.reshape(1, ch), *halo_rows)


def guest_kernel(count, members, video_ref, packet_ref, weight_ref, gain_ref, shift_ref, *refs):
    keep_ref, mate_ref, *away_refs = refs[:-3]
    hidden_ref, wide_ref, sem = refs[-3:]
    outs = [[keep_ref], [mate_ref]] + [[ref.at[k] for ref in away_refs] for k in range(2)]
    frames, band, width, ch = video_ref.shape
    rows = (packet_ref.shape[1] - 96) // width
    here = lax.axis_index("tm")

    @pl.when(jnp.logical_and(here >= members, here % 2 == 0))
    def _():
        widen(weight_ref, wide_ref)
        for frame in range(frames):
            sums = []
            for i in range(2):
                at = rows * width + i * 48
                parts = packet_ref[frame, at : at + 48].astype(F32)
                sums.append(parts[:16] + parts[16:32] + parts[32:])
            apply = norm_of(sums, count, gain_ref, shift_ref)

            def write(row, value):
                hidden_ref[frame, row] = apply(value)

            read = padded_read(
                band,
                lambda r: video_ref[frame, r],
                lambda: packet_ref[frame, :width],
                lambda: packet_ref[frame, (rows - 1) * width : rows * width],
            )
            conv_rows(band, read, wide_ref, write)
            for copy in piece_copies(hidden_ref, frame, outs, members, sem):
                copy.start()
        for frame in range(frames):
            for copy in piece_copies(hidden_ref, frame, outs, members, sem):
                copy.wait()

    @pl.when(here < members)
    def _():
        hidden_ref[...] = jnp.zeros_like(hidden_ref)
        for frame in range(frames):
            for copy in piece_copies(hidden_ref, frame, outs, members, sem):
                copy.start()
        for frame in range(frames):
            for copy in piece_copies(hidden_ref, frame, outs, members, sem):
                copy.wait()


def guest_call(video, packet, weight, gain, shift, count, members, sizes):
    frames, band, width, ch = video.shape
    piece = (frames, band * width // members, ch)
    shapes = [piece, piece] + [(2, frames, size, ch) for size in sizes]
    return pl.pallas_call(
        functools.partial(guest_kernel, count, members),
        in_specs=[vspec()] * 5,
        out_specs=[hspec()] * len(shapes),
        out_shape=[pltpu.HBM(shape, BF16) for shape in shapes],
        scratch_shapes=[
            VMEM(video.shape, BF16),
            VMEM((4 * ch, 6 * ch), BF16),
            pltpu.SemaphoreType.DMA((2 + 2 * len(sizes), frames)),
        ],
        compiler_params=params(24),
        cost_estimate=LONG,
        name="guest",
    )(video, packet, weight, gain.reshape(1, ch), shift.reshape(1, ch))


def pack_kernel(weight_ref, out_ref):
    ch = weight_ref.shape[-1]
    out_ref[...] = jnp.zeros_like(out_ref)
    for layer in range(3):
        for out in range(2):
            for tap in range(3):
                row = out + 2 - tap
                out_ref[layer, row * ch : (row + 1) * ch, out * ch : (out + 1) * ch] = weight_ref[
                    layer, tap
                ]


def pack_call(weight):
    layers, _, ch, _ = weight.shape
    return pl.pallas_call(
        pack_kernel,
        in_specs=[vspec()],
        out_specs=vspec(),
        out_shape=jax.ShapeDtypeStruct((layers, 4 * ch, 2 * ch), BF16),
        compiler_params=params(8),
        cost_estimate=LONG,
        name="pack",
    )(weight)


def pair(read, write, time, layer, wide_ref):
    ch = wide_ref.shape[2] // 2
    dilation = 2**layer
    frames = [read(time + (a - 2) * dilation) for a in range(4)]
    both = jnp.dot(jnp.concatenate(frames, axis=-1), wide_ref[layer], preferred_element_type=F32)
    write(time, (both[:, :ch] + frames[2].astype(F32)).astype(BF16))
    write(time + dilation, (both[:, ch:] + frames[3].astype(F32)).astype(BF16))


def ahead_kernel(members, *refs):
    pieces, (wide_ref, out_ref, u0_ref) = refs[:members], refs[members:]
    step = pieces[0].shape[0]
    me = lax.axis_index("tm") % members
    for k in range(members):
        u0_ref[pl.ds((me ^ k) * step, step)] = pieces[k][...]

    def write1(t, value):
        out_ref[t - 2] = value

    for time in range(2, SPAN, 2):
        pair(lambda t: u0_ref[t], write1, time, 0, wide_ref)


def ahead_call(own, wide, cost):
    members = len(own)
    _, size, ch = own[0].shape
    return pl.pallas_call(
        functools.partial(ahead_kernel, members),
        in_specs=[vspec()] * (members + 1),
        out_specs=vspec(),
        out_shape=jax.ShapeDtypeStruct((SPAN - 2, size, ch), BF16),
        scratch_shapes=[VMEM((SPAN, size, ch), BF16)],
        compiler_params=params(16),
        cost_estimate=cost,
        name="ahead",
    )(*own, wide)


def early_kernel(members, plan, first, *refs):
    arrays, (ahead_ref, wide_ref, out_ref, u0_ref, u1_ref) = refs[: len(plan)], refs[len(plan) :]
    size = out_ref.shape[1]
    lead = SPAN - 2
    me = lax.axis_index("tm") % members
    for ref, (kind, k, source, target, rows) in zip(arrays, plan):
        value = ref.at[0] if len(ref.shape) == 4 else ref
        step = value.shape[0]
        here, there = slice(target, target + rows), slice(source, source + rows)
        if kind == "own":

            @pl.when(me == k)
            def _():
                u0_ref[lead : lead + step, here] = value[:, there]

        elif kind == "middle":
            u0_ref[2:4, here] = value[:, there]
        else:

            @pl.when((me ^ k) % 2 == 0)
            def _():
                u0_ref[pl.ds(2 * (me ^ k), step), here] = value[:, there]

    def write1(t, value):
        u1_ref[t + 4] = value

    def read1(t):
        return u1_ref[t + 4] if t < 2 else ahead_ref[t - 2, first : first + size]

    def write2(t, value):
        out_ref[t] = value

    for time in range(-4, 2, 2):
        pair(lambda t: u0_ref[t + lead], write1, time, 0, wide_ref)
    for time in range(0, SPAN, 4):
        for odd in range(2):
            pair(read1, write2, time + odd, 1, wide_ref)


def early_call(sources, aheads, wide, members, first, size):
    plan, arrays = [], []
    start, ahead = first, aheads[0]
    for block in aheads[1:]:
        if start >= ahead.shape[1]:
            start, ahead = start - ahead.shape[1], block
    for kind, k, blocks in sources:
        at = 0
        for block in blocks:
            rows = block.shape[-2]
            low, high = max(first, at), min(first + size, at + rows)
            if low < high:
                plan.append((kind, k, low - at, low - first, high - low))
                arrays.append(block)
            at += rows
    ch = wide.shape[-1] // 2
    return pl.pallas_call(
        functools.partial(early_kernel, members, plan, start),
        in_specs=[vspec()] * (len(arrays) + 2),
        out_specs=vspec(),
        out_shape=jax.ShapeDtypeStruct((SPAN, size, ch), BF16),
        scratch_shapes=[VMEM((SPAN, size, ch), BF16), VMEM((6, size, ch), BF16)],
        compiler_params=params(16),
        cost_estimate=COST,
        name="early",
    )(*arrays, ahead, wide)


def late_kernel(members, own_ref, halo_ref, wide_ref, *refs):
    outs, u3_ref = refs[:-1], refs[-1]
    step = outs[0].shape[0]
    me = lax.axis_index("tm") % members

    def write3(t, value):
        u3_ref[t] = value

    for time in range(4):
        pair(
            lambda t: own_ref[t] if t >= 0 else halo_ref[t + SPAN], write3, time, 2, wide_ref
        )
    for k in range(members):
        outs[k][...] = u3_ref[pl.ds((me ^ k) * step, step)]


def late_call(own, halo, wide, members):
    frames, size, ch = own.shape
    return pl.pallas_call(
        functools.partial(late_kernel, members),
        in_specs=[vspec()] * 3,
        out_specs=[vspec()] * members,
        out_shape=[jax.ShapeDtypeStruct((frames // members, size, ch), BF16)] * members,
        scratch_shapes=[VMEM(own.shape, BF16)],
        compiler_params=params(12),
        cost_estimate=COST,
        name="late",
    )(own, halo, wide)


def place_kernel(members, offsets, *refs):
    count = members * len(offsets)
    pieces, (out_ref, sem) = refs[:count], refs[-2:]
    me = lax.axis_index("tm") % members
    copies = []
    for i, offset in enumerate(offsets):
        for k in range(members):
            n = i * members + k
            rows = pl.ds(offset, pieces[n].shape[1])
            copies.append(
                pltpu.make_async_copy(pieces[n], out_ref.at[:, me ^ k, rows], sem.at[n])
            )
    for copy in copies:
        copy.start()
    for copy in copies:
        copy.wait()


def place_call(chunks, offsets, quarter, before=None):
    members = len(chunks[0])
    frames, _, ch = chunks[0][0].shape
    pieces = sum(chunks, [])
    shape = jax.ShapeDtypeStruct((frames, members, quarter, ch), BF16)
    return pl.pallas_call(
        functools.partial(place_kernel, members, offsets),
        in_specs=[vspec()] * len(pieces) + [hspec()] * (before is not None),
        out_specs=hspec(),
        out_shape=pltpu.HBM(shape.shape, BF16),
        input_output_aliases={} if before is None else {len(pieces): 0},
        scratch_shapes=[pltpu.SemaphoreType.DMA((len(pieces),))],
        compiler_params=params(8),
        cost_estimate=COST,
        name="place",
    )(*pieces, *([] if before is None else [hbm(before)]))


def halo_rows(video):
    size, row = lax.axis_size("rows"), lax.axis_index("rows")
    band = video.shape[1]
    if size == 2:
        mine = lax.dynamic_slice_in_dim(video, jnp.where(row == 0, band - 1, 0), 1, axis=1)[:, 0]
        other = lax.ppermute(mine, "rows", [(0, 1), (1, 0)])
        return other, other
    up = [(i, i + 1) for i in range(size - 1)]
    down = [(j, i) for i, j in up]
    return lax.ppermute(video[:, -1], "rows", up), lax.ppermute(video[:, 0], "rows", down)


def other_sums(sums):
    if lax.axis_size("rows") == 2:
        return lax.ppermute(sums, "rows", [(0, 1), (1, 0)])
    return lax.psum(sums, "rows") - sums


def after(value, *others):
    return lax.optimization_barrier((value, *others))[0]


def body(video, spatial_weight, norm_gain, norm_shift, temporal_weight):
    frames, band, width, ch = video.shape
    total = lax.axis_size("tm")
    me = lax.axis_index("tm") % (SPAN // frames)
    rows = lax.axis_size("rows")
    members = SPAN // frames
    swaps = [[(i, i ^ k) for i in range(total)] for k in range(members)]
    onward = [(i, i + members) for i in range(total - members)]
    guest_pairs = [(i, i + members - 1) for i in range(1, total - members, 2)]
    guest_swaps = [[(i, i ^ k) for i in range(0, total, 2)] for k in range(members)]

    guest_video = lax.ppermute(video, "tm", guest_pairs)
    above, below = halo_rows(video)
    conv, sums = conv_call(video, spatial_weight)
    conv, sums = edge_call(conv, above, below, spatial_weight, sums)
    count = band * rows * width * (ch // GROUPS)
    quarter = band * width // members
    own_sizes, guest_sizes, out_sizes = [
        [quarter * part // 60 for part in parts] for parts in (OWN_PARTS, GUEST_PARTS, OUT_PARTS)
    ]
    halo_list = [above] if above is below else [above, below]
    packet, *pieces = norm_call(
        conv, sums, other_sums(sums), halo_list, norm_gain, norm_shift, count, members, own_sizes
    )

    def swap(four, waits=None):
        got = [four[0]]
        for k in range(1, members):
            value = four[k] if waits is None else after(four[k], waits[k])
            got.append(lax.ppermute(value, "tm", swaps[k]))
        return got

    guest_packet = lax.ppermute(packet, "tm", guest_pairs)
    keep, mate, *aways = guest_call(
        guest_video, guest_packet, spatial_weight, norm_gain, norm_shift, count, members, guest_sizes
    )
    wide = pack_call(after(temporal_weight, keep))
    sources = [(kind, k, []) for kind in ("own", "guest") for k in range(members)]
    sources.append(("middle", 0, []))

    def add(start, arrays):
        for (_, _, blocks), array in zip(sources[start:], arrays):
            blocks.append(array)

    aheads, passed, results = [], [], []

    def block(i, gate):
        four = pieces[i * members : (i + 1) * members]
        own = swap(four, [gate] * members if i else None)
        crossed = lax.ppermute(after(aways[i], own[2]) if i else aways[i], "tm", guest_swaps[2])
        four = own if i else after(own, wide)
        middle = functools.reduce(
            lambda acc, k: jnp.where(me == (2 ^ k), four[k], acc), range(1, members), four[0]
        )
        add(0, own)
        add(2 * members, [lax.ppermute(middle, "tm", onward)])
        if i == 0:
            add(members, [keep, lax.ppermute(after(mate, wide), "tm", guest_swaps[1])])
        waits = [middle] if i else [middle, crossed]
        aheads.append(ahead_call(own, after(wide, *waits), COST if i else LONG))
        forward = crossed[1] if i else after(crossed[1], aheads[0])
        add(members + 2, [crossed, lax.ppermute(forward, "tm", guest_swaps[1])])

    block(0, None)
    first = 0
    for i, size in enumerate(out_sizes):
        u2 = early_call(sources, aheads, wide, members, first, size)
        if i == 0:
            block(1, aheads[0])
        if i > 1:
            u2 = after(u2, passed[0] if i == 2 else late[0])
        passed.append(lax.ppermute(u2, "tm", onward))
        following = late_call(u2, passed[-1], wide, members)
        results.append(swap(following, results[-1] if results else None))
        late = following if i < 2 else late
        first += size
    offsets = [sum(out_sizes[:i]) for i in range(len(out_sizes))]
    out = place_call(results[:2], offsets[:2], quarter)
    out = place_call(results[2:], offsets[2:], quarter, out)
    return out.reshape(frames, band, width, ch)


def solution(mesh):
    return jax.shard_map(
        body,
        mesh=mesh,
        in_specs=(P("tm", "rows", None, None), P(), P(), P(), P()),
        out_specs=P("tm", "rows", None, None),
        check_vma=False,
    )
```

```python
import functools

import jax
import jax.numpy as jnp
from jax import lax
from jax.experimental import pallas as pl
from jax.experimental.pallas import tpu as pltpu
from jax.sharding import PartitionSpec as P

GROUPS = 32
SPAN = 8
OWN_PARTS = (42, 18)
GUEST_PARTS = (42, 18)
OUT_PARTS = (32, 10, 10, 8)
VMEM = pltpu.VMEM
ANY = pl.ANY
F32 = jnp.float32
BF16 = jnp.bfloat16


def vspec():
    return pl.BlockSpec(memory_space=VMEM)


def params(mib):
    return pltpu.CompilerParams(vmem_limit_bytes=mib << 20)


COST = pl.CostEstimate(flops=0, bytes_accessed=0, transcendentals=0)
LONG = pl.CostEstimate(flops=20_000_000_000, bytes_accessed=0, transcendentals=0)


def hspec():
    return pl.BlockSpec(memory_space=ANY)


def hbm(value):
    return pltpu.with_memory_space_constraint(value, pltpu.HBM)


def shifted_sum(taps):
    width, ch = taps.shape[0], taps.shape[1] // 3
    column = lax.broadcasted_iota(jnp.int32, (width, ch), 0)
    left = jnp.where(column == 0, 0.0, pltpu.roll(taps[:, :ch], 1, 0))
    right = jnp.where(column == width - 1, 0.0, pltpu.roll(taps[:, 2 * ch :], width - 1, 0))
    return left + taps[:, ch : 2 * ch] + right


def fold(value):
    return jnp.sum(value.reshape(value.shape[0] // 8, 8, value.shape[1]), axis=0)


def widen(weight_ref, wide_ref):
    ch = weight_ref.shape[-1]
    wide_ref[...] = jnp.zeros_like(wide_ref)
    for out in range(2):
        for col in range(3):
            for row in range(3):
                wide_ref[
                    (out + row) * ch : (out + row + 1) * ch,
                    (out * 3 + col) * ch : (out * 3 + col + 1) * ch,
                ] = weight_ref[row, col]


def conv_rows(band, read, wide_ref, write):
    ch = wide_ref.shape[0] // 4
    for first in range(0, band, 2):
        lhs = jnp.concatenate([read(r) for r in range(first - 1, first + 3)], axis=-1)
        wide = jnp.dot(lhs, wide_ref[...], preferred_element_type=F32)
        for out in range(2):
            write(first + out, shifted_sum(wide[:, out * 3 * ch : (out + 1) * 3 * ch]))


def padded_read(band, row_of, above, below):
    row, rows = lax.axis_index("rows"), lax.axis_size("rows")

    def read(r):
        if r < 0:
            return jnp.where(row > 0, above(), jnp.zeros_like(above()))
        if r == band:
            return jnp.where(row < rows - 1, below(), jnp.zeros_like(below()))
        return row_of(r)

    return read


def conv_kernel(band, video_ref, weight_ref, out_ref, sums_ref, wide_ref):
    @pl.when(pl.program_id(0) == 0)
    def _():
        widen(weight_ref, wide_ref)

    ch = weight_ref.shape[-1]
    sums = [jnp.zeros((8, ch), F32), jnp.zeros((8, ch), F32)]

    def read(row):
        if 0 <= row < band:
            return video_ref[0, row]
        return jnp.zeros_like(video_ref[0, 0])

    def write(row, value):
        out_ref[0, row] = value
        if 0 < row < band - 1:
            sums[0] = sums[0] + fold(value)
            sums[1] = sums[1] + fold(value * value)

    conv_rows(band, read, wide_ref, write)
    sums_ref[0, 0] = sums[0]
    sums_ref[0, 1] = sums[1]


def frame_spec(*shape):
    return pl.BlockSpec((1,) + shape, lambda f, *_: (f,) + (0,) * len(shape))


def conv_call(video, weight):
    frames, band, width, ch = video.shape
    return pl.pallas_call(
        functools.partial(conv_kernel, band),
        grid=(frames,),
        in_specs=[
            frame_spec(band, width, ch),
            pl.BlockSpec(weight.shape, lambda f: (0, 0, 0, 0)),
        ],
        out_specs=[frame_spec(band, width, ch), frame_spec(2, 8, ch)],
        out_shape=[
            jax.ShapeDtypeStruct(video.shape, F32),
            jax.ShapeDtypeStruct((frames, 2, 8, ch), F32),
        ],
        scratch_shapes=[VMEM((4 * ch, 6 * ch), BF16)],
        compiler_params=params(16),
        cost_estimate=LONG,
        name="conv",
    )(hbm(video), hbm(weight))


def edge_kernel(conv_ref, above_ref, below_ref, weight_ref, sums_ref, out_ref, out_sums_ref):
    frames, band = conv_ref.shape[:2]
    row, rows = lax.axis_index("rows"), lax.axis_size("rows")
    sides = ((0, above_ref, 0, row > 0), (band - 1, below_ref, 2, row < rows - 1))
    for frame in range(frames):
        total, square = sums_ref[frame, 0], sums_ref[frame, 1]
        for place, halo_ref, tap, there in sides:
            halo = jnp.where(there, halo_ref[frame], jnp.zeros_like(halo_ref[frame]))
            taps = jnp.concatenate([weight_ref[tap, col] for col in range(3)], axis=-1)
            wide = jnp.dot(halo, taps, preferred_element_type=F32)
            value = conv_ref[frame, place] + shifted_sum(wide)
            out_ref[frame, place] = value
            total = total + fold(value)
            square = square + fold(value * value)
        out_sums_ref[frame, 0] = total
        out_sums_ref[frame, 1] = square


def edge_call(conv, above, below, weight, sums):
    return pl.pallas_call(
        edge_kernel,
        in_specs=[vspec()] * 5,
        out_specs=[vspec()] * 2,
        out_shape=[
            jax.ShapeDtypeStruct(conv.shape, F32),
            jax.ShapeDtypeStruct(sums.shape, F32),
        ],
        input_output_aliases={0: 0},
        compiler_params=params(12),
        cost_estimate=COST,
        name="edge",
    )(conv, above, below, weight, sums)


def over_groups(value, per_group):
    lane = lax.broadcasted_iota(jnp.int32, value.shape, 1)
    lanes = value.shape[1]
    step = 1
    while step < per_group:
        value = value + pltpu.roll(value, lanes - step, 1)
        step *= 2
    value = jnp.where(lane % per_group == 0, value, 0.0)
    step = 1
    while step < per_group:
        value = value + pltpu.roll(value, step, 1)
        step *= 2
    return value


def norm_of(sums, count, gain_ref, shift_ref):
    ch = gain_ref.shape[-1]
    total = [
        over_groups(jnp.broadcast_to(jnp.sum(x, axis=0, keepdims=True), (8, ch)), ch // GROUPS)
        for x in sums
    ]
    mean = total[0] / count
    var = total[1] / count - mean * mean
    scale = (lax.rsqrt(var + 1e-05) * gain_ref[...])[:1]
    mean = mean[:1]
    shift = shift_ref[...]

    def apply(value):
        v = (value - mean) * scale + shift
        return (0.5 * v * (1.0 + jnp.tanh(0.5 * v))).astype(BF16)

    return apply


def piece_copies(hidden_ref, frame, outs, members, sem):
    frames, band, width, ch = hidden_ref.shape
    flat = hidden_ref.reshape(frames, band * width, ch)
    me = lax.axis_index("tm") % members
    quarter = band * width // members
    copies = []
    for k, blocks in enumerate(outs):
        offset = 0
        for block in blocks:
            rows = pl.ds(pl.multiple_of((me ^ k) * quarter + offset, 16), block.shape[1])
            copies.append(
                pltpu.make_async_copy(
                    flat.at[frame, rows], block.at[frame], sem.at[len(copies), frame]
                )
            )
            offset += block.shape[1]
    return copies


def norm_kernel(count, members, rows, conv_ref, own_ref, other_ref, gain_ref, shift_ref, *refs):
    row_refs, packet_ref, (hidden_ref, sem) = refs[:rows], refs[rows], refs[-2:]
    outs = [refs[rows + 1 + k : -2 : members] for k in range(members)]
    frames, band, width, ch = conv_ref.shape
    for frame in range(frames):
        sums = [own_ref[frame, i] + other_ref[frame, i] for i in range(2)]
        for i, ref in enumerate(row_refs):
            packet_ref[frame, i * width : (i + 1) * width] = ref[frame]
        rest = jnp.concatenate(sums, axis=0)
        for part in range(3):
            at = rows * width + part * 16
            short = rest.astype(BF16)
            rest = rest - short.astype(F32)
            packet_ref[frame, at : at + 16] = short
        apply = norm_of(sums, count, gain_ref, shift_ref)

        @pl.loop(0, band)
        def _(row):
            hidden_ref[frame, row] = apply(conv_ref[frame, row])

        for copy in piece_copies(hidden_ref, frame, outs, members, sem):
            copy.start()
    for frame in range(frames):
        for copy in piece_copies(hidden_ref, frame, outs, members, sem):
            copy.wait()


def norm_call(conv, own, other, halo_rows, gain, shift, count, members, sizes):
    frames, band, width, ch = conv.shape
    rows = len(halo_rows)
    return pl.pallas_call(
        functools.partial(norm_kernel, count, members, rows),
        in_specs=[vspec()] * (5 + rows),
        out_specs=[vspec()] + [hspec()] * (members * len(sizes)),
        out_shape=[jax.ShapeDtypeStruct((frames, rows * width + 48, ch), BF16)]
        + [pltpu.HBM((frames, size, ch), BF16) for size in sizes for _ in range(members)],
        scratch_shapes=[
            VMEM((frames, band, width, ch), BF16),
            pltpu.SemaphoreType.DMA((members * len(sizes), frames)),
        ],
        compiler_params=params(16),
        cost_estimate=COST,
        name="norm",
    )(conv, own, other, gain.reshape(1, ch), shift.reshape(1, ch), *halo_rows)


def guest_kernel(count, members, video_ref, packet_ref, weight_ref, gain_ref, shift_ref, *refs):
    keep_ref, mate_ref, *away_refs = refs[:-3]
    hidden_ref, wide_ref, sem = refs[-3:]
    outs = [[keep_ref], [mate_ref]] + [[ref.at[k] for ref in away_refs] for k in range(2)]
    frames, band, width, ch = video_ref.shape
    rows = (packet_ref.shape[1] - 48) // width
    here = lax.axis_index("tm")

    @pl.when(jnp.logical_and(here >= members, here % 2 == 0))
    def _():
        widen(weight_ref, wide_ref)
        for frame in range(frames):
            parts = packet_ref[frame, rows * width :].astype(F32)
            both = parts[:16] + parts[16:32] + parts[32:]
            sums = [both[:8], both[8:]]
            apply = norm_of(sums, count, gain_ref, shift_ref)

            def write(row, value):
                hidden_ref[frame, row] = apply(value)

            read = padded_read(
                band,
                lambda r: video_ref[frame, r],
                lambda: packet_ref[frame, :width],
                lambda: packet_ref[frame, (rows - 1) * width : rows * width],
            )
            conv_rows(band, read, wide_ref, write)
            for copy in piece_copies(hidden_ref, frame, outs, members, sem):
                copy.start()
        for frame in range(frames):
            for copy in piece_copies(hidden_ref, frame, outs, members, sem):
                copy.wait()

    @pl.when(here < members)
    def _():
        hidden_ref[...] = jnp.zeros_like(hidden_ref)
        for frame in range(frames):
            for copy in piece_copies(hidden_ref, frame, outs, members, sem):
                copy.start()
        for frame in range(frames):
            for copy in piece_copies(hidden_ref, frame, outs, members, sem):
                copy.wait()


def guest_call(video, packet, weight, gain, shift, count, members, sizes):
    frames, band, width, ch = video.shape
    piece = (frames, band * width // members, ch)
    shapes = [piece, piece] + [(2, frames, size, ch) for size in sizes]
    return pl.pallas_call(
        functools.partial(guest_kernel, count, members),
        in_specs=[vspec()] * 5,
        out_specs=[hspec()] * len(shapes),
        out_shape=[pltpu.HBM(shape, BF16) for shape in shapes],
        scratch_shapes=[
            VMEM(video.shape, BF16),
            VMEM((4 * ch, 6 * ch), BF16),
            pltpu.SemaphoreType.DMA((2 + 2 * len(sizes), frames)),
        ],
        compiler_params=params(24),
        cost_estimate=LONG,
        name="guest",
    )(video, packet, weight, gain.reshape(1, ch), shift.reshape(1, ch))


def pack_kernel(weight_ref, out_ref):
    ch = weight_ref.shape[-1]
    out_ref[...] = jnp.zeros_like(out_ref)
    for layer in range(3):
        for out in range(2):
            for tap in range(3):
                row = out + 2 - tap
                out_ref[layer, row * ch : (row + 1) * ch, out * ch : (out + 1) * ch] = weight_ref[
                    layer, tap
                ]


def pack_call(weight):
    layers, _, ch, _ = weight.shape
    return pl.pallas_call(
        pack_kernel,
        in_specs=[vspec()],
        out_specs=vspec(),
        out_shape=jax.ShapeDtypeStruct((layers, 4 * ch, 2 * ch), BF16),
        compiler_params=params(8),
        cost_estimate=LONG,
        name="pack",
    )(weight)


def pair(read, write, time, layer, wide_ref):
    ch = wide_ref.shape[2] // 2
    dilation = 2**layer
    frames = [read(time + (a - 2) * dilation) for a in range(4)]
    both = jnp.dot(jnp.concatenate(frames, axis=-1), wide_ref[layer], preferred_element_type=F32)
    write(time, (both[:, :ch] + frames[2].astype(F32)).astype(BF16))
    write(time + dilation, (both[:, ch:] + frames[3].astype(F32)).astype(BF16))


def ahead_kernel(members, *refs):
    pieces, (wide_ref, out_ref, u0_ref) = refs[:members], refs[members:]
    step = pieces[0].shape[0]
    me = lax.axis_index("tm") % members
    for k in range(members):
        u0_ref[pl.ds((me ^ k) * step, step)] = pieces[k][...]

    def write1(t, value):
        out_ref[t - 2] = value

    for time in range(2, SPAN, 2):
        pair(lambda t: u0_ref[t], write1, time, 0, wide_ref)


def ahead_call(own, wide, cost):
    members = len(own)
    _, size, ch = own[0].shape
    return pl.pallas_call(
        functools.partial(ahead_kernel, members),
        in_specs=[vspec()] * (members + 1),
        out_specs=vspec(),
        out_shape=jax.ShapeDtypeStruct((SPAN - 2, size, ch), BF16),
        scratch_shapes=[VMEM((SPAN, size, ch), BF16)],
        compiler_params=params(16),
        cost_estimate=cost,
        name="ahead",
    )(*own, wide)


def early_kernel(members, plan, first, *refs):
    arrays, (ahead_ref, wide_ref, out_ref, u0_ref, u1_ref) = refs[: len(plan)], refs[len(plan) :]
    size = out_ref.shape[1]
    lead = SPAN - 2
    me = lax.axis_index("tm") % members
    for ref, (kind, k, source, target, rows) in zip(arrays, plan):
        value = ref.at[0] if len(ref.shape) == 4 else ref
        step = value.shape[0]
        here, there = slice(target, target + rows), slice(source, source + rows)
        if kind == "own":

            @pl.when(me == k)
            def _():
                u0_ref[lead : lead + step, here] = value[:, there]

        elif kind == "middle":
            u0_ref[2:4, here] = value[:, there]
        else:

            @pl.when((me ^ k) % 2 == 0)
            def _():
                u0_ref[pl.ds(2 * (me ^ k), step), here] = value[:, there]

    def write1(t, value):
        u1_ref[t + 4] = value

    def read1(t):
        return u1_ref[t + 4] if t < 2 else ahead_ref[t - 2, first : first + size]

    def write2(t, value):
        out_ref[t] = value

    for time in range(-4, 2, 2):
        pair(lambda t: u0_ref[t + lead], write1, time, 0, wide_ref)
    for time in range(0, SPAN, 4):
        for odd in range(2):
            pair(read1, write2, time + odd, 1, wide_ref)


def early_call(sources, aheads, wide, members, first, size):
    plan, arrays = [], []
    start, ahead = first, aheads[0]
    for block in aheads[1:]:
        if start >= ahead.shape[1]:
            start, ahead = start - ahead.shape[1], block
    for kind, k, blocks in sources:
        at = 0
        for block in blocks:
            rows = block.shape[-2]
            low, high = max(first, at), min(first + size, at + rows)
            if low < high:
                plan.append((kind, k, low - at, low - first, high - low))
                arrays.append(block)
            at += rows
    ch = wide.shape[-1] // 2
    return pl.pallas_call(
        functools.partial(early_kernel, members, plan, start),
        in_specs=[vspec()] * (len(arrays) + 2),
        out_specs=vspec(),
        out_shape=jax.ShapeDtypeStruct((SPAN, size, ch), BF16),
        scratch_shapes=[VMEM((SPAN, size, ch), BF16), VMEM((6, size, ch), BF16)],
        compiler_params=params(16),
        cost_estimate=COST,
        name="early",
    )(*arrays, ahead, wide)


def late_kernel(members, own_ref, halo_ref, wide_ref, *refs):
    outs, u3_ref = refs[:-1], refs[-1]
    step = outs[0].shape[0]
    me = lax.axis_index("tm") % members

    def write3(t, value):
        u3_ref[t] = value

    for time in range(4):
        pair(
            lambda t: own_ref[t] if t >= 0 else halo_ref[t + SPAN], write3, time, 2, wide_ref
        )
    for k in range(members):
        outs[k][...] = u3_ref[pl.ds((me ^ k) * step, step)]


def late_call(own, halo, wide, members):
    frames, size, ch = own.shape
    return pl.pallas_call(
        functools.partial(late_kernel, members),
        in_specs=[vspec()] * 3,
        out_specs=[vspec()] * members,
        out_shape=[jax.ShapeDtypeStruct((frames // members, size, ch), BF16)] * members,
        scratch_shapes=[VMEM(own.shape, BF16)],
        compiler_params=params(12),
        cost_estimate=COST,
        name="late",
    )(own, halo, wide)


def place_kernel(members, offsets, *refs):
    count = members * len(offsets)
    pieces, (out_ref, sem) = refs[:count], refs[-2:]
    me = lax.axis_index("tm") % members
    copies = []
    for i, offset in enumerate(offsets):
        for k in range(members):
            n = i * members + k
            rows = pl.ds(offset, pieces[n].shape[1])
            copies.append(
                pltpu.make_async_copy(pieces[n], out_ref.at[:, me ^ k, rows], sem.at[n])
            )
    for copy in copies:
        copy.start()
    for copy in copies:
        copy.wait()


def place_call(chunks, offsets, quarter, before=None):
    members = len(chunks[0])
    frames, _, ch = chunks[0][0].shape
    pieces = sum(chunks, [])
    shape = jax.ShapeDtypeStruct((frames, members, quarter, ch), BF16)
    return pl.pallas_call(
        functools.partial(place_kernel, members, offsets),
        in_specs=[vspec()] * len(pieces) + [hspec()] * (before is not None),
        out_specs=hspec(),
        out_shape=pltpu.HBM(shape.shape, BF16),
        input_output_aliases={} if before is None else {len(pieces): 0},
        scratch_shapes=[pltpu.SemaphoreType.DMA((len(pieces),))],
        compiler_params=params(8),
        cost_estimate=COST,
        name="place",
    )(*pieces, *([] if before is None else [hbm(before)]))


def halo_rows(video):
    size, row = lax.axis_size("rows"), lax.axis_index("rows")
    band = video.shape[1]
    if size == 2:
        mine = lax.dynamic_slice_in_dim(video, jnp.where(row == 0, band - 1, 0), 1, axis=1)[:, 0]
        other = lax.ppermute(mine, "rows", [(0, 1), (1, 0)])
        return other, other
    up = [(i, i + 1) for i in range(size - 1)]
    down = [(j, i) for i, j in up]
    return lax.ppermute(video[:, -1], "rows", up), lax.ppermute(video[:, 0], "rows", down)


def other_sums(sums):
    if lax.axis_size("rows") == 2:
        return lax.ppermute(sums, "rows", [(0, 1), (1, 0)])
    return lax.psum(sums, "rows") - sums


def after(value, *others):
    return lax.optimization_barrier((value, *others))[0]


def body(video, spatial_weight, norm_gain, norm_shift, temporal_weight):
    frames, band, width, ch = video.shape
    total = lax.axis_size("tm")
    me = lax.axis_index("tm") % (SPAN // frames)
    rows = lax.axis_size("rows")
    members = SPAN // frames
    swaps = [[(i, i ^ k) for i in range(total)] for k in range(members)]
    onward = [(i, i + members) for i in range(total - members)]
    guest_pairs = [(i, i + members - 1) for i in range(1, total - members, 2)]
    guest_swaps = [[(i, i ^ k) for i in range(0, total, 2)] for k in range(members)]

    guest_video = lax.ppermute(video, "tm", guest_pairs)
    above, below = halo_rows(video)
    conv, sums = conv_call(video, spatial_weight)
    conv, sums = edge_call(conv, above, below, spatial_weight, sums)
    count = band * rows * width * (ch // GROUPS)
    quarter = band * width // members
    own_sizes, guest_sizes, out_sizes = [
        [quarter * part // 60 for part in parts] for parts in (OWN_PARTS, GUEST_PARTS, OUT_PARTS)
    ]
    halo_list = [above] if above is below else [above, below]
    packet, *pieces = norm_call(
        conv, sums, other_sums(sums), halo_list, norm_gain, norm_shift, count, members, own_sizes
    )

    def swap(four, waits=None):
        got = [four[0]]
        for k in range(1, members):
            value = four[k] if waits is None else after(four[k], waits[k])
            got.append(lax.ppermute(value, "tm", swaps[k]))
        return got

    guest_packet = lax.ppermute(packet, "tm", guest_pairs)
    keep, mate, *aways = guest_call(
        guest_video, guest_packet, spatial_weight, norm_gain, norm_shift, count, members, guest_sizes
    )
    wide = pack_call(after(temporal_weight, keep))
    sources = [(kind, k, []) for kind in ("own", "guest") for k in range(members)]
    sources.append(("middle", 0, []))

    def add(start, arrays):
        for (_, _, blocks), array in zip(sources[start:], arrays):
            blocks.append(array)

    aheads, passed, results = [], [], []

    def block(i, gate):
        four = pieces[i * members : (i + 1) * members]
        own = swap(four, [gate] * members if i else None)
        crossed = lax.ppermute(after(aways[i], own[2]) if i else aways[i], "tm", guest_swaps[2])
        four = own if i else after(own, wide)
        middle = functools.reduce(
            lambda acc, k: jnp.where(me == (2 ^ k), four[k], acc), range(1, members), four[0]
        )
        add(0, own)
        add(2 * members, [lax.ppermute(middle, "tm", onward)])
        if i == 0:
            add(members, [keep, lax.ppermute(after(mate, wide), "tm", guest_swaps[1])])
        waits = [middle] if i else [middle, crossed]
        aheads.append(ahead_call(own, after(wide, *waits), COST if i else LONG))
        forward = crossed[1] if i else after(crossed[1], aheads[0])
        add(members + 2, [crossed, lax.ppermute(forward, "tm", guest_swaps[1])])

    block(0, None)
    first = 0
    for i, size in enumerate(out_sizes):
        u2 = early_call(sources, aheads, wide, members, first, size)
        if i == 0:
            block(1, aheads[0])
        if i > 1:
            u2 = after(u2, passed[0] if i == 2 else late[0])
        passed.append(lax.ppermute(u2, "tm", onward))
        following = late_call(u2, passed[-1], wide, members)
        results.append(swap(following, results[-1] if results else None))
        late = following if i < 2 else late
        first += size
    offsets = [sum(out_sizes[:i]) for i in range(len(out_sizes))]
    out = place_call(results[:2], offsets[:2], quarter)
    out = place_call(results[2:], offsets[2:], quarter, out)
    return out.reshape(frames, band, width, ch)


def solution(mesh):
    return jax.shard_map(
        body,
        mesh=mesh,
        in_specs=(P("tm", "rows", None, None), P(), P(), P(), P()),
        out_specs=P("tm", "rows", None, None),
        check_vma=False,
    )
```

```python
import functools

import jax
import jax.numpy as jnp
from jax import lax
from jax.experimental import pallas as pl
from jax.experimental.pallas import tpu as pltpu
from jax.sharding import PartitionSpec as P

GROUPS = 32
SPAN = 8
OWN_PARTS = (42, 18)
GUEST_PARTS = (42, 18)
OUT_PARTS = (32, 10, 10, 8)
VMEM = pltpu.VMEM
ANY = pl.ANY
F32 = jnp.float32
BF16 = jnp.bfloat16


def vspec():
    return pl.BlockSpec(memory_space=VMEM)


def params(mib):
    return pltpu.CompilerParams(vmem_limit_bytes=mib << 20)


COST = pl.CostEstimate(flops=0, bytes_accessed=0, transcendentals=0)
LONG = pl.CostEstimate(flops=20_000_000_000, bytes_accessed=0, transcendentals=0)


def hspec():
    return pl.BlockSpec(memory_space=ANY)


def hbm(value):
    return pltpu.with_memory_space_constraint(value, pltpu.HBM)


def shifted_sum(taps):
    width, ch = taps.shape[0], taps.shape[1] // 3
    column = lax.broadcasted_iota(jnp.int32, (width, ch), 0)
    left = jnp.where(column == 0, 0.0, pltpu.roll(taps[:, :ch], 1, 0))
    right = jnp.where(column == width - 1, 0.0, pltpu.roll(taps[:, 2 * ch :], width - 1, 0))
    return left + taps[:, ch : 2 * ch] + right


def fold(value):
    return jnp.sum(value.reshape(value.shape[0] // 8, 8, value.shape[1]), axis=0)


def widen(weight_ref, wide_ref):
    ch = weight_ref.shape[-1]
    wide_ref[...] = jnp.zeros_like(wide_ref)
    for out in range(2):
        for col in range(3):
            for row in range(3):
                wide_ref[
                    (out + row) * ch : (out + row + 1) * ch,
                    (out * 3 + col) * ch : (out * 3 + col + 1) * ch,
                ] = weight_ref[row, col]


def conv_rows(band, read, wide_ref, write):
    ch = wide_ref.shape[0] // 4
    for first in range(0, band, 2):
        lhs = jnp.concatenate([read(r) for r in range(first - 1, first + 3)], axis=-1)
        wide = jnp.dot(lhs, wide_ref[...], preferred_element_type=F32)
        for out in range(2):
            write(first + out, shifted_sum(wide[:, out * 3 * ch : (out + 1) * 3 * ch]))


def padded_read(band, row_of, above, below):
    row, rows = lax.axis_index("rows"), lax.axis_size("rows")

    def read(r):
        if r < 0:
            return jnp.where(row > 0, above(), jnp.zeros_like(above()))
        if r == band:
            return jnp.where(row < rows - 1, below(), jnp.zeros_like(below()))
        return row_of(r)

    return read


def conv_kernel(band, video_ref, weight_ref, out_ref, sums_ref, wide_ref):
    @pl.when(pl.program_id(0) == 0)
    def _():
        widen(weight_ref, wide_ref)

    ch = weight_ref.shape[-1]
    sums = [jnp.zeros((8, ch), F32), jnp.zeros((8, ch), F32)]

    def read(row):
        if 0 <= row < band:
            return video_ref[0, row]
        return jnp.zeros_like(video_ref[0, 0])

    def write(row, value):
        out_ref[0, row] = value
        if 0 < row < band - 1:
            sums[0] = sums[0] + fold(value)
            sums[1] = sums[1] + fold(value * value)

    conv_rows(band, read, wide_ref, write)
    sums_ref[0, 0] = sums[0]
    sums_ref[0, 1] = sums[1]


def frame_spec(*shape):
    return pl.BlockSpec((1,) + shape, lambda f, *_: (f,) + (0,) * len(shape))


def conv_call(video, weight):
    frames, band, width, ch = video.shape
    return pl.pallas_call(
        functools.partial(conv_kernel, band),
        grid=(frames,),
        in_specs=[
            frame_spec(band, width, ch),
            pl.BlockSpec(weight.shape, lambda f: (0, 0, 0, 0)),
        ],
        out_specs=[frame_spec(band, width, ch), frame_spec(2, 8, ch)],
        out_shape=[
            jax.ShapeDtypeStruct(video.shape, F32),
            jax.ShapeDtypeStruct((frames, 2, 8, ch), F32),
        ],
        scratch_shapes=[VMEM((4 * ch, 6 * ch), BF16)],
        compiler_params=params(16),
        cost_estimate=LONG,
        name="conv",
    )(hbm(video), hbm(weight))


def edge_kernel(conv_ref, above_ref, below_ref, weight_ref, sums_ref, out_ref, out_sums_ref):
    frames, band = conv_ref.shape[:2]
    row, rows = lax.axis_index("rows"), lax.axis_size("rows")
    sides = ((0, above_ref, 0, row > 0), (band - 1, below_ref, 2, row < rows - 1))
    for frame in range(frames):
        total, square = sums_ref[frame, 0], sums_ref[frame, 1]
        for place, halo_ref, tap, there in sides:
            halo = jnp.where(there, halo_ref[frame], jnp.zeros_like(halo_ref[frame]))
            taps = jnp.concatenate([weight_ref[tap, col] for col in range(3)], axis=-1)
            wide = jnp.dot(halo, taps, preferred_element_type=F32)
            value = conv_ref[frame, place] + shifted_sum(wide)
            out_ref[frame, place] = value
            total = total + fold(value)
            square = square + fold(value * value)
        out_sums_ref[frame, 0] = total
        out_sums_ref[frame, 1] = square


def edge_call(conv, above, below, weight, sums):
    return pl.pallas_call(
        edge_kernel,
        in_specs=[vspec()] * 5,
        out_specs=[vspec()] * 2,
        out_shape=[
            jax.ShapeDtypeStruct(conv.shape, F32),
            jax.ShapeDtypeStruct(sums.shape, F32),
        ],
        input_output_aliases={0: 0},
        compiler_params=params(12),
        cost_estimate=COST,
        name="edge",
    )(conv, above, below, weight, sums)


def over_groups(value, per_group):
    lane = lax.broadcasted_iota(jnp.int32, value.shape, 1)
    lanes = value.shape[1]
    step = 1
    while step < per_group:
        value = value + pltpu.roll(value, lanes - step, 1)
        step *= 2
    value = jnp.where(lane % per_group == 0, value, 0.0)
    step = 1
    while step < per_group:
        value = value + pltpu.roll(value, step, 1)
        step *= 2
    return value


def norm_of(sums, count, gain_ref, shift_ref):
    ch = gain_ref.shape[-1]
    total = [
        over_groups(jnp.broadcast_to(jnp.sum(x, axis=0, keepdims=True), (8, ch)), ch // GROUPS)
        for x in sums
    ]
    mean = total[0] / count
    var = total[1] / count - mean * mean
    scale = (lax.rsqrt(var + 1e-05) * gain_ref[...])[:1]
    mean = mean[:1]
    shift = shift_ref[...]

    def apply(value):
        v = (value - mean) * scale + shift
        return (0.5 * v * (1.0 + jnp.tanh(0.5 * v))).astype(BF16)

    return apply


def piece_copies(hidden_ref, frame, outs, members, sem):
    frames, band, width, ch = hidden_ref.shape
    flat = hidden_ref.reshape(frames, band * width, ch)
    me = lax.axis_index("tm") % members
    quarter = band * width // members
    copies = []
    for k, blocks in enumerate(outs):
        offset = 0
        for block in blocks:
            rows = pl.ds(pl.multiple_of((me ^ k) * quarter + offset, 16), block.shape[1])
            copies.append(
                pltpu.make_async_copy(
                    flat.at[frame, rows], block.at[frame], sem.at[len(copies), frame]
                )
            )
            offset += block.shape[1]
    return copies


def norm_kernel(count, members, rows, conv_ref, own_ref, other_ref, gain_ref, shift_ref, *refs):
    row_refs, packet_ref, (hidden_ref, sem) = refs[:rows], refs[rows], refs[-2:]
    outs = [refs[rows + 1 + k : -2 : members] for k in range(members)]
    frames, band, width, ch = conv_ref.shape
    for frame in range(frames):
        sums = [own_ref[frame, i] + other_ref[frame, i] for i in range(2)]
        for i, ref in enumerate(row_refs):
            packet_ref[frame, i * width : (i + 1) * width] = ref[frame]
        rest = jnp.concatenate(sums, axis=0)
        for part in range(3):
            at = rows * width + part * 16
            short = rest.astype(BF16)
            rest = rest - short.astype(F32)
            packet_ref[frame, at : at + 16] = short
        apply = norm_of(sums, count, gain_ref, shift_ref)

        @pl.loop(0, band)
        def _(row):
            hidden_ref[frame, row] = apply(conv_ref[frame, row])

        for copy in piece_copies(hidden_ref, frame, outs, members, sem):
            copy.start()
    for frame in range(frames):
        for copy in piece_copies(hidden_ref, frame, outs, members, sem):
            copy.wait()


def norm_call(conv, own, other, halo_rows, gain, shift, count, members, sizes):
    frames, band, width, ch = conv.shape
    rows = len(halo_rows)
    return pl.pallas_call(
        functools.partial(norm_kernel, count, members, rows),
        in_specs=[vspec()] * (5 + rows),
        out_specs=[vspec()] + [hspec()] * (members * len(sizes)),
        out_shape=[jax.ShapeDtypeStruct((frames, rows * width + 48, ch), BF16)]
        + [pltpu.HBM((frames, size, ch), BF16) for size in sizes for _ in range(members)],
        scratch_shapes=[
            VMEM((frames, band, width, ch), BF16),
            pltpu.SemaphoreType.DMA((members * len(sizes), frames)),
        ],
        compiler_params=params(16),
        cost_estimate=COST,
        name="norm",
    )(conv, own, other, gain.reshape(1, ch), shift.reshape(1, ch), *halo_rows)


def guest_kernel(count, members, video_ref, packet_ref, weight_ref, gain_ref, shift_ref, *refs):
    keep_ref, mate_ref, *away_refs = refs[:-3]
    hidden_ref, wide_ref, sem = refs[-3:]
    outs = [[keep_ref], [mate_ref]] + [[ref.at[k] for ref in away_refs] for k in range(2)]
    frames, band, width, ch = video_ref.shape
    rows = (packet_ref.shape[1] - 48) // width
    here = lax.axis_index("tm")

    @pl.when(jnp.logical_and(here >= members, here % 2 == 0))
    def _():
        widen(weight_ref, wide_ref)
        for frame in range(frames):
            parts = packet_ref[frame, rows * width :].astype(F32)
            both = parts[:16] + parts[16:32] + parts[32:]
            sums = [both[:8], both[8:]]
            apply = norm_of(sums, count, gain_ref, shift_ref)

            def write(row, value):
                hidden_ref[frame, row] = apply(value)

            read = padded_read(
                band,
                lambda r: video_ref[frame, r],
                lambda: packet_ref[frame, :width],
                lambda: packet_ref[frame, (rows - 1) * width : rows * width],
            )
            conv_rows(band, read, wide_ref, write)
            for copy in piece_copies(hidden_ref, frame, outs, members, sem):
                copy.start()
        for frame in range(frames):
            for copy in piece_copies(hidden_ref, frame, outs, members, sem):
                copy.wait()

    @pl.when(here < members)
    def _():
        hidden_ref[...] = jnp.zeros_like(hidden_ref)
        for frame in range(frames):
            for copy in piece_copies(hidden_ref, frame, outs, members, sem):
                copy.start()
        for frame in range(frames):
            for copy in piece_copies(hidden_ref, frame, outs, members, sem):
                copy.wait()


def guest_call(video, packet, weight, gain, shift, count, members, sizes):
    frames, band, width, ch = video.shape
    piece = (frames, band * width // members, ch)
    shapes = [piece, piece] + [(2, frames, size, ch) for size in sizes]
    return pl.pallas_call(
        functools.partial(guest_kernel, count, members),
        in_specs=[vspec()] * 5,
        out_specs=[hspec()] * len(shapes),
        out_shape=[pltpu.HBM(shape, BF16) for shape in shapes],
        scratch_shapes=[
            VMEM(video.shape, BF16),
            VMEM((4 * ch, 6 * ch), BF16),
            pltpu.SemaphoreType.DMA((2 + 2 * len(sizes), frames)),
        ],
        compiler_params=params(24),
        cost_estimate=LONG,
        name="guest",
    )(video, packet, weight, gain.reshape(1, ch), shift.reshape(1, ch))


def pack_kernel(weight_ref, out_ref):
    ch = weight_ref.shape[-1]
    out_ref[...] = jnp.zeros_like(out_ref)
    for layer in range(3):
        for out in range(2):
            for tap in range(3):
                row = out + 2 - tap
                out_ref[layer, row * ch : (row + 1) * ch, out * ch : (out + 1) * ch] = weight_ref[
                    layer, tap
                ]


def pack_call(weight):
    layers, _, ch, _ = weight.shape
    return pl.pallas_call(
        pack_kernel,
        in_specs=[vspec()],
        out_specs=vspec(),
        out_shape=jax.ShapeDtypeStruct((layers, 4 * ch, 2 * ch), BF16),
        compiler_params=params(8),
        cost_estimate=LONG,
        name="pack",
    )(weight)


def pair(read, write, time, layer, wide_ref):
    ch = wide_ref.shape[2] // 2
    dilation = 2**layer
    frames = [read(time + (a - 2) * dilation) for a in range(4)]
    both = jnp.dot(jnp.concatenate(frames, axis=-1), wide_ref[layer], preferred_element_type=F32)
    write(time, (both[:, :ch] + frames[2].astype(F32)).astype(BF16))
    write(time + dilation, (both[:, ch:] + frames[3].astype(F32)).astype(BF16))


def ahead_kernel(members, *refs):
    pieces, (wide_ref, out_ref, u0_ref) = refs[:members], refs[members:]
    step = pieces[0].shape[0]
    me = lax.axis_index("tm") % members
    for k in range(members):
        u0_ref[pl.ds((me ^ k) * step, step)] = pieces[k][...]

    def write1(t, value):
        out_ref[t - 2] = value

    for time in range(2, SPAN, 2):
        pair(lambda t: u0_ref[t], write1, time, 0, wide_ref)


def ahead_call(own, wide, cost):
    members = len(own)
    _, size, ch = own[0].shape
    return pl.pallas_call(
        functools.partial(ahead_kernel, members),
        in_specs=[vspec()] * (members + 1),
        out_specs=vspec(),
        out_shape=jax.ShapeDtypeStruct((SPAN - 2, size, ch), BF16),
        scratch_shapes=[VMEM((SPAN, size, ch), BF16)],
        compiler_params=params(16),
        cost_estimate=cost,
        name="ahead",
    )(*own, wide)


def early_kernel(members, plan, first, *refs):
    arrays, (ahead_ref, wide_ref, out_ref, u0_ref, u1_ref) = refs[: len(plan)], refs[len(plan) :]
    size = out_ref.shape[1]
    lead = SPAN - 2
    me = lax.axis_index("tm") % members
    for ref, (kind, k, source, target, rows) in zip(arrays, plan):
        value = ref.at[0] if len(ref.shape) == 4 else ref
        step = value.shape[0]
        here, there = slice(target, target + rows), slice(source, source + rows)
        if kind == "own":

            @pl.when(me == k)
            def _():
                u0_ref[lead : lead + step, here] = value[:, there]

        elif kind == "middle":
            u0_ref[2:4, here] = value[:, there]
        else:

            @pl.when((me ^ k) % 2 == 0)
            def _():
                u0_ref[pl.ds(2 * (me ^ k), step), here] = value[:, there]

    def write1(t, value):
        u1_ref[t + 4] = value

    def read1(t):
        return u1_ref[t + 4] if t < 2 else ahead_ref[t - 2, first : first + size]

    def write2(t, value):
        out_ref[t] = value

    for time in range(-4, 2, 2):
        pair(lambda t: u0_ref[t + lead], write1, time, 0, wide_ref)
    for time in range(0, SPAN, 4):
        for odd in range(2):
            pair(read1, write2, time + odd, 1, wide_ref)


def early_call(sources, aheads, wide, members, first, size):
    plan, arrays = [], []
    start, ahead = first, aheads[0]
    for block in aheads[1:]:
        if start >= ahead.shape[1]:
            start, ahead = start - ahead.shape[1], block
    for kind, k, blocks in sources:
        at = 0
        for block in blocks:
            rows = block.shape[-2]
            low, high = max(first, at), min(first + size, at + rows)
            if low < high:
                plan.append((kind, k, low - at, low - first, high - low))
                arrays.append(block)
            at += rows
    ch = wide.shape[-1] // 2
    return pl.pallas_call(
        functools.partial(early_kernel, members, plan, start),
        in_specs=[vspec()] * (len(arrays) + 2),
        out_specs=vspec(),
        out_shape=jax.ShapeDtypeStruct((SPAN, size, ch), BF16),
        scratch_shapes=[VMEM((SPAN, size, ch), BF16), VMEM((6, size, ch), BF16)],
        compiler_params=params(16),
        cost_estimate=COST,
        name="early",
    )(*arrays, ahead, wide)


def late_kernel(members, own_ref, halo_ref, wide_ref, *refs):
    outs, u3_ref = refs[:-1], refs[-1]
    step = outs[0].shape[0]
    me = lax.axis_index("tm") % members

    def write3(t, value):
        u3_ref[t] = value

    for time in range(4):
        pair(
            lambda t: own_ref[t] if t >= 0 else halo_ref[t + SPAN], write3, time, 2, wide_ref
        )
    for k in range(members):
        outs[k][...] = u3_ref[pl.ds((me ^ k) * step, step)]


def late_call(own, halo, wide, members):
    frames, size, ch = own.shape
    return pl.pallas_call(
        functools.partial(late_kernel, members),
        in_specs=[vspec()] * 3,
        out_specs=[vspec()] * members,
        out_shape=[jax.ShapeDtypeStruct((frames // members, size, ch), BF16)] * members,
        scratch_shapes=[VMEM(own.shape, BF16)],
        compiler_params=params(12),
        cost_estimate=COST,
        name="late",
    )(own, halo, wide)


def place_kernel(members, offsets, *refs):
    count = members * len(offsets)
    pieces, (out_ref, sem) = refs[:count], refs[-2:]
    me = lax.axis_index("tm") % members
    copies = []
    for i, offset in enumerate(offsets):
        for k in range(members):
            n = i * members + k
            rows = pl.ds(offset, pieces[n].shape[1])
            copies.append(
                pltpu.make_async_copy(pieces[n], out_ref.at[:, me ^ k, rows], sem.at[n])
            )
    for copy in copies:
        copy.start()
    for copy in copies:
        copy.wait()


def place_call(chunks, offsets, quarter, before=None):
    members = len(chunks[0])
    frames, _, ch = chunks[0][0].shape
    pieces = sum(chunks, [])
    shape = jax.ShapeDtypeStruct((frames, members, quarter, ch), BF16)
    return pl.pallas_call(
        functools.partial(place_kernel, members, offsets),
        in_specs=[vspec()] * len(pieces) + [hspec()] * (before is not None),
        out_specs=hspec(),
        out_shape=pltpu.HBM(shape.shape, BF16),
        input_output_aliases={} if before is None else {len(pieces): 0},
        scratch_shapes=[pltpu.SemaphoreType.DMA((len(pieces),))],
        compiler_params=params(8),
        cost_estimate=COST,
        name="place",
    )(*pieces, *([] if before is None else [hbm(before)]))


def halo_rows(video):
    size, row = lax.axis_size("rows"), lax.axis_index("rows")
    band = video.shape[1]
    if size == 2:
        mine = lax.dynamic_slice_in_dim(video, jnp.where(row == 0, band - 1, 0), 1, axis=1)[:, 0]
        other = lax.ppermute(mine, "rows", [(0, 1), (1, 0)])
        return other, other
    up = [(i, i + 1) for i in range(size - 1)]
    down = [(j, i) for i, j in up]
    return lax.ppermute(video[:, -1], "rows", up), lax.ppermute(video[:, 0], "rows", down)


def other_sums(sums):
    if lax.axis_size("rows") == 2:
        return lax.ppermute(sums, "rows", [(0, 1), (1, 0)])
    return lax.psum(sums, "rows") - sums


def after(value, *others):
    return lax.optimization_barrier((value, *others))[0]


def body(video, spatial_weight, norm_gain, norm_shift, temporal_weight):
    frames, band, width, ch = video.shape
    total = lax.axis_size("tm")
    me = lax.axis_index("tm") % (SPAN // frames)
    rows = lax.axis_size("rows")
    members = SPAN // frames
    swaps = [[(i, i ^ k) for i in range(total)] for k in range(members)]
    onward = [(i, i + members) for i in range(total - members)]
    guest_pairs = [(i, i + members - 1) for i in range(1, total - members, 2)]
    guest_swaps = [[(i, i ^ k) for i in range(0, total, 2)] for k in range(members)]

    guest_video = lax.ppermute(video, "tm", guest_pairs)
    above, below = halo_rows(video)
    conv, sums = conv_call(video, spatial_weight)
    conv, sums = edge_call(conv, above, below, spatial_weight, sums)
    count = band * rows * width * (ch // GROUPS)
    quarter = band * width // members
    own_sizes, guest_sizes, out_sizes = [
        [quarter * part // 60 for part in parts] for parts in (OWN_PARTS, GUEST_PARTS, OUT_PARTS)
    ]
    halo_list = [above] if above is below else [above, below]
    packet, *pieces = norm_call(
        conv, sums, other_sums(sums), halo_list, norm_gain, norm_shift, count, members, own_sizes
    )

    def swap(four, waits=None):
        got = [four[0]]
        for k in range(1, members):
            value = four[k] if waits is None else after(four[k], waits[k])
            got.append(lax.ppermute(value, "tm", swaps[k]))
        return got

    guest_packet = lax.ppermute(packet, "tm", guest_pairs)
    keep, mate, *aways = guest_call(
        guest_video, guest_packet, spatial_weight, norm_gain, norm_shift, count, members, guest_sizes
    )
    wide = pack_call(after(temporal_weight, keep))
    sources = [(kind, k, []) for kind in ("own", "guest") for k in range(members)]
    sources.append(("middle", 0, []))

    def add(start, arrays):
        for (_, _, blocks), array in zip(sources[start:], arrays):
            blocks.append(array)

    aheads, passed, results = [], [], []

    def block(i, gate):
        four = pieces[i * members : (i + 1) * members]
        own = swap(four, [gate] * members if i else None)
        crossed = lax.ppermute(after(aways[i], own[2]) if i else aways[i], "tm", guest_swaps[2])
        four = own if i else after(own, wide)
        middle = functools.reduce(
            lambda acc, k: jnp.where(me == (2 ^ k), four[k], acc), range(1, members), four[0]
        )
        add(0, own)
        add(2 * members, [lax.ppermute(middle, "tm", onward)])
        if i == 0:
            add(members, [keep, lax.ppermute(after(mate, wide), "tm", guest_swaps[1])])
        waits = [middle] if i else [middle, crossed]
        aheads.append(ahead_call(own, after(wide, *waits), COST if i else LONG))
        forward = crossed[1] if i else after(crossed[1], aheads[0])
        add(members + 2, [crossed, lax.ppermute(forward, "tm", guest_swaps[1])])

    block(0, None)
    first = 0
    for i, size in enumerate(out_sizes):
        u2 = early_call(sources, aheads, wide, members, first, size)
        if i == 0:
            block(1, aheads[0])
        if i > 1:
            u2 = after(u2, passed[i - 2])
        passed.append(lax.ppermute(u2, "tm", onward))
        following = late_call(u2, passed[-1], wide, members)
        results.append(swap(following, results[-1] if results else None))
        late = following if i < 2 else late
        first += size
    offsets = [sum(out_sizes[:i]) for i in range(len(out_sizes))]
    out = place_call(results[:2], offsets[:2], quarter)
    out = place_call(results[2:], offsets[2:], quarter, out)
    return out.reshape(frames, band, width, ch)


def solution(mesh):
    return jax.shard_map(
        body,
        mesh=mesh,
        in_specs=(P("tm", "rows", None, None), P(), P(), P(), P()),
        out_specs=P("tm", "rows", None, None),
        check_vma=False,
    )
```

```python
import functools

import jax
import jax.numpy as jnp
from jax import lax
from jax.experimental import pallas as pl
from jax.experimental.pallas import tpu as pltpu
from jax.sharding import PartitionSpec as P

GROUPS = 32
SPAN = 8
OWN_PARTS = (42, 18)
GUEST_PARTS = (42, 18)
OUT_PARTS = (32, 10, 9, 9)
VMEM = pltpu.VMEM
ANY = pl.ANY
F32 = jnp.float32
BF16 = jnp.bfloat16


def vspec():
    return pl.BlockSpec(memory_space=VMEM)


def params(mib):
    return pltpu.CompilerParams(vmem_limit_bytes=mib << 20)


COST = pl.CostEstimate(flops=0, bytes_accessed=0, transcendentals=0)
LONG = pl.CostEstimate(flops=20_000_000_000, bytes_accessed=0, transcendentals=0)


def hspec():
    return pl.BlockSpec(memory_space=ANY)


def hbm(value):
    return pltpu.with_memory_space_constraint(value, pltpu.HBM)


def shifted_sum(taps):
    width, ch = taps.shape[0], taps.shape[1] // 3
    column = lax.broadcasted_iota(jnp.int32, (width, ch), 0)
    left = jnp.where(column == 0, 0.0, pltpu.roll(taps[:, :ch], 1, 0))
    right = jnp.where(column == width - 1, 0.0, pltpu.roll(taps[:, 2 * ch :], width - 1, 0))
    return left + taps[:, ch : 2 * ch] + right


def fold(value):
    return jnp.sum(value.reshape(value.shape[0] // 8, 8, value.shape[1]), axis=0)


def widen(weight_ref, wide_ref):
    ch = weight_ref.shape[-1]
    wide_ref[...] = jnp.zeros_like(wide_ref)
    for out in range(2):
        for col in range(3):
            for row in range(3):
                wide_ref[
                    (out + row) * ch : (out + row + 1) * ch,
                    (out * 3 + col) * ch : (out * 3 + col + 1) * ch,
                ] = weight_ref[row, col]


def conv_rows(band, read, wide_ref, write):
    ch = wide_ref.shape[0] // 4
    for first in range(0, band, 2):
        lhs = jnp.concatenate([read(r) for r in range(first - 1, first + 3)], axis=-1)
        wide = jnp.dot(lhs, wide_ref[...], preferred_element_type=F32)
        for out in range(2):
            write(first + out, shifted_sum(wide[:, out * 3 * ch : (out + 1) * 3 * ch]))


def padded_read(band, row_of, above, below):
    row, rows = lax.axis_index("rows"), lax.axis_size("rows")

    def read(r):
        if r < 0:
            return jnp.where(row > 0, above(), jnp.zeros_like(above()))
        if r == band:
            return jnp.where(row < rows - 1, below(), jnp.zeros_like(below()))
        return row_of(r)

    return read


def conv_kernel(band, video_ref, weight_ref, out_ref, sums_ref, wide_ref):
    @pl.when(pl.program_id(0) == 0)
    def _():
        widen(weight_ref, wide_ref)

    ch = weight_ref.shape[-1]
    sums = [jnp.zeros((8, ch), F32), jnp.zeros((8, ch), F32)]

    def read(row):
        if 0 <= row < band:
            return video_ref[0, row]
        return jnp.zeros_like(video_ref[0, 0])

    def write(row, value):
        out_ref[0, row] = value
        if 0 < row < band - 1:
            sums[0] = sums[0] + fold(value)
            sums[1] = sums[1] + fold(value * value)

    conv_rows(band, read, wide_ref, write)
    sums_ref[0, 0] = sums[0]
    sums_ref[0, 1] = sums[1]


def frame_spec(*shape):
    return pl.BlockSpec((1,) + shape, lambda f, *_: (f,) + (0,) * len(shape))


def conv_call(video, weight):
    frames, band, width, ch = video.shape
    return pl.pallas_call(
        functools.partial(conv_kernel, band),
        grid=(frames,),
        in_specs=[
            frame_spec(band, width, ch),
            pl.BlockSpec(weight.shape, lambda f: (0, 0, 0, 0)),
        ],
        out_specs=[frame_spec(band, width, ch), frame_spec(2, 8, ch)],
        out_shape=[
            jax.ShapeDtypeStruct(video.shape, F32),
            jax.ShapeDtypeStruct((frames, 2, 8, ch), F32),
        ],
        scratch_shapes=[VMEM((4 * ch, 6 * ch), BF16)],
        compiler_params=params(16),
        cost_estimate=LONG,
        name="conv",
    )(hbm(video), hbm(weight))


def edge_kernel(conv_ref, above_ref, below_ref, weight_ref, sums_ref, out_ref, out_sums_ref):
    frames, band = conv_ref.shape[:2]
    row, rows = lax.axis_index("rows"), lax.axis_size("rows")
    sides = ((0, above_ref, 0, row > 0), (band - 1, below_ref, 2, row < rows - 1))
    for frame in range(frames):
        total, square = sums_ref[frame, 0], sums_ref[frame, 1]
        for place, halo_ref, tap, there in sides:
            halo = jnp.where(there, halo_ref[frame], jnp.zeros_like(halo_ref[frame]))
            taps = jnp.concatenate([weight_ref[tap, col] for col in range(3)], axis=-1)
            wide = jnp.dot(halo, taps, preferred_element_type=F32)
            value = conv_ref[frame, place] + shifted_sum(wide)
            out_ref[frame, place] = value
            total = total + fold(value)
            square = square + fold(value * value)
        out_sums_ref[frame, 0] = total
        out_sums_ref[frame, 1] = square


def edge_call(conv, above, below, weight, sums):
    return pl.pallas_call(
        edge_kernel,
        in_specs=[vspec()] * 5,
        out_specs=[vspec()] * 2,
        out_shape=[
            jax.ShapeDtypeStruct(conv.shape, F32),
            jax.ShapeDtypeStruct(sums.shape, F32),
        ],
        input_output_aliases={0: 0},
        compiler_params=params(12),
        cost_estimate=COST,
        name="edge",
    )(conv, above, below, weight, sums)


def over_groups(value, per_group):
    lane = lax.broadcasted_iota(jnp.int32, value.shape, 1)
    lanes = value.shape[1]
    step = 1
    while step < per_group:
        value = value + pltpu.roll(value, lanes - step, 1)
        step *= 2
    value = jnp.where(lane % per_group == 0, value, 0.0)
    step = 1
    while step < per_group:
        value = value + pltpu.roll(value, step, 1)
        step *= 2
    return value


def norm_of(sums, count, gain_ref, shift_ref):
    ch = gain_ref.shape[-1]
    total = [
        over_groups(jnp.broadcast_to(jnp.sum(x, axis=0, keepdims=True), (8, ch)), ch // GROUPS)
        for x in sums
    ]
    mean = total[0] / count
    var = total[1] / count - mean * mean
    scale = (lax.rsqrt(var + 1e-05) * gain_ref[...])[:1]
    mean = mean[:1]
    shift = shift_ref[...]

    def apply(value):
        v = (value - mean) * scale + shift
        return (0.5 * v * (1.0 + jnp.tanh(0.5 * v))).astype(BF16)

    return apply


def piece_copies(hidden_ref, frame, outs, members, sem):
    frames, band, width, ch = hidden_ref.shape
    flat = hidden_ref.reshape(frames, band * width, ch)
    me = lax.axis_index("tm") % members
    quarter = band * width // members
    copies = []
    for k, blocks in enumerate(outs):
        offset = 0
        for block in blocks:
            rows = pl.ds(pl.multiple_of((me ^ k) * quarter + offset, 16), block.shape[1])
            copies.append(
                pltpu.make_async_copy(
                    flat.at[frame, rows], block.at[frame], sem.at[len(copies), frame]
                )
            )
            offset += block.shape[1]
    return copies


def norm_kernel(count, members, rows, conv_ref, own_ref, other_ref, gain_ref, shift_ref, *refs):
    row_refs, packet_ref, (hidden_ref, sem) = refs[:rows], refs[rows], refs[-2:]
    outs = [refs[rows + 1 + k : -2 : members] for k in range(members)]
    frames, band, width, ch = conv_ref.shape
    for frame in range(frames):
        sums = [own_ref[frame, i] + other_ref[frame, i] for i in range(2)]
        for i, ref in enumerate(row_refs):
            packet_ref[frame, i * width : (i + 1) * width] = ref[frame]
        rest = jnp.concatenate(sums, axis=0)
        for part in range(3):
            at = rows * width + part * 16
            short = rest.astype(BF16)
            rest = rest - short.astype(F32)
            packet_ref[frame, at : at + 16] = short
        apply = norm_of(sums, count, gain_ref, shift_ref)

        @pl.loop(0, band)
        def _(row):
            hidden_ref[frame, row] = apply(conv_ref[frame, row])

        for copy in piece_copies(hidden_ref, frame, outs, members, sem):
            copy.start()
    for frame in range(frames):
        for copy in piece_copies(hidden_ref, frame, outs, members, sem):
            copy.wait()


def norm_call(conv, own, other, halo_rows, gain, shift, count, members, sizes):
    frames, band, width, ch = conv.shape
    rows = len(halo_rows)
    return pl.pallas_call(
        functools.partial(norm_kernel, count, members, rows),
        in_specs=[vspec()] * (5 + rows),
        out_specs=[vspec()] + [hspec()] * (members * len(sizes)),
        out_shape=[jax.ShapeDtypeStruct((frames, rows * width + 48, ch), BF16)]
        + [pltpu.HBM((frames, size, ch), BF16) for size in sizes for _ in range(members)],
        scratch_shapes=[
            VMEM((frames, band, width, ch), BF16),
            pltpu.SemaphoreType.DMA((members * len(sizes), frames)),
        ],
        compiler_params=params(16),
        cost_estimate=COST,
        name="norm",
    )(conv, own, other, gain.reshape(1, ch), shift.reshape(1, ch), *halo_rows)


def guest_kernel(count, members, video_ref, packet_ref, weight_ref, gain_ref, shift_ref, *refs):
    keep_ref, mate_ref, *away_refs = refs[:-3]
    hidden_ref, wide_ref, sem = refs[-3:]
    outs = [[keep_ref], [mate_ref]] + [[ref.at[k] for ref in away_refs] for k in range(2)]
    frames, band, width, ch = video_ref.shape
    rows = (packet_ref.shape[1] - 48) // width
    here = lax.axis_index("tm")

    @pl.when(jnp.logical_and(here >= members, here % 2 == 0))
    def _():
        widen(weight_ref, wide_ref)
        for frame in range(frames):
            parts = packet_ref[frame, rows * width :].astype(F32)
            both = parts[:16] + parts[16:32] + parts[32:]
            sums = [both[:8], both[8:]]
            apply = norm_of(sums, count, gain_ref, shift_ref)

            def write(row, value):
                hidden_ref[frame, row] = apply(value)

            read = padded_read(
                band,
                lambda r: video_ref[frame, r],
                lambda: packet_ref[frame, :width],
                lambda: packet_ref[frame, (rows - 1) * width : rows * width],
            )
            conv_rows(band, read, wide_ref, write)
            for copy in piece_copies(hidden_ref, frame, outs, members, sem):
                copy.start()
        for frame in range(frames):
            for copy in piece_copies(hidden_ref, frame, outs, members, sem):
                copy.wait()

    @pl.when(here < members)
    def _():
        hidden_ref[...] = jnp.zeros_like(hidden_ref)
        for frame in range(frames):
            for copy in piece_copies(hidden_ref, frame, outs, members, sem):
                copy.start()
        for frame in range(frames):
            for copy in piece_copies(hidden_ref, frame, outs, members, sem):
                copy.wait()


def guest_call(video, packet, weight, gain, shift, count, members, sizes):
    frames, band, width, ch = video.shape
    piece = (frames, band * width // members, ch)
    shapes = [piece, piece] + [(2, frames, size, ch) for size in sizes]
    return pl.pallas_call(
        functools.partial(guest_kernel, count, members),
        in_specs=[vspec()] * 5,
        out_specs=[hspec()] * len(shapes),
        out_shape=[pltpu.HBM(shape, BF16) for shape in shapes],
        scratch_shapes=[
            VMEM(video.shape, BF16),
            VMEM((4 * ch, 6 * ch), BF16),
            pltpu.SemaphoreType.DMA((2 + 2 * len(sizes), frames)),
        ],
        compiler_params=params(24),
        cost_estimate=LONG,
        name="guest",
    )(video, packet, weight, gain.reshape(1, ch), shift.reshape(1, ch))


def pack_kernel(weight_ref, out_ref):
    ch = weight_ref.shape[-1]
    out_ref[...] = jnp.zeros_like(out_ref)
    for layer in range(3):
        for out in range(2):
            for tap in range(3):
                row = out + 2 - tap
                out_ref[layer, row * ch : (row + 1) * ch, out * ch : (out + 1) * ch] = weight_ref[
                    layer, tap
                ]


def pack_call(weight):
    layers, _, ch, _ = weight.shape
    return pl.pallas_call(
        pack_kernel,
        in_specs=[vspec()],
        out_specs=vspec(),
        out_shape=jax.ShapeDtypeStruct((layers, 4 * ch, 2 * ch), BF16),
        compiler_params=params(8),
        cost_estimate=LONG,
        name="pack",
    )(weight)


def pair(read, write, time, layer, wide_ref):
    ch = wide_ref.shape[2] // 2
    dilation = 2**layer
    frames = [read(time + (a - 2) * dilation) for a in range(4)]
    both = jnp.dot(jnp.concatenate(frames, axis=-1), wide_ref[layer], preferred_element_type=F32)
    write(time, (both[:, :ch] + frames[2].astype(F32)).astype(BF16))
    write(time + dilation, (both[:, ch:] + frames[3].astype(F32)).astype(BF16))


def ahead_kernel(members, *refs):
    pieces, (wide_ref, out_ref, u0_ref) = refs[:members], refs[members:]
    step = pieces[0].shape[0]
    me = lax.axis_index("tm") % members
    for k in range(members):
        u0_ref[pl.ds((me ^ k) * step, step)] = pieces[k][...]

    def write1(t, value):
        out_ref[t - 2] = value

    for time in range(2, SPAN, 2):
        pair(lambda t: u0_ref[t], write1, time, 0, wide_ref)


def ahead_call(own, wide, cost):
    members = len(own)
    _, size, ch = own[0].shape
    return pl.pallas_call(
        functools.partial(ahead_kernel, members),
        in_specs=[vspec()] * (members + 1),
        out_specs=vspec(),
        out_shape=jax.ShapeDtypeStruct((SPAN - 2, size, ch), BF16),
        scratch_shapes=[VMEM((SPAN, size, ch), BF16)],
        compiler_params=params(16),
        cost_estimate=cost,
        name="ahead",
    )(*own, wide)


def early_kernel(members, plan, first, *refs):
    arrays, (ahead_ref, wide_ref, out_ref, u0_ref, u1_ref) = refs[: len(plan)], refs[len(plan) :]
    size = out_ref.shape[1]
    lead = SPAN - 2
    me = lax.axis_index("tm") % members
    for ref, (kind, k, source, target, rows) in zip(arrays, plan):
        value = ref.at[0] if len(ref.shape) == 4 else ref
        step = value.shape[0]
        here, there = slice(target, target + rows), slice(source, source + rows)
        if kind == "own":

            @pl.when(me == k)
            def _():
                u0_ref[lead : lead + step, here] = value[:, there]

        elif kind == "middle":
            u0_ref[2:4, here] = value[:, there]
        else:

            @pl.when((me ^ k) % 2 == 0)
            def _():
                u0_ref[pl.ds(2 * (me ^ k), step), here] = value[:, there]

    def write1(t, value):
        u1_ref[t + 4] = value

    def read1(t):
        return u1_ref[t + 4] if t < 2 else ahead_ref[t - 2, first : first + size]

    def write2(t, value):
        out_ref[t] = value

    for time in range(-4, 2, 2):
        pair(lambda t: u0_ref[t + lead], write1, time, 0, wide_ref)
    for time in range(0, SPAN, 4):
        for odd in range(2):
            pair(read1, write2, time + odd, 1, wide_ref)


def early_call(sources, aheads, wide, members, first, size):
    plan, arrays = [], []
    start, ahead = first, aheads[0]
    for block in aheads[1:]:
        if start >= ahead.shape[1]:
            start, ahead = start - ahead.shape[1], block
    for kind, k, blocks in sources:
        at = 0
        for block in blocks:
            rows = block.shape[-2]
            low, high = max(first, at), min(first + size, at + rows)
            if low < high:
                plan.append((kind, k, low - at, low - first, high - low))
                arrays.append(block)
            at += rows
    ch = wide.shape[-1] // 2
    return pl.pallas_call(
        functools.partial(early_kernel, members, plan, start),
        in_specs=[vspec()] * (len(arrays) + 2),
        out_specs=vspec(),
        out_shape=jax.ShapeDtypeStruct((SPAN, size, ch), BF16),
        scratch_shapes=[VMEM((SPAN, size, ch), BF16), VMEM((6, size, ch), BF16)],
        compiler_params=params(16),
        cost_estimate=COST,
        name="early",
    )(*arrays, ahead, wide)


def late_kernel(members, own_ref, halo_ref, wide_ref, *refs):
    outs, u3_ref = refs[:-1], refs[-1]
    step = outs[0].shape[0]
    me = lax.axis_index("tm") % members

    def write3(t, value):
        u3_ref[t] = value

    for time in range(4):
        pair(
            lambda t: own_ref[t] if t >= 0 else halo_ref[t + SPAN], write3, time, 2, wide_ref
        )
    for k in range(members):
        outs[k][...] = u3_ref[pl.ds((me ^ k) * step, step)]


def late_call(own, halo, wide, members):
    frames, size, ch = own.shape
    return pl.pallas_call(
        functools.partial(late_kernel, members),
        in_specs=[vspec()] * 3,
        out_specs=[vspec()] * members,
        out_shape=[jax.ShapeDtypeStruct((frames // members, size, ch), BF16)] * members,
        scratch_shapes=[VMEM(own.shape, BF16)],
        compiler_params=params(12),
        cost_estimate=COST,
        name="late",
    )(own, halo, wide)


def place_kernel(members, offsets, *refs):
    count = members * len(offsets)
    pieces, (out_ref, sem) = refs[:count], refs[-2:]
    me = lax.axis_index("tm") % members
    copies = []
    for i, offset in enumerate(offsets):
        for k in range(members):
            n = i * members + k
            rows = pl.ds(offset, pieces[n].shape[1])
            copies.append(
                pltpu.make_async_copy(pieces[n], out_ref.at[:, me ^ k, rows], sem.at[n])
            )
    for copy in copies:
        copy.start()
    for copy in copies:
        copy.wait()


def place_call(chunks, offsets, quarter, before=None):
    members = len(chunks[0])
    frames, _, ch = chunks[0][0].shape
    pieces = sum(chunks, [])
    shape = jax.ShapeDtypeStruct((frames, members, quarter, ch), BF16)
    return pl.pallas_call(
        functools.partial(place_kernel, members, offsets),
        in_specs=[vspec()] * len(pieces) + [hspec()] * (before is not None),
        out_specs=hspec(),
        out_shape=pltpu.HBM(shape.shape, BF16),
        input_output_aliases={} if before is None else {len(pieces): 0},
        scratch_shapes=[pltpu.SemaphoreType.DMA((len(pieces),))],
        compiler_params=params(8),
        cost_estimate=COST,
        name="place",
    )(*pieces, *([] if before is None else [hbm(before)]))


def halo_rows(video):
    size, row = lax.axis_size("rows"), lax.axis_index("rows")
    band = video.shape[1]
    if size == 2:
        mine = lax.dynamic_slice_in_dim(video, jnp.where(row == 0, band - 1, 0), 1, axis=1)[:, 0]
        other = lax.ppermute(mine, "rows", [(0, 1), (1, 0)])
        return other, other
    up = [(i, i + 1) for i in range(size - 1)]
    down = [(j, i) for i, j in up]
    return lax.ppermute(video[:, -1], "rows", up), lax.ppermute(video[:, 0], "rows", down)


def other_sums(sums):
    if lax.axis_size("rows") == 2:
        return lax.ppermute(sums, "rows", [(0, 1), (1, 0)])
    return lax.psum(sums, "rows") - sums


def after(value, *others):
    return lax.optimization_barrier((value, *others))[0]


def body(video, spatial_weight, norm_gain, norm_shift, temporal_weight):
    frames, band, width, ch = video.shape
    total = lax.axis_size("tm")
    me = lax.axis_index("tm") % (SPAN // frames)
    rows = lax.axis_size("rows")
    members = SPAN // frames
    swaps = [[(i, i ^ k) for i in range(total)] for k in range(members)]
    onward = [(i, i + members) for i in range(total - members)]
    guest_pairs = [(i, i + members - 1) for i in range(1, total - members, 2)]
    guest_swaps = [[(i, i ^ k) for i in range(0, total, 2)] for k in range(members)]

    guest_video = lax.ppermute(video, "tm", guest_pairs)
    above, below = halo_rows(video)
    conv, sums = conv_call(video, spatial_weight)
    conv, sums = edge_call(conv, above, below, spatial_weight, sums)
    count = band * rows * width * (ch // GROUPS)
    quarter = band * width // members
    own_sizes, guest_sizes, out_sizes = [
        [quarter * part // 60 for part in parts] for parts in (OWN_PARTS, GUEST_PARTS, OUT_PARTS)
    ]
    halo_list = [above] if above is below else [above, below]
    packet, *pieces = norm_call(
        conv, sums, other_sums(sums), halo_list, norm_gain, norm_shift, count, members, own_sizes
    )

    def swap(four, waits=None):
        got = [four[0]]
        for k in range(1, members):
            value = four[k] if waits is None else after(four[k], waits[k])
            got.append(lax.ppermute(value, "tm", swaps[k]))
        return got

    guest_packet = lax.ppermute(packet, "tm", guest_pairs)
    keep, mate, *aways = guest_call(
        guest_video, guest_packet, spatial_weight, norm_gain, norm_shift, count, members, guest_sizes
    )
    wide = pack_call(after(temporal_weight, keep))
    sources = [(kind, k, []) for kind in ("own", "guest") for k in range(members)]
    sources.append(("middle", 0, []))

    def add(start, arrays):
        for (_, _, blocks), array in zip(sources[start:], arrays):
            blocks.append(array)

    aheads, passed, results = [], [], []

    def block(i, gate):
        four = pieces[i * members : (i + 1) * members]
        own = swap(four, [gate] * members if i else None)
        crossed = lax.ppermute(after(aways[i], own[2]) if i else aways[i], "tm", guest_swaps[2])
        four = own if i else after(own, wide)
        middle = functools.reduce(
            lambda acc, k: jnp.where(me == (2 ^ k), four[k], acc), range(1, members), four[0]
        )
        add(0, own)
        add(2 * members, [lax.ppermute(middle, "tm", onward)])
        if i == 0:
            add(members, [keep, lax.ppermute(after(mate, wide), "tm", guest_swaps[1])])
        waits = [middle] if i else [middle, crossed]
        aheads.append(ahead_call(own, after(wide, *waits), COST if i else LONG))
        forward = crossed[1] if i else after(crossed[1], aheads[0])
        add(members + 2, [crossed, lax.ppermute(forward, "tm", guest_swaps[1])])

    block(0, None)
    first = 0
    for i, size in enumerate(out_sizes):
        u2 = early_call(sources, aheads, wide, members, first, size)
        if i == 0:
            block(1, aheads[0])
        if i > 1:
            u2 = after(u2, passed[0] if i == 2 else late[0])
        passed.append(lax.ppermute(u2, "tm", onward))
        following = late_call(u2, passed[-1], wide, members)
        results.append(swap(following, results[-1] if results else None))
        late = following if i < 2 else late
        first += size
    offsets = [sum(out_sizes[:i]) for i in range(len(out_sizes))]
    out = place_call(results[:2], offsets[:2], quarter)
    out = place_call(results[2:], offsets[2:], quarter, out)
    return out.reshape(frames, band, width, ch)


def solution(mesh):
    return jax.shard_map(
        body,
        mesh=mesh,
        in_specs=(P("tm", "rows", None, None), P(), P(), P(), P()),
        out_specs=P("tm", "rows", None, None),
        check_vma=False,
    )
```

```python
import functools

import jax
import jax.numpy as jnp
from jax import lax
from jax.experimental import pallas as pl
from jax.experimental.pallas import tpu as pltpu
from jax.sharding import PartitionSpec as P

GROUPS = 32
SPAN = 8
OWN_PARTS = (42, 18)
GUEST_PARTS = (42, 18)
OUT_PARTS = (32, 10, 9, 9)
VMEM = pltpu.VMEM
ANY = pl.ANY
F32 = jnp.float32
BF16 = jnp.bfloat16


def vspec():
    return pl.BlockSpec(memory_space=VMEM)


def params(mib):
    return pltpu.CompilerParams(vmem_limit_bytes=mib << 20)


COST = pl.CostEstimate(flops=0, bytes_accessed=0, transcendentals=0)
LONG = pl.CostEstimate(flops=20_000_000_000, bytes_accessed=0, transcendentals=0)


def hspec():
    return pl.BlockSpec(memory_space=ANY)


def hbm(value):
    return pltpu.with_memory_space_constraint(value, pltpu.HBM)


def shifted_sum(taps):
    width, ch = taps.shape[0], taps.shape[1] // 3
    column = lax.broadcasted_iota(jnp.int32, (width, ch), 0)
    left = jnp.where(column == 0, 0.0, pltpu.roll(taps[:, :ch], 1, 0))
    right = jnp.where(column == width - 1, 0.0, pltpu.roll(taps[:, 2 * ch :], width - 1, 0))
    return left + taps[:, ch : 2 * ch] + right


def fold(value):
    return jnp.sum(value.reshape(value.shape[0] // 8, 8, value.shape[1]), axis=0)


def widen(weight_ref, wide_ref):
    ch = weight_ref.shape[-1]
    wide_ref[...] = jnp.zeros_like(wide_ref)
    for out in range(2):
        for col in range(3):
            for row in range(3):
                wide_ref[
                    (out + row) * ch : (out + row + 1) * ch,
                    (out * 3 + col) * ch : (out * 3 + col + 1) * ch,
                ] = weight_ref[row, col]


def conv_rows(band, read, wide_ref, write):
    ch = wide_ref.shape[0] // 4
    for first in range(0, band, 2):
        lhs = jnp.concatenate([read(r) for r in range(first - 1, first + 3)], axis=-1)
        wide = jnp.dot(lhs, wide_ref[...], preferred_element_type=F32)
        for out in range(2):
            write(first + out, shifted_sum(wide[:, out * 3 * ch : (out + 1) * 3 * ch]))


def padded_read(band, row_of, above, below):
    row, rows = lax.axis_index("rows"), lax.axis_size("rows")

    def read(r):
        if r < 0:
            return jnp.where(row > 0, above(), jnp.zeros_like(above()))
        if r == band:
            return jnp.where(row < rows - 1, below(), jnp.zeros_like(below()))
        return row_of(r)

    return read


def conv_kernel(band, video_ref, weight_ref, out_ref, sums_ref, wide_ref):
    @pl.when(pl.program_id(0) == 0)
    def _():
        widen(weight_ref, wide_ref)

    ch = weight_ref.shape[-1]
    sums = [jnp.zeros((8, ch), F32), jnp.zeros((8, ch), F32)]

    def read(row):
        if 0 <= row < band:
            return video_ref[0, row]
        return jnp.zeros_like(video_ref[0, 0])

    def write(row, value):
        out_ref[0, row] = value
        if 0 < row < band - 1:
            sums[0] = sums[0] + fold(value)
            sums[1] = sums[1] + fold(value * value)

    conv_rows(band, read, wide_ref, write)
    sums_ref[0, 0] = sums[0]
    sums_ref[0, 1] = sums[1]


def frame_spec(*shape):
    return pl.BlockSpec((1,) + shape, lambda f, *_: (f,) + (0,) * len(shape))


def conv_call(video, weight):
    frames, band, width, ch = video.shape
    return pl.pallas_call(
        functools.partial(conv_kernel, band),
        grid=(frames,),
        in_specs=[
            frame_spec(band, width, ch),
            pl.BlockSpec(weight.shape, lambda f: (0, 0, 0, 0)),
        ],
        out_specs=[frame_spec(band, width, ch), frame_spec(2, 8, ch)],
        out_shape=[
            jax.ShapeDtypeStruct(video.shape, F32),
            jax.ShapeDtypeStruct((frames, 2, 8, ch), F32),
        ],
        scratch_shapes=[VMEM((4 * ch, 6 * ch), BF16)],
        compiler_params=params(16),
        cost_estimate=LONG,
        name="conv",
    )(hbm(video), hbm(weight))


def edge_kernel(conv_ref, above_ref, below_ref, weight_ref, sums_ref, out_ref, out_sums_ref):
    frames, band = conv_ref.shape[:2]
    row, rows = lax.axis_index("rows"), lax.axis_size("rows")
    sides = ((0, above_ref, 0, row > 0), (band - 1, below_ref, 2, row < rows - 1))
    for frame in range(frames):
        total, square = sums_ref[frame, 0], sums_ref[frame, 1]
        for place, halo_ref, tap, there in sides:
            halo = jnp.where(there, halo_ref[frame], jnp.zeros_like(halo_ref[frame]))
            taps = jnp.concatenate([weight_ref[tap, col] for col in range(3)], axis=-1)
            wide = jnp.dot(halo, taps, preferred_element_type=F32)
            value = conv_ref[frame, place] + shifted_sum(wide)
            out_ref[frame, place] = value
            total = total + fold(value)
            square = square + fold(value * value)
        out_sums_ref[frame, 0] = total
        out_sums_ref[frame, 1] = square


def edge_call(conv, above, below, weight, sums):
    return pl.pallas_call(
        edge_kernel,
        in_specs=[vspec()] * 5,
        out_specs=[vspec()] * 2,
        out_shape=[
            jax.ShapeDtypeStruct(conv.shape, F32),
            jax.ShapeDtypeStruct(sums.shape, F32),
        ],
        input_output_aliases={0: 0},
        compiler_params=params(12),
        cost_estimate=COST,
        name="edge",
    )(conv, above, below, weight, sums)


def over_groups(value, per_group):
    lane = lax.broadcasted_iota(jnp.int32, value.shape, 1)
    lanes = value.shape[1]
    step = 1
    while step < per_group:
        value = value + pltpu.roll(value, lanes - step, 1)
        step *= 2
    value = jnp.where(lane % per_group == 0, value, 0.0)
    step = 1
    while step < per_group:
        value = value + pltpu.roll(value, step, 1)
        step *= 2
    return value


def norm_of(sums, count, gain_ref, shift_ref):
    ch = gain_ref.shape[-1]
    total = [
        over_groups(jnp.broadcast_to(jnp.sum(x, axis=0, keepdims=True), (8, ch)), ch // GROUPS)
        for x in sums
    ]
    mean = total[0] / count
    var = total[1] / count - mean * mean
    scale = (lax.rsqrt(var + 1e-05) * gain_ref[...])[:1]
    mean = mean[:1]
    shift = shift_ref[...]

    def apply(value):
        v = (value - mean) * scale + shift
        return (0.5 * v * (1.0 + jnp.tanh(0.5 * v))).astype(BF16)

    return apply


def piece_copies(hidden_ref, frame, outs, members, sem):
    frames, band, width, ch = hidden_ref.shape
    flat = hidden_ref.reshape(frames, band * width, ch)
    me = lax.axis_index("tm") % members
    quarter = band * width // members
    copies = []
    for k, blocks in enumerate(outs):
        offset = 0
        for block in blocks:
            rows = pl.ds(pl.multiple_of((me ^ k) * quarter + offset, 16), block.shape[1])
            copies.append(
                pltpu.make_async_copy(
                    flat.at[frame, rows], block.at[frame], sem.at[len(copies), frame]
                )
            )
            offset += block.shape[1]
    return copies


def norm_kernel(count, members, rows, conv_ref, own_ref, other_ref, gain_ref, shift_ref, *refs):
    row_refs, packet_ref, (hidden_ref, sem) = refs[:rows], refs[rows], refs[-2:]
    outs = [refs[rows + 1 + k : -2 : members] for k in range(members)]
    frames, band, width, ch = conv_ref.shape
    for frame in range(frames):
        sums = [own_ref[frame, i] + other_ref[frame, i] for i in range(2)]
        for i, ref in enumerate(row_refs):
            packet_ref[frame, i * width : (i + 1) * width] = ref[frame]
        rest = jnp.concatenate(sums, axis=0)
        for part in range(3):
            at = rows * width + part * 16
            short = rest.astype(BF16)
            rest = rest - short.astype(F32)
            packet_ref[frame, at : at + 16] = short
        apply = norm_of(sums, count, gain_ref, shift_ref)

        @pl.loop(0, band, unroll=4)
        def _(row):
            hidden_ref[frame, row] = apply(conv_ref[frame, row])

        for copy in piece_copies(hidden_ref, frame, outs, members, sem):
            copy.start()
    for frame in range(frames):
        for copy in piece_copies(hidden_ref, frame, outs, members, sem):
            copy.wait()


def norm_call(conv, own, other, halo_rows, gain, shift, count, members, sizes):
    frames, band, width, ch = conv.shape
    rows = len(halo_rows)
    return pl.pallas_call(
        functools.partial(norm_kernel, count, members, rows),
        in_specs=[vspec()] * (5 + rows),
        out_specs=[vspec()] + [hspec()] * (members * len(sizes)),
        out_shape=[jax.ShapeDtypeStruct((frames, rows * width + 48, ch), BF16)]
        + [pltpu.HBM((frames, size, ch), BF16) for size in sizes for _ in range(members)],
        scratch_shapes=[
            VMEM((frames, band, width, ch), BF16),
            pltpu.SemaphoreType.DMA((members * len(sizes), frames)),
        ],
        compiler_params=params(16),
        cost_estimate=COST,
        name="norm",
    )(conv, own, other, gain.reshape(1, ch), shift.reshape(1, ch), *halo_rows)


def guest_kernel(count, members, video_ref, packet_ref, weight_ref, gain_ref, shift_ref, *refs):
    keep_ref, mate_ref, *away_refs = refs[:-3]
    hidden_ref, wide_ref, sem = refs[-3:]
    outs = [[keep_ref], [mate_ref]] + [[ref.at[k] for ref in away_refs] for k in range(2)]
    frames, band, width, ch = video_ref.shape
    rows = (packet_ref.shape[1] - 48) // width
    here = lax.axis_index("tm")

    @pl.when(jnp.logical_and(here >= members, here % 2 == 0))
    def _():
        widen(weight_ref, wide_ref)
        for frame in range(frames):
            parts = packet_ref[frame, rows * width :].astype(F32)
            both = parts[:16] + parts[16:32] + parts[32:]
            sums = [both[:8], both[8:]]
            apply = norm_of(sums, count, gain_ref, shift_ref)

            def write(row, value):
                hidden_ref[frame, row] = apply(value)

            read = padded_read(
                band,
                lambda r: video_ref[frame, r],
                lambda: packet_ref[frame, :width],
                lambda: packet_ref[frame, (rows - 1) * width : rows * width],
            )
            conv_rows(band, read, wide_ref, write)
            for copy in piece_copies(hidden_ref, frame, outs, members, sem):
                copy.start()
        for frame in range(frames):
            for copy in piece_copies(hidden_ref, frame, outs, members, sem):
                copy.wait()

    @pl.when(here < members)
    def _():
        hidden_ref[...] = jnp.zeros_like(hidden_ref)
        for frame in range(frames):
            for copy in piece_copies(hidden_ref, frame, outs, members, sem):
                copy.start()
        for frame in range(frames):
            for copy in piece_copies(hidden_ref, frame, outs, members, sem):
                copy.wait()


def guest_call(video, packet, weight, gain, shift, count, members, sizes):
    frames, band, width, ch = video.shape
    piece = (frames, band * width // members, ch)
    shapes = [piece, piece] + [(2, frames, size, ch) for size in sizes]
    return pl.pallas_call(
        functools.partial(guest_kernel, count, members),
        in_specs=[vspec()] * 5,
        out_specs=[hspec()] * len(shapes),
        out_shape=[pltpu.HBM(shape, BF16) for shape in shapes],
        scratch_shapes=[
            VMEM(video.shape, BF16),
            VMEM((4 * ch, 6 * ch), BF16),
            pltpu.SemaphoreType.DMA((2 + 2 * len(sizes), frames)),
        ],
        compiler_params=params(24),
        cost_estimate=LONG,
        name="guest",
    )(video, packet, weight, gain.reshape(1, ch), shift.reshape(1, ch))


def pack_kernel(weight_ref, out_ref):
    ch = weight_ref.shape[-1]
    out_ref[...] = jnp.zeros_like(out_ref)
    for layer in range(3):
        for out in range(2):
            for tap in range(3):
                row = out + 2 - tap
                out_ref[layer, row * ch : (row + 1) * ch, out * ch : (out + 1) * ch] = weight_ref[
                    layer, tap
                ]


def pack_call(weight):
    layers, _, ch, _ = weight.shape
    return pl.pallas_call(
        pack_kernel,
        in_specs=[vspec()],
        out_specs=vspec(),
        out_shape=jax.ShapeDtypeStruct((layers, 4 * ch, 2 * ch), BF16),
        compiler_params=params(8),
        cost_estimate=LONG,
        name="pack",
    )(weight)


def pair(read, write, time, layer, wide_ref):
    ch = wide_ref.shape[2] // 2
    dilation = 2**layer
    frames = [read(time + (a - 2) * dilation) for a in range(4)]
    both = jnp.dot(jnp.concatenate(frames, axis=-1), wide_ref[layer], preferred_element_type=F32)
    write(time, (both[:, :ch] + frames[2].astype(F32)).astype(BF16))
    write(time + dilation, (both[:, ch:] + frames[3].astype(F32)).astype(BF16))


def ahead_kernel(members, *refs):
    pieces, (wide_ref, out_ref, u0_ref) = refs[:members], refs[members:]
    step = pieces[0].shape[0]
    me = lax.axis_index("tm") % members
    for k in range(members):
        u0_ref[pl.ds((me ^ k) * step, step)] = pieces[k][...]

    def write1(t, value):
        out_ref[t - 2] = value

    for time in range(2, SPAN, 2):
        pair(lambda t: u0_ref[t], write1, time, 0, wide_ref)


def ahead_call(own, wide, cost):
    members = len(own)
    _, size, ch = own[0].shape
    return pl.pallas_call(
        functools.partial(ahead_kernel, members),
        in_specs=[vspec()] * (members + 1),
        out_specs=vspec(),
        out_shape=jax.ShapeDtypeStruct((SPAN - 2, size, ch), BF16),
        scratch_shapes=[VMEM((SPAN, size, ch), BF16)],
        compiler_params=params(16),
        cost_estimate=cost,
        name="ahead",
    )(*own, wide)


def early_kernel(members, plan, first, *refs):
    arrays, (ahead_ref, wide_ref, out_ref, u0_ref, u1_ref) = refs[: len(plan)], refs[len(plan) :]
    size = out_ref.shape[1]
    lead = SPAN - 2
    me = lax.axis_index("tm") % members
    for ref, (kind, k, source, target, rows) in zip(arrays, plan):
        value = ref.at[0] if len(ref.shape) == 4 else ref
        step = value.shape[0]
        here, there = slice(target, target + rows), slice(source, source + rows)
        if kind == "own":

            @pl.when(me == k)
            def _():
                u0_ref[lead : lead + step, here] = value[:, there]

        elif kind == "middle":
            u0_ref[2:4, here] = value[:, there]
        else:

            @pl.when((me ^ k) % 2 == 0)
            def _():
                u0_ref[pl.ds(2 * (me ^ k), step), here] = value[:, there]

    def write1(t, value):
        u1_ref[t + 4] = value

    def read1(t):
        return u1_ref[t + 4] if t < 2 else ahead_ref[t - 2, first : first + size]

    def write2(t, value):
        out_ref[t] = value

    for time in range(-4, 2, 2):
        pair(lambda t: u0_ref[t + lead], write1, time, 0, wide_ref)
    for time in range(0, SPAN, 4):
        for odd in range(2):
            pair(read1, write2, time + odd, 1, wide_ref)


def early_call(sources, aheads, wide, members, first, size):
    plan, arrays = [], []
    start, ahead = first, aheads[0]
    for block in aheads[1:]:
        if start >= ahead.shape[1]:
            start, ahead = start - ahead.shape[1], block
    for kind, k, blocks in sources:
        at = 0
        for block in blocks:
            rows = block.shape[-2]
            low, high = max(first, at), min(first + size, at + rows)
            if low < high:
                plan.append((kind, k, low - at, low - first, high - low))
                arrays.append(block)
            at += rows
    ch = wide.shape[-1] // 2
    return pl.pallas_call(
        functools.partial(early_kernel, members, plan, start),
        in_specs=[vspec()] * (len(arrays) + 2),
        out_specs=vspec(),
        out_shape=jax.ShapeDtypeStruct((SPAN, size, ch), BF16),
        scratch_shapes=[VMEM((SPAN, size, ch), BF16), VMEM((6, size, ch), BF16)],
        compiler_params=params(16),
        cost_estimate=COST,
        name="early",
    )(*arrays, ahead, wide)


def late_kernel(members, own_ref, halo_ref, wide_ref, *refs):
    outs, u3_ref = refs[:-1], refs[-1]
    step = outs[0].shape[0]
    me = lax.axis_index("tm") % members

    def write3(t, value):
        u3_ref[t] = value

    for time in range(4):
        pair(
            lambda t: own_ref[t] if t >= 0 else halo_ref[t + SPAN], write3, time, 2, wide_ref
        )
    for k in range(members):
        outs[k][...] = u3_ref[pl.ds((me ^ k) * step, step)]


def late_call(own, halo, wide, members):
    frames, size, ch = own.shape
    return pl.pallas_call(
        functools.partial(late_kernel, members),
        in_specs=[vspec()] * 3,
        out_specs=[vspec()] * members,
        out_shape=[jax.ShapeDtypeStruct((frames // members, size, ch), BF16)] * members,
        scratch_shapes=[VMEM(own.shape, BF16)],
        compiler_params=params(12),
        cost_estimate=COST,
        name="late",
    )(own, halo, wide)


def place_kernel(members, offsets, *refs):
    count = members * len(offsets)
    pieces, (out_ref, sem) = refs[:count], refs[-2:]
    me = lax.axis_index("tm") % members
    copies = []
    for i, offset in enumerate(offsets):
        for k in range(members):
            n = i * members + k
            rows = pl.ds(offset, pieces[n].shape[1])
            copies.append(
                pltpu.make_async_copy(pieces[n], out_ref.at[:, me ^ k, rows], sem.at[n])
            )
    for copy in copies:
        copy.start()
    for copy in copies:
        copy.wait()


def place_call(chunks, offsets, quarter, before=None):
    members = len(chunks[0])
    frames, _, ch = chunks[0][0].shape
    pieces = sum(chunks, [])
    shape = jax.ShapeDtypeStruct((frames, members, quarter, ch), BF16)
    return pl.pallas_call(
        functools.partial(place_kernel, members, offsets),
        in_specs=[vspec()] * len(pieces) + [hspec()] * (before is not None),
        out_specs=hspec(),
        out_shape=pltpu.HBM(shape.shape, BF16),
        input_output_aliases={} if before is None else {len(pieces): 0},
        scratch_shapes=[pltpu.SemaphoreType.DMA((len(pieces),))],
        compiler_params=params(8),
        cost_estimate=COST,
        name="place",
    )(*pieces, *([] if before is None else [hbm(before)]))


def halo_rows(video):
    size, row = lax.axis_size("rows"), lax.axis_index("rows")
    band = video.shape[1]
    if size == 2:
        mine = lax.dynamic_slice_in_dim(video, jnp.where(row == 0, band - 1, 0), 1, axis=1)[:, 0]
        other = lax.ppermute(mine, "rows", [(0, 1), (1, 0)])
        return other, other
    up = [(i, i + 1) for i in range(size - 1)]
    down = [(j, i) for i, j in up]
    return lax.ppermute(video[:, -1], "rows", up), lax.ppermute(video[:, 0], "rows", down)


def other_sums(sums):
    if lax.axis_size("rows") == 2:
        return lax.ppermute(sums, "rows", [(0, 1), (1, 0)])
    return lax.psum(sums, "rows") - sums


def after(value, *others):
    return lax.optimization_barrier((value, *others))[0]


def body(video, spatial_weight, norm_gain, norm_shift, temporal_weight):
    frames, band, width, ch = video.shape
    total = lax.axis_size("tm")
    me = lax.axis_index("tm") % (SPAN // frames)
    rows = lax.axis_size("rows")
    members = SPAN // frames
    swaps = [[(i, i ^ k) for i in range(total)] for k in range(members)]
    onward = [(i, i + members) for i in range(total - members)]
    guest_pairs = [(i, i + members - 1) for i in range(1, total - members, 2)]
    guest_swaps = [[(i, i ^ k) for i in range(0, total, 2)] for k in range(members)]

    guest_video = lax.ppermute(video, "tm", guest_pairs)
    above, below = halo_rows(video)
    conv, sums = conv_call(video, spatial_weight)
    conv, sums = edge_call(conv, above, below, spatial_weight, sums)
    count = band * rows * width * (ch // GROUPS)
    quarter = band * width // members
    own_sizes, guest_sizes, out_sizes = [
        [quarter * part // 60 for part in parts] for parts in (OWN_PARTS, GUEST_PARTS, OUT_PARTS)
    ]
    halo_list = [above] if above is below else [above, below]
    packet, *pieces = norm_call(
        conv, sums, other_sums(sums), halo_list, norm_gain, norm_shift, count, members, own_sizes
    )

    def swap(four, waits=None):
        got = [four[0]]
        for k in range(1, members):
            value = four[k] if waits is None else after(four[k], waits[k])
            got.append(lax.ppermute(value, "tm", swaps[k]))
        return got

    guest_packet = lax.ppermute(packet, "tm", guest_pairs)
    keep, mate, *aways = guest_call(
        guest_video, guest_packet, spatial_weight, norm_gain, norm_shift, count, members, guest_sizes
    )
    wide = pack_call(after(temporal_weight, keep))
    sources = [(kind, k, []) for kind in ("own", "guest") for k in range(members)]
    sources.append(("middle", 0, []))

    def add(start, arrays):
        for (_, _, blocks), array in zip(sources[start:], arrays):
            blocks.append(array)

    aheads, passed, results = [], [], []

    def block(i, gate):
        four = pieces[i * members : (i + 1) * members]
        own = swap(four, [gate] * members if i else None)
        crossed = lax.ppermute(after(aways[i], own[2]) if i else aways[i], "tm", guest_swaps[2])
        four = own if i else after(own, wide)
        middle = functools.reduce(
            lambda acc, k: jnp.where(me == (2 ^ k), four[k], acc), range(1, members), four[0]
        )
        add(0, own)
        add(2 * members, [lax.ppermute(middle, "tm", onward)])
        if i == 0:
            add(members, [keep, lax.ppermute(after(mate, wide), "tm", guest_swaps[1])])
        waits = [middle] if i else [middle, crossed]
        aheads.append(ahead_call(own, after(wide, *waits), COST if i else LONG))
        forward = crossed[1] if i else after(crossed[1], aheads[0])
        add(members + 2, [crossed, lax.ppermute(forward, "tm", guest_swaps[1])])

    block(0, None)
    first = 0
    for i, size in enumerate(out_sizes):
        u2 = early_call(sources, aheads, wide, members, first, size)
        if i == 0:
            block(1, aheads[0])
        if i > 1:
            u2 = after(u2, passed[i - 2])
        passed.append(lax.ppermute(u2, "tm", onward))
        following = late_call(u2, passed[-1], wide, members)
        results.append(swap(following, results[-1] if results else None))
        late = following if i < 2 else late
        first += size
    offsets = [sum(out_sizes[:i]) for i in range(len(out_sizes))]
    out = place_call(results[:2], offsets[:2], quarter)
    out = place_call(results[2:], offsets[2:], quarter, out)
    return out.reshape(frames, band, width, ch)


def solution(mesh):
    return jax.shard_map(
        body,
        mesh=mesh,
        in_specs=(P("tm", "rows", None, None), P(), P(), P(), P()),
        out_specs=P("tm", "rows", None, None),
        check_vma=False,
    )
```
